128 devices in a mesh: gx: 4 (over x), gy: 8 (over z, core), gz: 4 (over y).
Axes of the slice: x: 4, y: 4, z: 4, core: 2. Of those that a mesh axis runs over, the one named last changes fastest.
Arguments:
- point_data: float32 [128, 128, 7, 32], P(('gx', 'gy', 'gz')), may hold values from -2.8 to 2.8, as said below
- point_cells: int32 [128, 128, 3, 32], P(('gx', 'gy', 'gz')), may hold values from 0 to 127, as said below
- send_counts: int32 [128, 128], P(('gx', 'gy', 'gz')), may hold values from 0 to 32, as said below
Outputs:
- indicator: float32 [64, 128, 512], P('gx', 'gy', 'gz')
- point_values: float32 [128, 128, 32], P(('gx', 'gy', 'gz'))
The draws below stay inside these ranges and needn't reach their ends.
Inputs may be any that keep to these rules, and one draw needn't show every extreme that they name: `point_data`: channels 0 to 2 of a slot are an oriented normal, channel 3 a confidence between 0.05 and 1, channels 4 to 6 offsets inside the cell between 0 and 1. `point_cells`: channel 0 lies below 16, channel 1 below 16, channel 2 below 128. Slot j from block s to brick d is live where j < send_counts[s, d]. In every draw some brick receives 32 live slots from every block.
All inputs are finite; a program needn't handle non-finite values.
Results may differ from the reference program's by a relative error of at most 0.00002.
Values sent between devices are 32-bit elements; how exact they have to be, the bound alone decides.
A program may use at most 128 MiB of HBM per device.

```python
import jax
import jax.numpy as jnp

CX = 16
CY = 16
CZ = 128
CAP = 32
ITERS = 6
BRICKS = 128
NX = 64
NY = 128
NZ = 512
N_GY = 8
N_GZ = 4


def draw_point_data(key, part):
    key_normal, key_conf, key_offset = jax.random.split(key, 3)
    shape_normal = (BRICKS, BRICKS, 3, CAP)
    normal = jnp.clip(0.7 * jax.random.normal(key_normal, shape_normal, jnp.float32), -2.8, 2.8)
    confidence = jax.random.uniform(key_conf, (BRICKS, BRICKS, 1, CAP), jnp.float32, 0.2, 1.0)
    offsets = jax.random.uniform(key_offset, shape_normal, jnp.float32, 0.0, 1.0)
    return jnp.concatenate([normal, confidence, offsets], axis=2).astype(jnp.float32)


def draw_point_cells(key, part):
    limits = jnp.array([CX, CY, CZ], jnp.int32)[None, None, :, None]
    raw_bits = jax.random.randint(key, (BRICKS, BRICKS, 3, CAP), 0, 1048576)
    return (raw_bits % limits).astype(jnp.int32)


def draw_send_counts(key, part):
    key_heavy, key_level, key_count = jax.random.split(jax.random.fold_in(key, 7), 3)
    heavy = jax.random.randint(key_heavy, (), 0, BRICKS)
    levels = jax.random.randint(key_level, (BRICKS,), 1, 5)
    raw_count = jax.random.randint(key_count, (BRICKS, BRICKS), 0, CAP + 1)
    counts = jnp.minimum(CAP, raw_count * levels[None, :] // 4)
    dest_ids = jnp.arange(BRICKS, dtype=jnp.int32)
    return jnp.where(dest_ids[None, :] == heavy, CAP, counts).astype(jnp.int32)


def setup_inputs(seed: int = 0) -> dict:
    key_list = jax.random.split(jax.random.key(seed), 4)
    return {
        "point_data": draw_point_data(jax.random.fold_in(key_list[3], 71), 0),
        "point_cells": draw_point_cells(jax.random.fold_in(key_list[3], 71), 0),
        "send_counts": draw_send_counts(jax.random.fold_in(key_list[3], 71), 0),
    }


base_screen = 0.25
point_screen = 4.0


def trilinear(offsets, corner_x, corner_y, corner_z):
    along_x = offsets[..., 0, :] if corner_x else 1.0 - offsets[..., 0, :]
    along_y = offsets[..., 1, :] if corner_y else 1.0 - offsets[..., 1, :]
    along_z = offsets[..., 2, :] if corner_z else 1.0 - offsets[..., 2, :]
    return along_x * along_y * along_z


def six_sum(padded):
    total = padded[2:, 1:-1, 1:-1] + padded[:-2, 1:-1, 1:-1]
    total = total + padded[1:-1, 2:, 1:-1] + padded[1:-1, :-2, 1:-1]
    return total + padded[1:-1, 1:-1, 2:] + padded[1:-1, 1:-1, :-2]


def divergence(padded):
    total = padded[0, 2:, 1:-1, 1:-1] - padded[0, :-2, 1:-1, 1:-1]
    total = total + padded[1, 1:-1, 2:, 1:-1] - padded[1, 1:-1, :-2, 1:-1]
    return total + padded[2, 1:-1, 1:-1, 2:] - padded[2, 1:-1, 1:-1, :-2]


def chebyshev(source_term, diagonal, operate):
    half_width = 6.0 / (6.0 + base_screen)
    sigma_ratio = 1.0 / half_width
    rho_prev = half_width
    solution = jnp.zeros_like(source_term)
    residual = source_term
    direction = source_term / diagonal
    for sweep in range(ITERS):
        solution = solution + direction
        residual = residual - operate(direction)
        if sweep + 1 < ITERS:
            rho_next = 1.0 / (2.0 * sigma_ratio - rho_prev)
            direction = (rho_next * rho_prev) * direction + (2.0 * rho_next / half_width) * residual / diagonal
            rho_prev = rho_next
    return solution


def reference(point_data, point_cells, send_counts):
    slot_index = jnp.arange(CAP, dtype=jnp.int32)
    live_mask = (slot_index[None, None, :] < send_counts[:, :, None]).astype(jnp.float32)
    weight = point_data[:, :, 3, :] * live_mask
    offsets = point_data[:, :, 4:7, :]
    brick_ids = jnp.arange(BRICKS, dtype=jnp.int32)
    cell_x = point_cells[:, :, 0, :] + ((brick_ids // (N_GY * N_GZ)) * CX)[None, :, None]
    cell_y = point_cells[:, :, 1, :] + (((brick_ids // N_GZ) % N_GY) * CY)[None, :, None]
    cell_z = point_cells[:, :, 2, :] + ((brick_ids % N_GZ) * CZ)[None, :, None]
    volume = jnp.zeros((4, (NX + 1) * (NY + 1) * (NZ + 1)), jnp.float32)
    for corner_x in (0, 1):
        for corner_y in (0, 1):
            for corner_z in (0, 1):
                point_mass = weight * trilinear(offsets, corner_x, corner_y, corner_z)
                contrib = jnp.stack([point_data[:, :, 0, :] * point_mass, point_data[:, :, 1, :] * point_mass,
                                     point_data[:, :, 2, :] * point_mass, point_mass]).reshape(4, -1)
                linear_at = ((cell_x + corner_x) * (NY + 1) + cell_y + corner_y) * (NZ + 1) + cell_z + corner_z
                volume = volume.at[:, linear_at.reshape(-1)].add(contrib)
    splat = volume.reshape(4, NX + 1, NY + 1, NZ + 1)[:, :NX, :NY, :NZ]
    padded = jnp.pad(splat[:3], ((0, 0), (1, 1), (1, 1), (1, 1)))
    source_term = -0.5 * divergence(padded)
    diagonal = 6.0 + base_screen + point_screen * splat[3]

    def operate(field):
        return diagonal * field - six_sum(jnp.pad(field, 1))

    indicator = chebyshev(source_term, diagonal, operate)
    top_padded = jnp.pad(indicator, ((0, 1), (0, 1), (0, 1))).reshape(-1)
    values = jnp.zeros(live_mask.shape, jnp.float32)
    for corner_x in (0, 1):
        for corner_y in (0, 1):
            for corner_z in (0, 1):
                linear_at = ((cell_x + corner_x) * (NY + 1) + cell_y + corner_y) * (NZ + 1) + cell_z + corner_z
                values = values + trilinear(offsets, corner_x, corner_y, corner_z) * top_padded[linear_at]
    return indicator, values * live_mask
```

```python
import functools

import jax
import jax.numpy as jnp
from jax import lax
from jax.experimental import pallas as pl
from jax.experimental.pallas import tpu as pltpu
from jax.sharding import PartitionSpec as P

MESH = pl.DeviceIdType.MESH
F32 = jnp.float32
BF16 = jnp.bfloat16

DEVICES = 128
CAP = 32
CHANNELS = 10
WIDTH = 384
POINTS = 512
ROWS = 304
ITERS = 6

base_screen = 0.25
point_screen = 4.0


def sweep_factors():
    half_width = 6.0 / (6.0 + base_screen)
    rho_prev = half_width
    factors = []
    for _ in range(ITERS - 1):
        rho_next = 1.0 / (2.0 / half_width - rho_prev)
        factors.append((rho_next * rho_prev, 2.0 * rho_next / half_width))
        rho_prev = rho_next
    return factors


def position(sizes):
    return tuple(lax.axis_index(name) for name in ("gx", "gy", "gz"))


def coordinates(sizes, index):
    ny, nz = sizes[1], sizes[2]
    return (index // (ny * nz), lax.rem(index // nz, ny), lax.rem(index, nz))


def vmem():
    return pl.BlockSpec(memory_space=pltpu.VMEM)


def greet_all(sizes, me):
    barrier = pltpu.get_barrier_semaphore()

    @pl.loop(1, DEVICES)
    def _(step):
        other = lax.rem(me + step, DEVICES)
        pl.semaphore_signal(barrier, inc=1, device_id=coordinates(sizes, other), device_id_type=MESH)


def exchange_rows(sizes, me, send, recv, sent, send_sem, recv_sem):
    pl.semaphore_wait(pltpu.get_barrier_semaphore(), DEVICES - 1)

    @pl.loop(1, DEVICES)
    def _(step):
        other = lax.rem(me + step, DEVICES)
        pltpu.make_async_remote_copy(
            src_ref=send.at[pl.ds(other, 1)],
            dst_ref=recv.at[pl.ds(me, 1)],
            send_sem=send_sem,
            recv_sem=recv_sem,
            device_id=coordinates(sizes, other),
            device_id_type=MESH,
        ).start()

    pltpu.make_async_copy(send.at[pl.ds(me, 1)], recv.at[pl.ds(me, 1)], recv_sem).start()
    pltpu.make_async_copy(send.at[pl.ds(me, 1)], sent, send_sem).start()
    pltpu.make_async_copy(send, recv, send_sem).wait()
    pltpu.make_async_copy(send, recv, recv_sem).wait()


def route_kernel(sizes, data_ref, cells_ref, counts_ref, out_ref, send, recv, sent, send_sem, recv_sem):
    gx, gy, gz = position(sizes)
    me = (gx * sizes[1] + gy) * sizes[2] + gz
    greet_all(sizes, me)
    slot = lax.broadcasted_iota(jnp.int32, (CAP, DEVICES), 0)
    weight = jnp.where(slot < counts_ref[...], data_ref[3], 0.0)
    parts = [data_ref[c] * weight for c in range(3)] + [weight]
    parts += [data_ref[4 + c] for c in range(3)] + [cells_ref[c].astype(F32) for c in range(3)]
    parts += [jnp.zeros((WIDTH - CAP * CHANNELS, DEVICES), F32)]
    send[...] = jnp.concatenate(parts, axis=0).T
    exchange_rows(sizes, me, send, recv, sent, send_sem, recv_sem)
    out_ref[...] = recv[...].T[: CAP * CHANNELS].reshape(CHANNELS, CAP, DEVICES)


def return_kernel(sizes, values_ref, counts_ref, out_ref, send, recv, sent, send_sem, recv_sem):
    gx, gy, gz = position(sizes)
    me = (gx * sizes[1] + gy) * sizes[2] + gz
    greet_all(sizes, me)
    padded = jnp.concatenate([values_ref[...], jnp.zeros((DEVICES - CAP, DEVICES), F32)], axis=0)
    send[...] = padded.T
    exchange_rows(sizes, me, send, recv, sent, send_sem, recv_sem)
    slot = lax.broadcasted_iota(jnp.int32, (CAP, DEVICES), 0)
    out_ref[...] = jnp.where(slot < counts_ref[...], recv[...].T[:CAP], 0.0)


def split(value):
    high = value.astype(BF16)
    return high, (value - high.astype(F32)).astype(BF16)


def point_rows(d_ref, group, channel):
    count = POINTS // DEVICES
    rows = [d_ref[channel, pl.ds(group * count + q, 1), :] for q in range(count)]
    return jnp.concatenate(rows, axis=1)


def spread(row):
    return jnp.broadcast_to(row, (16, POINTS)).astype(BF16)


def spread_split(row):
    wide = jnp.broadcast_to(row, (16, POINTS))
    return split(wide)


def splat_kernel(d_ref, acc_ref, ov_ref, a_ref, b_ref):
    acc_ref[...] = jnp.zeros_like(acc_ref)
    ov_ref[...] = jnp.zeros_like(ov_ref)
    iota = lax.broadcasted_iota(jnp.int32, (16, POINTS), 0).astype(F32).astype(BF16)
    zero = jnp.zeros((16, POINTS), BF16)

    def store_a(first, high, low):
        rows = pl.ds(first, 16)
        a_ref[rows, 0:POINTS] = high
        a_ref[rows, POINTS : 2 * POINTS] = low
        a_ref[rows, 2 * POINTS : 3 * POINTS] = high

    def store_b(first, high, low):
        rows = pl.ds(first, 16)
        b_ref[rows, 0:POINTS] = high
        b_ref[rows, POINTS : 2 * POINTS] = high
        b_ref[rows, 2 * POINTS : 3 * POINTS] = low

    @pl.loop(0, CAP * DEVICES // POINTS)
    def _(group):
        v = [point_rows(d_ref, group, c) for c in range(4)]
        fx, fy, fz, cx, cy, cz = [point_rows(d_ref, group, 4 + c) for c in range(6)]
        bx, by, bz = spread(cx), spread(cy), spread(cz)
        y0, y1 = by == iota, (by + 1.0).astype(BF16) == iota
        near = [], []
        for along, out in ((1.0 - fx, 0), (fx, 1)):
            w0 = spread_split(along * (1.0 - fy))
            w1 = spread_split(along * fy)
            for part in range(2):
                near[out].append(jnp.where(y0, w0[part], jnp.where(y1, w1[part], zero)))
        for x in range(17):
            x0, x1 = bx == x, bx == x - 1
            high, low = [jnp.where(x0, near[0][part], jnp.where(x1, near[1][part], zero)) for part in range(2)]
            store_a(16 * x, high, low)
        edge = jnp.where(cy == 15.0, fy, 0.0)
        e0, e1 = spread_split((1.0 - fx) * edge), spread_split(fx * edge)
        for t in range(2):
            at = iota + jnp.asarray(16 * t, BF16)
            x0, x1 = bx == at, (bx + 1.0).astype(BF16) == at
            high, low = [jnp.where(x0, e0[part], jnp.where(x1, e1[part], zero)) for part in range(2)]
            store_a(272 + 16 * t, high, low)
        g0 = [spread_split(v[c] * (1.0 - fz)) for c in range(4)]
        g1 = [spread_split(v[c] * fz) for c in range(4)]
        for t in range(8):
            at = iota + jnp.asarray(16 * t, BF16)
            z0, z1 = bz == at, (bz + 1.0).astype(BF16) == at
            for c in range(4):
                high, low = [jnp.where(z0, g0[c][part], jnp.where(z1, g1[c][part], zero)) for part in range(2)]
                store_b(128 * c + 16 * t, high, low)
        top = bz == 127
        high, low = zero, zero
        for c in range(4):
            here = jnp.logical_and(top, iota == c)
            high, low = jnp.where(here, g1[c][0], high), jnp.where(here, g1[c][1], low)
        store_b(512, high, low)
        dims = (((1,), (1,)), ((), ()))
        acc_ref[...] += lax.dot_general(a_ref[...], b_ref[0:512, :], dims, preferred_element_type=F32)
        ov_ref[:, 0:16] += lax.dot_general(a_ref[...], b_ref[512:528, :], dims, preferred_element_type=F32)


def interp_kernel(d_ref, u_ref, halo_ref, uz_ref, out_ref, l_ref, r_ref):
    for first, source in ((0, u_ref), (256, halo_ref)):
        value = source[...]
        rows = pl.ds(first, value.shape[0])
        high, low = split(value)
        l_ref[rows, 0:128] = high
        l_ref[rows, 128:256] = low
        l_ref[rows, 256:384] = high
    top = jnp.broadcast_to(uz_ref[:, 0:1], (ROWS, 128))
    high = top.astype(BF16).astype(F32)
    lane = lax.broadcasted_iota(jnp.int32, (ROWS, 128), 1)
    low = jnp.where(lane == 1, top - high, 0.0)
    l_ref[:, 384:512] = jnp.where(jnp.logical_or(lane == 0, lane == 2), high, low).astype(BF16)
    r_ref[400:512, :] = jnp.zeros((112, POINTS), BF16)
    iota_f = lax.broadcasted_iota(jnp.int32, (16, POINTS), 0).astype(F32)
    iota = iota_f.astype(BF16)
    zero = jnp.zeros((16, POINTS), BF16)

    @pl.loop(0, CAP * DEVICES // POINTS)
    def _(group):
        fx, fy, fz, cx, cy, cz = [point_rows(d_ref, group, 4 + c) for c in range(6)]
        bz = spread(cz)
        g0, g1 = spread_split(1.0 - fz), spread_split(fz)
        for t in range(8):
            at = iota + jnp.asarray(16 * t, BF16)
            z0, z1 = bz == at, (bz + 1.0).astype(BF16) == at
            high, low = [jnp.where(z0, g0[part], jnp.where(z1, g1[part], zero)) for part in range(2)]
            r_ref[pl.ds(16 * t, 16), :] = high
            r_ref[pl.ds(128 + 16 * t, 16), :] = high
            r_ref[pl.ds(256 + 16 * t, 16), :] = low
        top = bz == 127
        high = jnp.where(jnp.logical_and(top, iota <= 1), g1[0], zero)
        r_ref[384:400, :] = jnp.where(jnp.logical_and(top, iota == 2), g1[1], high)
        g = jnp.dot(l_ref[...], r_ref[...], preferred_element_type=F32)
        total = jnp.zeros((16, POINTS), F32)
        for x in range(17):
            hat = jnp.where(cx == x, 1.0 - fx, jnp.where(cx == x - 1, fx, 0.0))
            total = total + hat * g[16 * x : 16 * x + 16]
        hat = jnp.where(cy == iota_f, 1.0 - fy, jnp.where(cy + 1.0 == iota_f, fy, 0.0))
        total = total * hat
        edge = jnp.where(cy == 15.0, fy, 0.0)
        for t in range(2):
            at = iota_f + 16.0 * t
            hat = jnp.where(cx == at, 1.0 - fx, jnp.where(cx + 1.0 == at, fx, 0.0))
            total = total + hat * edge * g[272 + 16 * t : 288 + 16 * t]
        value = jnp.sum(total, axis=0, keepdims=True)
        count = POINTS // DEVICES
        for q in range(count):
            out_ref[pl.ds(group * count + q, 1), :] = value[:, q * DEVICES : (q + 1) * DEVICES]


def roll_to(tile, source, target):
    shift = (target - source) % 128
    return pltpu.roll(tile, shift, 1) if shift else tile


def solve_kernel(
    sizes, s_ref, ov_ref, u_ref, halo_ref, uz_ref,
    m_ref, zs_ref, sx, sy, sxy, sz, p_ref, zp_ref, rx, ry, rz, r_ref, inv_ref, diag_ref,
    fx, fy, fxy, fz, s_send, s_recv, h_send, h_recv, f_send, f_recv,
):
    here = position(sizes)
    lower = [here[a] > 0 for a in range(3)]
    upper = [here[a] < sizes[a] - 1 for a in range(3)]
    steps = [(1, 0, 0), (0, 1, 0), (0, 0, 1), (1, 1, 0), (1, 0, 1), (0, 1, 1), (1, 1, 1)]

    def all_of(flags, step):
        wanted = [flags[a] for a in range(3) if step[a]]
        return functools.reduce(jnp.logical_and, wanted)

    def shifted(step, sign):
        return tuple(here[a] + sign * step[a] for a in range(3))

    barrier = pltpu.get_barrier_semaphore()
    known = jnp.int32(0)
    for step in steps:
        for flags, sign in ((lower, -1), (upper, 1)):
            present = all_of(flags, step)
            known = known + present.astype(jnp.int32)

            @pl.when(present)
            def _(step=step, sign=sign):
                pl.semaphore_signal(barrier, inc=1, device_id=shifted(step, sign), device_id_type=MESH)

    lane = lax.broadcasted_iota(jnp.int32, (8, 128), 1)
    sub = lax.broadcasted_iota(jnp.int32, (8, 128), 0)
    zero = jnp.zeros((8, 128), F32)

    for a, bufs in ((0, (sx, rx.at[:, 0])), (1, (sy, ry.at[:, 0])), (2, (sz.at[0], rz.at[:, 0]))):
        @pl.when(jnp.logical_not(lower[a]))
        def _(bufs=bufs):
            for buf in bufs:
                buf[...] = jnp.zeros(buf.shape, F32)
    for a, bufs in ((0, (fx, rx.at[:, 1])), (1, (fy, ry.at[:, 1])), (2, (fz.at[0], rz.at[:, 1]))):
        @pl.when(jnp.logical_not(upper[a]))
        def _(bufs=bufs):
            for buf in bufs:
                buf[...] = jnp.zeros(buf.shape, F32)
    for step, low_buf, high_buf in (
        (steps[3], sxy, fxy), (steps[4], sz.at[1], fz.at[1]),
        (steps[5], sz.at[2], fz.at[2]), (steps[6], sz.at[3], fz.at[3]),
    ):
        for flags, buf in ((lower, low_buf), (upper, high_buf)):
            @pl.when(jnp.logical_not(all_of(flags, step)))
            def _(buf=buf):
                buf[...] = jnp.zeros(buf.shape, F32)

    for part, tiles in ((0, 32), (1, 5)):
        packed = zero
        for i in range(tiles):
            tile = ov_ref[pl.ds(256 * part + 8 * i, 8), :]
            here_lanes = jnp.logical_and(lane >= 4 * i, lane < 4 * i + 4)
            packed = jnp.where(here_lanes, roll_to(tile, 0, 4 * i), packed)
        zs_ref[part] = packed
    for c in range(4):
        m_ref[c] = s_ref[0:256, 128 * c : 128 * c + 128].reshape(16, 2, 8, 128)
    pl.semaphore_wait(barrier, known)

    def corner_copies(sources, targets, send, recv, sign):
        copies = []
        for i, step in enumerate(steps):
            copies.append(pltpu.make_async_remote_copy(
                src_ref=sources[i], dst_ref=targets[i], send_sem=send.at[i], recv_sem=recv.at[i],
                device_id=shifted(step, sign), device_id_type=MESH,
            ))
        return copies

    def each(copies, flags, action):
        for copy, step in zip(copies, steps):
            @pl.when(all_of(flags, step))
            def _(copy=copy):
                action(copy)

    mass = corner_copies(
        [s_ref.at[256:272], s_ref.at[272:288], zs_ref.at[0], s_ref.at[288:289], zs_ref.at[1], zs_ref.at[1], zs_ref.at[1]],
        [sx, sy, sz.at[0], sxy, sz.at[1], sz.at[2], sz.at[3]], s_send, s_recv, 1,
    )
    each(mass, upper, lambda copy: copy.start())
    each(mass, lower, lambda copy: copy.wait_recv())

    for c in range(4):
        columns = slice(128 * c, 128 * c + 128)
        m_ref[c, 0] += sx[:, columns].reshape(2, 8, 128)
        from_y = sy[:, columns]
        near_z = [roll_to(sz[2], 8 + 4 * t + c, 0) for t in range(2)]
        for x in range(16):
            row = from_y[x : x + 1, :] + jnp.where(lane[0:1] == 0, near_z[x // 8][x % 8 : x % 8 + 1, :], 0.0)
            m_ref[c, x, 0, 0:1, :] += row
        for i in range(32):
            m_ref[c, i // 2, i % 2] += jnp.where(lane == 0, roll_to(sz[0], 4 * i + c, 0), 0.0)
        for t in range(2):
            m_ref[c, 0, t] += jnp.where(lane == 0, roll_to(sz[1], 4 * t + c, 0), 0.0)
        corner = sxy[:, columns] + jnp.where(lane[0:1] == 0, roll_to(sz[3], 16 + c, 0)[0:1], 0.0)
        m_ref[c, 0, 0, 0:1, :] += corner
    each(mass, upper, lambda copy: copy.wait_send())

    def pack(read, source):
        packed = zero
        for i in range(32):
            packed = jnp.where(lane == i, roll_to(read(i), source, i), packed)
        return packed

    def unpack(packed, target):
        mine = lane == target
        tiles = [jnp.where(mine, roll_to(packed, i, target), 0.0) for i in range(32)]
        return jnp.stack(tiles).reshape(16, 2, 8, 128)

    def face_copies(e, xs, ys):
        sources = [xs.at[15], xs.at[0], ys.at[:, 1, 7, :], ys.at[:, 0, 0, :], zp_ref.at[e, 1], zp_ref.at[e, 0]]
        targets = [rx.at[e, 0], rx.at[e, 1], ry.at[e, 0, :, 0, :], ry.at[e, 1, :, 0, :], rz.at[e, 0], rz.at[e, 1]]
        copies = []
        for d in range(6):
            step = tuple(int(a == d // 2) for a in range(3))
            copies.append(pltpu.make_async_remote_copy(
                src_ref=sources[d], dst_ref=targets[d], send_sem=h_send.at[e, d], recv_sem=h_recv.at[e, d],
                device_id=shifted(step, 1 - 2 * (d % 2)), device_id_type=MESH,
            ))
        return copies

    def arriving(d):
        return (lower, upper)[d % 2][d // 2]

    def leaving(d):
        return (upper, lower)[d % 2][d // 2]

    def each_face(copies, when, action):
        for d, copy in enumerate(copies):
            @pl.when(when(d))
            def _(copy=copy):
                action(copy)

    lanes4 = lax.broadcasted_iota(jnp.int32, (16, 2, 8, 128), 3)
    subs3 = lax.broadcasted_iota(jnp.int32, (16, 8, 128), 1)

    def x_sides(value, e):
        low = jnp.concatenate([rx[e, 0][None], value[:-1]], axis=0)
        high = jnp.concatenate([value[1:], rx[e, 1][None]], axis=0)
        return low, high

    def y_sides(value, e):
        down = pltpu.roll(value.reshape(32, 8, 128), 1, 1).reshape(16, 2, 8, 128)
        up = pltpu.roll(value.reshape(32, 8, 128), 7, 1).reshape(16, 2, 8, 128)
        first = subs3 == 0
        low = jnp.stack([jnp.where(first, ry[e, 0], down[:, 0]), jnp.where(first, down[:, 0], down[:, 1])], axis=1)
        last = subs3 == 7
        high = jnp.stack([jnp.where(last, up[:, 1], up[:, 0]), jnp.where(last, ry[e, 1], up[:, 1])], axis=1)
        return low, high

    def z_sides(value, e):
        flat = value.reshape(256, 128)
        down = pltpu.roll(flat, 1, 1).reshape(16, 2, 8, 128)
        up = pltpu.roll(flat, 127, 1).reshape(16, 2, 8, 128)
        low = jnp.where(lanes4 == 0, unpack(rz[e, 0], 0), down)
        high = jnp.where(lanes4 == 127, unpack(rz[e, 1], 127), up)
        return low, high

    def pack_faces(e, read):
        zp_ref[e, 0] = pack(read, 0)
        zp_ref[e, 1] = pack(read, 127)

    pack_faces(0, lambda i: m_ref[2, i // 2, i % 2])
    copies = face_copies(0, m_ref.at[0], m_ref.at[1])
    each_face(copies, leaving, lambda copy: copy.start())
    diagonal = 6.0 + base_screen + point_screen * m_ref[3]
    diag_ref[...] = diagonal
    inv_ref[...] = 1.0 / diagonal
    each_face(copies, arriving, lambda copy: copy.wait_recv())
    low, high = x_sides(m_ref[0], 0)
    total = high - low
    low, high = y_sides(m_ref[1], 0)
    total = total + (high - low)
    low, high = z_sides(m_ref[2], 0)
    total = -0.5 * (total + (high - low))
    r_ref[...] = total
    p_ref[1] = total * inv_ref[...]
    each_face(copies, leaving, lambda copy: copy.wait_send())

    for k, (keep, push) in enumerate(sweep_factors(), 1):
        pack_faces(k, lambda i: p_ref[k, i // 2, i % 2])
        copies = face_copies(k, p_ref.at[k], p_ref.at[k])
        each_face(copies, leaving, lambda copy: copy.start())
        p = p_ref[k]
        if k == 1:
            u_ref[...] = p
        else:
            u_ref[...] += p
        each_face(copies, arriving, lambda copy: copy.wait_recv())
        around = sum(x_sides(p, k)) + sum(y_sides(p, k)) + sum(z_sides(p, k))
        r = r_ref[...] - (diag_ref[...] * p - around)
        r_ref[...] = r
        following = keep * p + push * (r * inv_ref[...])
        if k < ITERS - 1:
            p_ref[k + 1] = following
        else:
            u_ref[...] += following
        each_face(copies, leaving, lambda copy: copy.wait_send())

    zp_ref[6, 0] = pack(lambda i: u_ref[i // 2, i % 2], 0)
    layer = corner_copies(
        [u_ref.at[0], u_ref.at[:, 0, 0, :], zp_ref.at[6, 0], u_ref.at[0, 0, 0:1], zp_ref.at[6, 0], zp_ref.at[6, 0], zp_ref.at[6, 0]],
        [fx, fy, fz.at[0], fxy, fz.at[1], fz.at[2], fz.at[3]], f_send, f_recv, -1,
    )
    each(layer, lower, lambda copy: copy.start())
    each(layer, upper, lambda copy: copy.wait_recv())
    halo_ref[0:16] = fx[...].reshape(16, 128)
    halo_ref[16:32] = fy[...]
    halo_ref[32:40] = jnp.where(sub == 0, jnp.broadcast_to(fxy[...], (8, 128)), 0.0)
    halo_ref[40:48] = zero
    for i in range(32):
        uz_ref[8 * i : 8 * i + 8] = roll_to(fz[0], i, 0)
    for t in range(2):
        uz_ref[256 + 8 * t : 264 + 8 * t] = roll_to(fz[1], t, 0)
        picked = jnp.where(lane == 2 * (8 * t + sub), jnp.broadcast_to(fz[2, 0:1], (8, 128)), 0.0)
        column = jnp.sum(picked, axis=1, keepdims=True)
        uz_ref[272 + 8 * t : 280 + 8 * t] = jnp.broadcast_to(column, (8, 128))
    uz_ref[288:296] = jnp.where(sub == 0, fz[3], 0.0)
    uz_ref[296:304] = zero
    each(layer, lower, lambda copy: copy.wait_send())


def params(collective_id=None, limit=None):
    extra = {} if collective_id is None else {"collective_id": collective_id, "has_side_effects": True}
    return pltpu.CompilerParams(vmem_limit_bytes=limit or 48 * 1024 * 1024, **extra)


def on_device(sizes, point_data, point_cells, send_counts):
    data = jnp.transpose(point_data[0], (1, 2, 0))
    cells = jnp.transpose(point_cells[0], (1, 2, 0))
    dma = pltpu.SemaphoreType.DMA
    points = pl.pallas_call(
        functools.partial(route_kernel, sizes),
        out_shape=jax.ShapeDtypeStruct((CHANNELS, CAP, DEVICES), F32),
        in_specs=[vmem()] * 3,
        out_specs=vmem(),
        scratch_shapes=[pltpu.VMEM((DEVICES, WIDTH), F32)] * 2 + [pltpu.VMEM((1, WIDTH), F32), dma, dma],
        compiler_params=params(0),
        name="route",
    )(data, cells, send_counts)
    mass, over = pl.pallas_call(
        splat_kernel,
        out_shape=[jax.ShapeDtypeStruct((ROWS, 512), F32), jax.ShapeDtypeStruct((ROWS, 128), F32)],
        in_specs=[vmem()],
        out_specs=[vmem()] * 2,
        scratch_shapes=[pltpu.VMEM((ROWS, 3 * POINTS), BF16), pltpu.VMEM((528, 3 * POINTS), BF16)],
        compiler_params=params(),
        name="splat",
    )(points)
    field = (16, 2, 8, 128)
    shapes = [
        (4, *field), (2, 8, 128), (16, 512), (16, 512), (1, 512), (4, 8, 128),
        (6, *field), (7, 2, 8, 128), (6, 2, 2, 8, 128), (6, 2, 16, 1, 128), (6, 2, 8, 128), field, field, field,
        (2, 8, 128), (16, 128), (1, 128), (4, 8, 128),
    ]
    u, halo, uz = pl.pallas_call(
        functools.partial(solve_kernel, sizes),
        out_shape=[jax.ShapeDtypeStruct(s, F32) for s in (field, (48, 128), (ROWS, 128))],
        in_specs=[vmem()] * 2,
        out_specs=[vmem()] * 3,
        scratch_shapes=[pltpu.VMEM(s, F32) for s in shapes]
        + [dma((7,)), dma((7,)), dma((6, 6)), dma((6, 6)), dma((7,)), dma((7,))],
        compiler_params=params(1),
        name="solve",
    )(mass, over)
    values = pl.pallas_call(
        interp_kernel,
        out_shape=jax.ShapeDtypeStruct((CAP, DEVICES), F32),
        in_specs=[vmem()] * 4,
        out_specs=vmem(),
        scratch_shapes=[pltpu.VMEM((ROWS, 512), BF16), pltpu.VMEM((512, POINTS), BF16)],
        compiler_params=params(),
        name="interp",
    )(points, u.reshape(256, 128), halo, uz)
    returned = pl.pallas_call(
        functools.partial(return_kernel, sizes),
        out_shape=jax.ShapeDtypeStruct((CAP, DEVICES), F32),
        in_specs=[vmem()] * 2,
        out_specs=vmem(),
        scratch_shapes=[pltpu.VMEM((DEVICES, DEVICES), F32)] * 2 + [pltpu.VMEM((1, DEVICES), F32), dma, dma],
        compiler_params=params(2),
        name="give_back",
    )(values, send_counts)
    return u.reshape(16, 16, 128), returned.T[None]


def solution(mesh):
    sizes = tuple(mesh.shape[name] for name in ("gx", "gy", "gz"))
    spread_over = ("gx", "gy", "gz")
    in_specs = (P(spread_over, None, None, None), P(spread_over, None, None, None), P(spread_over, None))
    out_specs = (P("gx", "gy", "gz"), P(spread_over, None, None))
    return jax.shard_map(
        functools.partial(on_device, sizes), mesh=mesh, in_specs=in_specs, out_specs=out_specs, check_vma=False
    )
```

```python
import functools

import jax
import jax.numpy as jnp
from jax import lax
from jax.experimental import pallas as pl
from jax.experimental.pallas import tpu as pltpu
from jax.sharding import PartitionSpec as P

MESH = pl.DeviceIdType.MESH
F32 = jnp.float32
BF16 = jnp.bfloat16

DEVICES = 128
CAP = 32
CHANNELS = 10
WIDTH = 384
POINTS = 512
ROWS = 304
ITERS = 6

base_screen = 0.25
point_screen = 4.0


def sweep_factors():
    half_width = 6.0 / (6.0 + base_screen)
    rho_prev = half_width
    factors = []
    for _ in range(ITERS - 1):
        rho_next = 1.0 / (2.0 / half_width - rho_prev)
        factors.append((rho_next * rho_prev, 2.0 * rho_next / half_width))
        rho_prev = rho_next
    return factors


def position(sizes):
    return tuple(lax.axis_index(name) for name in ("gx", "gy", "gz"))


def coordinates(sizes, index):
    ny, nz = sizes[1], sizes[2]
    return (index // (ny * nz), lax.rem(index // nz, ny), lax.rem(index, nz))


def vmem():
    return pl.BlockSpec(memory_space=pltpu.VMEM)


def greet(sizes, here, relay_y, relay_x):
    barrier = pltpu.get_barrier_semaphore()

    def tell(axis, semaphore):
        for step in range(1, sizes[axis]):
            target = tuple(lax.rem(here[a] + step, sizes[a]) if a == axis else here[a] for a in range(3))
            pl.semaphore_signal(semaphore, inc=1, device_id=target, device_id_type=MESH)

    for axis in range(3):
        tell(axis, barrier)
    pl.semaphore_wait(barrier, sum(sizes) - 3)
    tell(1, relay_y)
    pl.semaphore_wait(relay_y, sizes[1] - 1)
    tell(0, relay_x)
    pl.semaphore_wait(relay_x, sizes[0] - 1)


def exchange_rows(me, send, recv, sent, send_sem, recv_sem):
    def post(step):
        other = me ^ ((step * 37) & (DEVICES - 1))
        pltpu.make_async_remote_copy(
            src_ref=send.at[pl.ds(other, 1)],
            dst_ref=recv.at[pl.ds(me, 1)],
            send_sem=send_sem,
            recv_sem=recv_sem,
            device_id=other,
            device_id_type=pl.DeviceIdType.LOGICAL,
        ).start()

    @pl.loop(0, DEVICES - 8, step=8)
    def _(step):
        for q in range(8):
            post(step + q + 1)

    for q in range(DEVICES - 7, DEVICES):
        post(q)
    pltpu.make_async_copy(send.at[pl.ds(me, 1)], recv.at[pl.ds(me, 1)], recv_sem).start()
    pltpu.make_async_copy(send.at[pl.ds(me, 1)], sent, send_sem).start()
    pltpu.make_async_copy(send, recv, recv_sem).wait()


def prepare_rows(data_ref, cells_ref, counts_ref, send):
    slot = lax.broadcasted_iota(jnp.int32, (CAP, DEVICES), 0)
    weight = jnp.where(slot < counts_ref[...], data_ref[3], 0.0)
    parts = [data_ref[c] * weight for c in range(3)] + [weight]
    parts += [data_ref[4 + c] for c in range(3)] + [cells_ref[c].astype(F32) for c in range(3)]
    parts += [jnp.zeros((WIDTH - CAP * CHANNELS, DEVICES), F32)]
    send[...] = jnp.concatenate(parts, axis=0).T


def split(value):
    high = value.astype(BF16)
    return high, (value - high.astype(F32)).astype(BF16)


def point_rows(d_ref, group, channel):
    count = POINTS // DEVICES
    rows = [d_ref[channel, pl.ds(group * count + q, 1), :] for q in range(count)]
    return jnp.concatenate(rows, axis=1)


def spread(row):
    return jnp.broadcast_to(row, (16, POINTS)).astype(BF16)


def spread_split(row):
    wide = jnp.broadcast_to(row, (16, POINTS))
    return split(wide)


def build_tiles(d_ref, group, a_ref, b_ref):
    iota = lax.broadcasted_iota(jnp.int32, (16, POINTS), 0).astype(F32).astype(BF16)
    zero = jnp.zeros((16, POINTS), BF16)

    def store_a(first, high, low):
        rows = pl.ds(first, 16)
        a_ref[rows, 0:POINTS] = high
        a_ref[rows, POINTS : 2 * POINTS] = low
        a_ref[rows, 2 * POINTS : 3 * POINTS] = high

    def store_b(first, high, low):
        rows = pl.ds(first, 16)
        b_ref[rows, 0:POINTS] = high
        b_ref[rows, POINTS : 2 * POINTS] = high
        b_ref[rows, 2 * POINTS : 3 * POINTS] = low

    v = [point_rows(d_ref, group, c) for c in range(4)]
    fx, fy, fz, cx, cy, cz = [point_rows(d_ref, group, 4 + c) for c in range(6)]
    bx, by, bz = spread(cx), spread(cy), spread(cz)
    y0, y1 = by == iota, (by + 1.0).astype(BF16) == iota
    near = [], []
    for along, out in ((1.0 - fx, 0), (fx, 1)):
        w0 = spread_split(along * (1.0 - fy))
        w1 = spread_split(along * fy)
        for part in range(2):
            near[out].append(jnp.where(y0, w0[part], jnp.where(y1, w1[part], zero)))
    for x in range(17):
        x0, x1 = bx == x, bx == x - 1
        high, low = [jnp.where(x0, near[0][part], jnp.where(x1, near[1][part], zero)) for part in range(2)]
        store_a(16 * x, high, low)
    edge = jnp.where(cy == 15.0, fy, 0.0)
    e0, e1 = spread_split((1.0 - fx) * edge), spread_split(fx * edge)
    for t in range(2):
        at = iota + jnp.asarray(16 * t, BF16)
        x0, x1 = bx == at, (bx + 1.0).astype(BF16) == at
        high, low = [jnp.where(x0, e0[part], jnp.where(x1, e1[part], zero)) for part in range(2)]
        store_a(272 + 16 * t, high, low)
    g0 = [spread_split(v[c] * (1.0 - fz)) for c in range(4)]
    g1 = [spread_split(v[c] * fz) for c in range(4)]
    for t in range(8):
        at = iota + jnp.asarray(16 * t, BF16)
        z0, z1 = bz == at, (bz + 1.0).astype(BF16) == at
        for c in range(4):
            high, low = [jnp.where(z0, g0[c][part], jnp.where(z1, g1[c][part], zero)) for part in range(2)]
            store_b(128 * c + 16 * t, high, low)
    top = bz == 127
    high, both = zero, zero
    for c in range(4):
        here = jnp.logical_and(top, iota == c)
        high = jnp.where(here, g1[c][0], high)
        both = jnp.where(jnp.logical_and(top, iota == c + 4), g1[c][1], both)
    b_ref[512:528, 0:POINTS] = jnp.where(iota < 4, high, both)
    b_ref[512:528, POINTS : 2 * POINTS] = high


def multiply_tiles(a_ref, b_ref, acc_ref, ov_ref):
    dims = (((1,), (1,)), ((), ()))
    acc_ref[...] += lax.dot_general(a_ref[...], b_ref[0:512, :], dims, preferred_element_type=F32)
    ov_ref[:, 0:16] += lax.dot_general(
        a_ref[:, 0 : 2 * POINTS], b_ref[512:528, 0 : 2 * POINTS], dims, preferred_element_type=F32
    )


def splat_points(d_ref, acc_ref, ov_ref, a0, b0, a1, b1):
    acc_ref[...] = jnp.zeros_like(acc_ref)
    ov_ref[...] = jnp.zeros_like(ov_ref)
    groups = CAP * DEVICES // POINTS
    build_tiles(d_ref, 0, a0, b0)

    @pl.loop(0, groups // 2)
    def _(pair):
        build_tiles(d_ref, 2 * pair + 1, a1, b1)
        multiply_tiles(a0, b0, acc_ref, ov_ref)
        build_tiles(d_ref, jnp.minimum(2 * pair + 2, groups - 1), a0, b0)
        multiply_tiles(a1, b1, acc_ref, ov_ref)


def interpolate(d_ref, u_ref, halo_ref, uz_ref, out_ref, l_ref, r_ref):
    for first, value in ((0, u_ref[...].reshape(256, 128)), (256, halo_ref[...])):
        rows = pl.ds(first, value.shape[0])
        high, low = split(value)
        l_ref[rows, 0:128] = high
        l_ref[rows, 128:256] = low
        l_ref[rows, 256:384] = high
    top = jnp.broadcast_to(uz_ref[:, 0:1], (ROWS, 128))
    high = top.astype(BF16).astype(F32)
    lane = lax.broadcasted_iota(jnp.int32, (ROWS, 128), 1)
    low = jnp.where(lane == 1, top - high, 0.0)
    l_ref[:, 384:512] = jnp.where(jnp.logical_or(lane == 0, lane == 2), high, low).astype(BF16)
    r_ref[400:512, :] = jnp.zeros((112, POINTS), BF16)
    iota_f = lax.broadcasted_iota(jnp.int32, (16, POINTS), 0).astype(F32)
    iota = iota_f.astype(BF16)
    zero = jnp.zeros((16, POINTS), BF16)

    @pl.loop(0, CAP * DEVICES // POINTS)
    def _(group):
        fx, fy, fz, cx, cy, cz = [point_rows(d_ref, group, 4 + c) for c in range(6)]
        bz = spread(cz)
        g0, g1 = spread_split(1.0 - fz), spread_split(fz)
        for t in range(8):
            at = iota + jnp.asarray(16 * t, BF16)
            z0, z1 = bz == at, (bz + 1.0).astype(BF16) == at
            high, low = [jnp.where(z0, g0[part], jnp.where(z1, g1[part], zero)) for part in range(2)]
            r_ref[pl.ds(16 * t, 16), :] = high
            r_ref[pl.ds(128 + 16 * t, 16), :] = high
            r_ref[pl.ds(256 + 16 * t, 16), :] = low
        top = bz == 127
        high = jnp.where(jnp.logical_and(top, iota <= 1), g1[0], zero)
        r_ref[384:400, :] = jnp.where(jnp.logical_and(top, iota == 2), g1[1], high)
        g = jnp.dot(l_ref[...], r_ref[...], preferred_element_type=F32)
        total = jnp.zeros((16, POINTS), F32)
        for x in range(17):
            hat = jnp.where(cx == x, 1.0 - fx, jnp.where(cx == x - 1, fx, 0.0))
            total = total + hat * g[16 * x : 16 * x + 16]
        hat = jnp.where(cy == iota_f, 1.0 - fy, jnp.where(cy + 1.0 == iota_f, fy, 0.0))
        total = total * hat
        edge = jnp.where(cy == 15.0, fy, 0.0)
        for t in range(2):
            at = iota_f + 16.0 * t
            hat = jnp.where(cx == at, 1.0 - fx, jnp.where(cx + 1.0 == at, fx, 0.0))
            total = total + hat * edge * g[272 + 16 * t : 288 + 16 * t]
        value = jnp.sum(total, axis=0, keepdims=True)
        count = POINTS // DEVICES
        for q in range(count):
            out_ref[pl.ds(group * count + q, 1), :] = value[:, q * DEVICES : (q + 1) * DEVICES]


def roll_to(tile, source, target):
    shift = (target - source) % 128
    return pltpu.roll(tile, shift, 1) if shift else tile


def solve(
    sizes, here, s_ref, ov_ref, u_ref, halo_ref, uz_ref,
    m_ref, zs_ref, sx, sy, sxy, sz, p_ref, zp_ref, rx, ry, rz, r_ref, inv_ref, diag_ref,
    fx, fy, fxy, fz, s_send, s_recv, h_send, h_recv, f_send, f_recv,
):
    lower = [here[a] > 0 for a in range(3)]
    upper = [here[a] < sizes[a] - 1 for a in range(3)]
    steps = [(1, 0, 0), (0, 1, 0), (0, 0, 1), (1, 1, 0), (1, 0, 1), (0, 1, 1), (1, 1, 1)]

    def all_of(flags, step):
        wanted = [flags[a] for a in range(3) if step[a]]
        return functools.reduce(jnp.logical_and, wanted)

    def shifted(step, sign):
        return tuple(here[a] + sign * step[a] for a in range(3))

    lane = lax.broadcasted_iota(jnp.int32, (8, 128), 1)
    sub = lax.broadcasted_iota(jnp.int32, (8, 128), 0)
    zero = jnp.zeros((8, 128), F32)

    for a, bufs in ((0, (sx, rx.at[:, 0])), (1, (sy, ry.at[:, 0])), (2, (sz.at[0], rz.at[:, 0]))):
        @pl.when(jnp.logical_not(lower[a]))
        def _(bufs=bufs):
            for buf in bufs:
                buf[...] = jnp.zeros(buf.shape, F32)
    for a, bufs in ((0, (fx, rx.at[:, 1])), (1, (fy, ry.at[:, 1])), (2, (fz.at[0], rz.at[:, 1]))):
        @pl.when(jnp.logical_not(upper[a]))
        def _(bufs=bufs):
            for buf in bufs:
                buf[...] = jnp.zeros(buf.shape, F32)
    for step, low_buf, high_buf in (
        (steps[3], sxy, fxy), (steps[4], sz.at[1], fz.at[1]),
        (steps[5], sz.at[2], fz.at[2]), (steps[6], sz.at[3], fz.at[3]),
    ):
        for flags, buf in ((lower, low_buf), (upper, high_buf)):
            @pl.when(jnp.logical_not(all_of(flags, step)))
            def _(buf=buf):
                buf[...] = jnp.zeros(buf.shape, F32)

    for part, tiles in ((0, 32), (1, 5)):
        packed = zero
        for i in range(tiles):
            tile = ov_ref[pl.ds(256 * part + 8 * i, 8), :]
            tile = tile + pltpu.roll(tile, 124, 1)
            here_lanes = jnp.logical_and(lane >= 4 * i, lane < 4 * i + 4)
            packed = jnp.where(here_lanes, roll_to(tile, 0, 4 * i), packed)
        zs_ref[part] = packed
    for c in range(4):
        m_ref[c] = s_ref[0:256, 128 * c : 128 * c + 128].reshape(16, 2, 8, 128)

    def corner_copies(sources, targets, send, recv, sign):
        copies = []
        for i, step in enumerate(steps):
            copies.append(pltpu.make_async_remote_copy(
                src_ref=sources[i], dst_ref=targets[i], send_sem=send.at[i], recv_sem=recv.at[i],
                device_id=shifted(step, sign), device_id_type=MESH,
            ))
        return copies

    def each(copies, flags, action):
        for copy, step in zip(copies, steps):
            @pl.when(all_of(flags, step))
            def _(copy=copy):
                action(copy)

    mass = corner_copies(
        [s_ref.at[256:272], s_ref.at[272:288], zs_ref.at[0], s_ref.at[288:289], zs_ref.at[1], zs_ref.at[1], zs_ref.at[1]],
        [sx, sy, sz.at[0], sxy, sz.at[1], sz.at[2], sz.at[3]], s_send, s_recv, 1,
    )
    each(mass, upper, lambda copy: copy.start())
    each(mass, lower, lambda copy: copy.wait_recv())

    for c in range(4):
        columns = slice(128 * c, 128 * c + 128)
        m_ref[c, 0] += sx[:, columns].reshape(2, 8, 128)
        from_y = sy[:, columns]
        near_z = [roll_to(sz[2], 8 + 4 * t + c, 0) for t in range(2)]
        for x in range(16):
            row = from_y[x : x + 1, :] + jnp.where(lane[0:1] == 0, near_z[x // 8][x % 8 : x % 8 + 1, :], 0.0)
            m_ref[c, x, 0, 0:1, :] += row
        for i in range(32):
            m_ref[c, i // 2, i % 2] += jnp.where(lane == 0, roll_to(sz[0], 4 * i + c, 0), 0.0)
        for t in range(2):
            m_ref[c, 0, t] += jnp.where(lane == 0, roll_to(sz[1], 4 * t + c, 0), 0.0)
        corner = sxy[:, columns] + jnp.where(lane[0:1] == 0, roll_to(sz[3], 16 + c, 0)[0:1], 0.0)
        m_ref[c, 0, 0, 0:1, :] += corner
    each(mass, upper, lambda copy: copy.wait_send())

    def pack(read, source):
        packed = zero
        for i in range(32):
            packed = jnp.where(lane == i, roll_to(read(i), source, i), packed)
        return packed

    def unpack(packed, target):
        mine = lane == target
        tiles = [jnp.where(mine, roll_to(packed, i, target), 0.0) for i in range(32)]
        return jnp.stack(tiles).reshape(16, 2, 8, 128)

    def face_copies(e, xs, ys):
        sources = [xs.at[15], xs.at[0], ys.at[:, 1, 7, :], ys.at[:, 0, 0, :], zp_ref.at[e, 1], zp_ref.at[e, 0]]
        targets = [rx.at[e, 0], rx.at[e, 1], ry.at[e, 0, :, 0, :], ry.at[e, 1, :, 0, :], rz.at[e, 0], rz.at[e, 1]]
        copies = []
        for d in range(6):
            step = tuple(int(a == d // 2) for a in range(3))
            copies.append(pltpu.make_async_remote_copy(
                src_ref=sources[d], dst_ref=targets[d], send_sem=h_send.at[e, d], recv_sem=h_recv.at[e, d],
                device_id=shifted(step, 1 - 2 * (d % 2)), device_id_type=MESH,
            ))
        return copies

    def arriving(d):
        return (lower, upper)[d % 2][d // 2]

    def leaving(d):
        return (upper, lower)[d % 2][d // 2]

    def each_face(copies, when, action):
        for d, copy in enumerate(copies):
            @pl.when(when(d))
            def _(copy=copy):
                action(copy)

    lanes4 = lax.broadcasted_iota(jnp.int32, (16, 2, 8, 128), 3)
    subs3 = lax.broadcasted_iota(jnp.int32, (16, 8, 128), 1)

    def x_sides(value, e):
        low = jnp.concatenate([rx[e, 0][None], value[:-1]], axis=0)
        high = jnp.concatenate([value[1:], rx[e, 1][None]], axis=0)
        return low, high

    def y_sides(value, e):
        down = pltpu.roll(value.reshape(32, 8, 128), 1, 1).reshape(16, 2, 8, 128)
        up = pltpu.roll(value.reshape(32, 8, 128), 7, 1).reshape(16, 2, 8, 128)
        first = subs3 == 0
        low = jnp.stack([jnp.where(first, ry[e, 0], down[:, 0]), jnp.where(first, down[:, 0], down[:, 1])], axis=1)
        last = subs3 == 7
        high = jnp.stack([jnp.where(last, up[:, 1], up[:, 0]), jnp.where(last, ry[e, 1], up[:, 1])], axis=1)
        return low, high

    def z_sides(value, e):
        flat = value.reshape(256, 128)
        down = pltpu.roll(flat, 1, 1).reshape(16, 2, 8, 128)
        up = pltpu.roll(flat, 127, 1).reshape(16, 2, 8, 128)
        low = jnp.where(lanes4 == 0, unpack(rz[e, 0], 0), down)
        high = jnp.where(lanes4 == 127, unpack(rz[e, 1], 127), up)
        return low, high

    def pack_faces(e, read):
        zp_ref[e, 0] = pack(read, 0)
        zp_ref[e, 1] = pack(read, 127)

    pack_faces(0, lambda i: m_ref[2, i // 2, i % 2])
    copies = face_copies(0, m_ref.at[0], m_ref.at[1])
    each_face(copies, leaving, lambda copy: copy.start())
    diagonal = 6.0 + base_screen + point_screen * m_ref[3]
    diag_ref[...] = diagonal
    inv_ref[...] = 1.0 / diagonal
    each_face(copies, arriving, lambda copy: copy.wait_recv())
    low, high = x_sides(m_ref[0], 0)
    total = high - low
    low, high = y_sides(m_ref[1], 0)
    total = total + (high - low)
    low, high = z_sides(m_ref[2], 0)
    total = -0.5 * (total + (high - low))
    r_ref[...] = total
    p_ref[1] = total * inv_ref[...]
    each_face(copies, leaving, lambda copy: copy.wait_send())

    for k, (keep, push) in enumerate(sweep_factors(), 1):
        pack_faces(k, lambda i: p_ref[k, i // 2, i % 2])
        copies = face_copies(k, p_ref.at[k], p_ref.at[k])
        each_face(copies, leaving, lambda copy: copy.start())
        p = p_ref[k]
        if k == 1:
            u_ref[...] = p
        else:
            u_ref[...] += p
        each_face(copies, arriving, lambda copy: copy.wait_recv())
        around = sum(x_sides(p, k)) + sum(y_sides(p, k)) + sum(z_sides(p, k))
        r = r_ref[...] - (diag_ref[...] * p - around)
        r_ref[...] = r
        following = keep * p + push * (r * inv_ref[...])
        if k < ITERS - 1:
            p_ref[k + 1] = following
        else:
            u_ref[...] += following
        each_face(copies, leaving, lambda copy: copy.wait_send())

    zp_ref[6, 0] = pack(lambda i: u_ref[i // 2, i % 2], 0)
    layer = corner_copies(
        [u_ref.at[0], u_ref.at[:, 0, 0, :], zp_ref.at[6, 0], u_ref.at[0, 0, 0:1], zp_ref.at[6, 0], zp_ref.at[6, 0], zp_ref.at[6, 0]],
        [fx, fy, fz.at[0], fxy, fz.at[1], fz.at[2], fz.at[3]], f_send, f_recv, -1,
    )
    each(layer, lower, lambda copy: copy.start())
    each(layer, upper, lambda copy: copy.wait_recv())
    halo_ref[0:16] = fx[...].reshape(16, 128)
    halo_ref[16:32] = fy[...]
    halo_ref[32:40] = jnp.where(sub == 0, jnp.broadcast_to(fxy[...], (8, 128)), 0.0)
    halo_ref[40:48] = zero
    for i in range(32):
        uz_ref[8 * i : 8 * i + 8] = roll_to(fz[0], i, 0)
    for t in range(2):
        uz_ref[256 + 8 * t : 264 + 8 * t] = roll_to(fz[1], t, 0)
        picked = jnp.where(lane == 2 * (8 * t + sub), jnp.broadcast_to(fz[2, 0:1], (8, 128)), 0.0)
        column = jnp.sum(picked, axis=1, keepdims=True)
        uz_ref[272 + 8 * t : 280 + 8 * t] = jnp.broadcast_to(column, (8, 128))
    uz_ref[288:296] = jnp.where(sub == 0, fz[3], 0.0)
    uz_ref[296:304] = zero
    each(layer, lower, lambda copy: copy.wait_send())


def kernel(sizes, data_hbm, cells_hbm, counts_hbm, u_ref, out_ref, *scratch):
    (data_ref, cells_ref, counts_ref, send, recv, sent, d_ref, a0, b0, a1, b1, acc_ref, ov_ref,
     l_ref, r_ref, halo_ref, uz_ref, val_ref, back_send, back_recv, back_sent,
     in_sem, send_sem, recv_sem, relay_y, relay_x, *rest) = scratch
    here = position(sizes)
    me = (here[0] * sizes[1] + here[1]) * sizes[2] + here[2]
    loads = [
        pltpu.make_async_copy(source, target, in_sem.at[i])
        for i, (source, target) in enumerate(((data_hbm, data_ref), (cells_hbm, cells_ref), (counts_hbm, counts_ref)))
    ]
    for load in loads:
        load.start()
    for load in loads:
        load.wait()
    prepare_rows(data_ref, cells_ref, counts_ref, send)
    greet(sizes, here, relay_y, relay_x)
    exchange_rows(me, send, recv, sent, send_sem.at[0], recv_sem.at[0])
    d_ref[...] = recv[...].T[: CAP * CHANNELS].reshape(CHANNELS, CAP, DEVICES)
    splat_points(d_ref, acc_ref, ov_ref, a0, b0, a1, b1)
    solve(sizes, here, acc_ref, ov_ref, u_ref, halo_ref, uz_ref, *rest)
    interpolate(d_ref, u_ref, halo_ref, uz_ref, val_ref, l_ref, r_ref)
    padded = jnp.concatenate([val_ref[...], jnp.zeros((DEVICES - CAP, DEVICES), F32)], axis=0)
    back_send[...] = padded.T
    exchange_rows(me, back_send, back_recv, back_sent, send_sem.at[1], recv_sem.at[1])
    slot = lax.broadcasted_iota(jnp.int32, (CAP, DEVICES), 0)
    out_ref[...] = jnp.where(slot < counts_ref[...], back_recv[...].T[:CAP], 0.0)
    pltpu.make_async_copy(send, recv, send_sem.at[0]).wait()
    pltpu.make_async_copy(back_send, back_recv, send_sem.at[1]).wait()


def on_device(sizes, point_data, point_cells, send_counts):
    data = jnp.transpose(point_data[0], (1, 2, 0))
    cells = jnp.transpose(point_cells[0], (1, 2, 0))
    dma, regular = pltpu.SemaphoreType.DMA, pltpu.SemaphoreType.REGULAR
    field = (16, 2, 8, 128)
    shapes = [
        ((7, CAP, DEVICES), F32), ((3, CAP, DEVICES), jnp.int32), ((1, DEVICES), jnp.int32),
        ((DEVICES, WIDTH), F32), ((DEVICES, WIDTH), F32), ((1, WIDTH), F32), ((CHANNELS, CAP, DEVICES), F32),
        ((ROWS, 3 * POINTS), BF16), ((528, 3 * POINTS), BF16), ((ROWS, 3 * POINTS), BF16), ((528, 3 * POINTS), BF16),
        ((ROWS, 512), F32), ((ROWS, 128), F32), ((ROWS, 512), BF16), ((512, POINTS), BF16),
        ((48, 128), F32), ((ROWS, 128), F32), ((CAP, DEVICES), F32),
        ((DEVICES, DEVICES), F32), ((DEVICES, DEVICES), F32), ((1, DEVICES), F32),
    ]
    halo_shapes = [
        (4, *field), (2, 8, 128), (16, 512), (16, 512), (1, 512), (4, 8, 128),
        (6, *field), (7, 2, 8, 128), (6, 2, 2, 8, 128), (6, 2, 16, 1, 128), (6, 2, 8, 128), field, field, field,
        (2, 8, 128), (16, 128), (1, 128), (4, 8, 128),
    ]
    u, returned = pl.pallas_call(
        functools.partial(kernel, sizes),
        out_shape=[jax.ShapeDtypeStruct(s, F32) for s in (field, (CAP, DEVICES))],
        in_specs=[pl.BlockSpec(memory_space=pl.ANY)] * 3,
        out_specs=[vmem()] * 2,
        scratch_shapes=[pltpu.VMEM(*s) for s in shapes]
        + [dma((3,)), dma((2,)), dma((2,)), regular, regular]
        + [pltpu.VMEM(s, F32) for s in halo_shapes]
        + [dma((7,)), dma((7,)), dma((6, 6)), dma((6, 6)), dma((7,)), dma((7,))],
        compiler_params=pltpu.CompilerParams(
            vmem_limit_bytes=24 * 1024 * 1024, collective_id=0, has_side_effects=True
        ),
        name="reconstruct",
    )(data, cells, send_counts)
    return u.reshape(16, 16, 128), returned.T[None]


def solution(mesh):
    sizes = tuple(mesh.shape[name] for name in ("gx", "gy", "gz"))
    spread_over = ("gx", "gy", "gz")
    in_specs = (P(spread_over, None, None, None), P(spread_over, None, None, None), P(spread_over, None))
    out_specs = (P("gx", "gy", "gz"), P(spread_over, None, None))
    return jax.shard_map(
        functools.partial(on_device, sizes), mesh=mesh, in_specs=in_specs, out_specs=out_specs, check_vma=False
    )
```

```python
import functools

import jax
import jax.numpy as jnp
from jax import lax
from jax.experimental import pallas as pl
from jax.experimental.pallas import tpu as pltpu
from jax.sharding import PartitionSpec as P

MESH = pl.DeviceIdType.MESH
F32 = jnp.float32
BF16 = jnp.bfloat16

DEVICES = 128
CAP = 32
CHANNELS = 10
WIDTH = 384
POINTS = 512
ROWS = 304
ITERS = 6

base_screen = 0.25
point_screen = 4.0


def sweep_factors():
    half_width = 6.0 / (6.0 + base_screen)
    rho_prev = half_width
    factors = []
    for _ in range(ITERS - 1):
        rho_next = 1.0 / (2.0 / half_width - rho_prev)
        factors.append((rho_next * rho_prev, 2.0 * rho_next / half_width))
        rho_prev = rho_next
    return factors


def position(sizes):
    return tuple(lax.axis_index(name) for name in ("gx", "gy", "gz"))


def vmem():
    return pl.BlockSpec(memory_space=pltpu.VMEM)


def greet(me, meanwhile):
    barrier = pltpu.get_barrier_semaphore()

    @pl.loop(0, DEVICES - 8, step=8)
    def _(step):
        for q in range(8):
            pl.semaphore_signal(barrier, inc=1, device_id=me ^ (step + q + 1), device_id_type=pl.DeviceIdType.LOGICAL)

    for q in range(DEVICES - 7, DEVICES):
        pl.semaphore_signal(barrier, inc=1, device_id=me ^ q, device_id_type=pl.DeviceIdType.LOGICAL)
    meanwhile()
    pl.semaphore_wait(barrier, DEVICES - 1)


def exchange_rows(me, send, recv, sent, send_sem, recv_sem):
    def post(step):
        other = me ^ ((step * 37) & (DEVICES - 1))
        pltpu.make_async_remote_copy(
            src_ref=send.at[pl.ds(other, 1)],
            dst_ref=recv.at[pl.ds(me, 1)],
            send_sem=send_sem,
            recv_sem=recv_sem,
            device_id=other,
            device_id_type=pl.DeviceIdType.LOGICAL,
        ).start()

    @pl.loop(0, DEVICES - 8, step=8)
    def _(step):
        for q in range(8):
            post(step + q + 1)

    for q in range(DEVICES - 7, DEVICES):
        post(q)
    pltpu.make_async_copy(send.at[pl.ds(me, 1)], recv.at[pl.ds(me, 1)], recv_sem).start()
    pltpu.make_async_copy(send.at[pl.ds(me, 1)], sent, send_sem).start()
    pltpu.make_async_copy(send, recv, recv_sem).wait()


def prepare_rows(data_ref, cells_ref, counts_ref, send):
    slot = lax.broadcasted_iota(jnp.int32, (CAP, DEVICES), 0)
    weight = jnp.where(slot < counts_ref[...], data_ref[3], 0.0)
    parts = [data_ref[c] * weight for c in range(3)] + [weight]
    parts += [data_ref[4 + c] for c in range(3)] + [cells_ref[c].astype(F32) for c in range(3)]
    parts += [jnp.zeros((WIDTH - CAP * CHANNELS, DEVICES), F32)]
    send[...] = jnp.concatenate(parts, axis=0).T


def split(value):
    high = value.astype(BF16)
    return high, (value - high.astype(F32)).astype(BF16)


def point_rows(d_ref, group, channel):
    count = POINTS // DEVICES
    rows = [d_ref[channel, pl.ds(group * count + q, 1), :] for q in range(count)]
    return jnp.concatenate(rows, axis=1)


def spread(row):
    return jnp.broadcast_to(row, (16, POINTS)).astype(BF16)


def spread_split(row):
    wide = jnp.broadcast_to(row, (16, POINTS))
    return split(wide)


def build_tiles(d_ref, group, a_ref, b_ref):
    iota = lax.broadcasted_iota(jnp.int32, (16, POINTS), 0).astype(F32).astype(BF16)
    zero = jnp.zeros((16, POINTS), BF16)

    def store_a(first, high, low):
        rows = pl.ds(first, 16)
        a_ref[rows, 0:POINTS] = high
        a_ref[rows, POINTS : 2 * POINTS] = low
        a_ref[rows, 2 * POINTS : 3 * POINTS] = high

    def store_b(first, high, low):
        rows = pl.ds(first, 16)
        b_ref[rows, 0:POINTS] = high
        b_ref[rows, POINTS : 2 * POINTS] = high
        b_ref[rows, 2 * POINTS : 3 * POINTS] = low

    v = [point_rows(d_ref, group, c) for c in range(4)]
    fx, fy, fz, cx, cy, cz = [point_rows(d_ref, group, 4 + c) for c in range(6)]
    bx, by, bz = spread(cx), spread(cy), spread(cz)
    y0, y1 = by == iota, (by + 1.0).astype(BF16) == iota
    near = [], []
    for along, out in ((1.0 - fx, 0), (fx, 1)):
        w0 = spread_split(along * (1.0 - fy))
        w1 = spread_split(along * fy)
        for part in range(2):
            near[out].append(jnp.where(y0, w0[part], jnp.where(y1, w1[part], zero)))
    for x in range(17):
        x0, x1 = bx == x, bx == x - 1
        high, low = [jnp.where(x0, near[0][part], jnp.where(x1, near[1][part], zero)) for part in range(2)]
        store_a(16 * x, high, low)
    edge = jnp.where(cy == 15.0, fy, 0.0)
    e0, e1 = spread_split((1.0 - fx) * edge), spread_split(fx * edge)
    for t in range(2):
        at = iota + jnp.asarray(16 * t, BF16)
        x0, x1 = bx == at, (bx + 1.0).astype(BF16) == at
        high, low = [jnp.where(x0, e0[part], jnp.where(x1, e1[part], zero)) for part in range(2)]
        store_a(272 + 16 * t, high, low)
    g0 = [spread_split(v[c] * (1.0 - fz)) for c in range(4)]
    g1 = [spread_split(v[c] * fz) for c in range(4)]
    for t in range(8):
        at = iota + jnp.asarray(16 * t, BF16)
        z0, z1 = bz == at, (bz + 1.0).astype(BF16) == at
        for c in range(4):
            high, low = [jnp.where(z0, g0[c][part], jnp.where(z1, g1[c][part], zero)) for part in range(2)]
            store_b(128 * c + 16 * t, high, low)
    top = bz == 127
    high, both = zero, zero
    for c in range(4):
        here = jnp.logical_and(top, iota == c)
        high = jnp.where(here, g1[c][0], high)
        both = jnp.where(jnp.logical_and(top, iota == c + 4), g1[c][1], both)
    b_ref[512:528, 0:POINTS] = jnp.where(iota < 4, high, both)
    b_ref[512:528, POINTS : 2 * POINTS] = high


def multiply_tiles(a_ref, b_ref, acc_ref, ov_ref):
    dims = (((1,), (1,)), ((), ()))
    acc_ref[...] += lax.dot_general(a_ref[...], b_ref[0:512, :], dims, preferred_element_type=F32)
    ov_ref[:, 0:16] += lax.dot_general(
        a_ref[:, 0 : 2 * POINTS], b_ref[512:528, 0 : 2 * POINTS], dims, preferred_element_type=F32
    )


def splat_points(d_ref, acc_ref, ov_ref, a0, b0, a1, b1):
    acc_ref[...] = jnp.zeros_like(acc_ref)
    ov_ref[...] = jnp.zeros_like(ov_ref)
    groups = CAP * DEVICES // POINTS
    build_tiles(d_ref, 0, a0, b0)

    @pl.loop(0, groups // 2)
    def _(pair):
        build_tiles(d_ref, 2 * pair + 1, a1, b1)
        multiply_tiles(a0, b0, acc_ref, ov_ref)
        build_tiles(d_ref, jnp.minimum(2 * pair + 2, groups - 1), a0, b0)
        multiply_tiles(a1, b1, acc_ref, ov_ref)


def interpolate(d_ref, u_ref, halo_ref, uz_ref, out_ref, l_ref, r_ref):
    for first, value in ((0, u_ref[...].reshape(256, 128)), (256, halo_ref[...])):
        rows = pl.ds(first, value.shape[0])
        high, low = split(value)
        l_ref[rows, 0:128] = high
        l_ref[rows, 128:256] = low
        l_ref[rows, 256:384] = high
    top = jnp.broadcast_to(uz_ref[:, 0:1], (ROWS, 128))
    high = top.astype(BF16).astype(F32)
    lane = lax.broadcasted_iota(jnp.int32, (ROWS, 128), 1)
    low = jnp.where(lane == 1, top - high, 0.0)
    l_ref[:, 384:512] = jnp.where(jnp.logical_or(lane == 0, lane == 2), high, low).astype(BF16)
    r_ref[400:512, :] = jnp.zeros((112, POINTS), BF16)
    iota_f = lax.broadcasted_iota(jnp.int32, (16, POINTS), 0).astype(F32)
    iota = iota_f.astype(BF16)
    zero = jnp.zeros((16, POINTS), BF16)

    @pl.loop(0, CAP * DEVICES // POINTS)
    def _(group):
        fx, fy, fz, cx, cy, cz = [point_rows(d_ref, group, 4 + c) for c in range(6)]
        bz = spread(cz)
        g0, g1 = spread_split(1.0 - fz), spread_split(fz)
        for t in range(8):
            at = iota + jnp.asarray(16 * t, BF16)
            z0, z1 = bz == at, (bz + 1.0).astype(BF16) == at
            high, low = [jnp.where(z0, g0[part], jnp.where(z1, g1[part], zero)) for part in range(2)]
            r_ref[pl.ds(16 * t, 16), :] = high
            r_ref[pl.ds(128 + 16 * t, 16), :] = high
            r_ref[pl.ds(256 + 16 * t, 16), :] = low
        top = bz == 127
        high = jnp.where(jnp.logical_and(top, iota <= 1), g1[0], zero)
        r_ref[384:400, :] = jnp.where(jnp.logical_and(top, iota == 2), g1[1], high)
        g = jnp.dot(l_ref[...], r_ref[...], preferred_element_type=F32)
        total = jnp.zeros((16, POINTS), F32)
        for x in range(17):
            hat = jnp.where(cx == x, 1.0 - fx, jnp.where(cx == x - 1, fx, 0.0))
            total = total + hat * g[16 * x : 16 * x + 16]
        hat = jnp.where(cy == iota_f, 1.0 - fy, jnp.where(cy + 1.0 == iota_f, fy, 0.0))
        total = total * hat
        edge = jnp.where(cy == 15.0, fy, 0.0)
        for t in range(2):
            at = iota_f + 16.0 * t
            hat = jnp.where(cx == at, 1.0 - fx, jnp.where(cx + 1.0 == at, fx, 0.0))
            total = total + hat * edge * g[272 + 16 * t : 288 + 16 * t]
        value = jnp.sum(total, axis=0, keepdims=True)
        count = POINTS // DEVICES
        for q in range(count):
            out_ref[pl.ds(group * count + q, 1), :] = value[:, q * DEVICES : (q + 1) * DEVICES]


FACES = [(1, 0, 0), (0, 1, 0), (0, 0, 1)]
UPPER = FACES + [(1, 1, 0), (1, 0, 1), (0, 1, 1), (1, 1, 1)]


def roll_to(tile, source, target):
    shift = (target - source) % 128
    return pltpu.roll(tile, shift, 1) if shift else tile


def grid_iotas():
    lane = lax.broadcasted_iota(jnp.int32, (8, 128), 1)
    sub = lax.broadcasted_iota(jnp.int32, (8, 128), 0)
    return lane, sub


def pack(read, source):
    lane, _ = grid_iotas()
    packed = jnp.zeros((8, 128), F32)
    for i in range(32):
        packed = jnp.where(lane == i, roll_to(read(i), source, i), packed)
    return packed


def slab_star(comb, along_x, along_y, along_z, rows, tiles):
    n = along_y.shape[0]
    total = comb(along_x[0:n], along_x[2 : n + 2])
    sub3 = lax.broadcasted_iota(jnp.int32, (n, 8, 128), 1)
    down = pltpu.roll(along_y.reshape(2 * n, 8, 128), 1, 1).reshape(n, 2, 8, 128)
    up = pltpu.roll(along_y.reshape(2 * n, 8, 128), 7, 1).reshape(n, 2, 8, 128)
    edge = [jnp.stack([rows(side, i) for i in range(n)]) for side in range(2)]
    first, last = sub3 == 0, sub3 == 7
    low = jnp.stack([jnp.where(first, edge[0], down[:, 0]), jnp.where(first, down[:, 0], down[:, 1])], axis=1)
    high = jnp.stack([jnp.where(last, up[:, 1], up[:, 0]), jnp.where(last, edge[1], up[:, 1])], axis=1)
    total = total + comb(low, high)
    lanes = lax.broadcasted_iota(jnp.int32, (2 * n, 8, 128), 2)
    flat = along_z.reshape(16 * n, 128)
    sides = []
    for side, shift, at in ((0, 1, 0), (1, 127, 127)):
        edge = jnp.stack([tiles(side, i, t) for i in range(n) for t in range(2)])
        sides.append(jnp.where(lanes == at, edge, pltpu.roll(flat, shift, 1).reshape(2 * n, 8, 128)))
    return total + comb(*sides).reshape(n, 2, 8, 128)


def layer_star_y(comb, side, fx, fy, fz):
    row = lax.broadcasted_iota(jnp.int32, (16, 128), 0)
    lane16 = lax.broadcasted_iota(jnp.int32, (16, 128), 1)
    plane = fx["plane"][side]
    low = jnp.where(row == 0, jnp.broadcast_to(fx["xy"][0][side], (16, 128)), pltpu.roll(plane, 1, 0))
    high = jnp.where(row == 15, jnp.broadcast_to(fx["xy"][1][side], (16, 128)), pltpu.roll(plane, 15, 0))
    total = comb(low, high)
    outer, own = fy["plane2"][side], fy["own_row"][side]
    total = total + (comb(outer, own) if side == 0 else comb(own, outer))
    plane = fz["plane"][side]
    parity, source = (1, 7) if side == 0 else (0, 0)
    sides = []
    for z_side, shift, at in ((0, 1, 0), (1, 127, 127)):
        values = jnp.broadcast_to(fz["yz"][side][z_side][source : source + 1], (16, 128))
        column = jnp.sum(jnp.where(lane16 == 2 * row + parity, values, 0.0), axis=1, keepdims=True)
        sides.append(jnp.where(lane16 == at, jnp.broadcast_to(column, (16, 128)), pltpu.roll(plane, shift, 1)))
    return total + comb(*sides)


def layer_star_z(comb, side, fx, fy, fz):
    lane, sub = grid_iotas()
    layer = fx["zp"][side]
    low = jnp.where(lane < 2, roll_to(fx["xz"][0][side], 30, 0), pltpu.roll(layer, 2, 1))
    high = jnp.where(lane >= 30, roll_to(fx["xz"][1][side], 0, 30), pltpu.roll(layer, 126, 1))
    total = comb(low, high)
    layer = fy["zp"][side]
    down, up = pltpu.roll(layer, 1, 0), pltpu.roll(layer, 7, 0)
    odd = lax.rem(lane, 2) == 1
    beyond = pltpu.roll(pltpu.roll(fy["yz"][0][side], 1, 0), 127, 1)
    low = jnp.where(sub == 0, jnp.where(odd, pltpu.roll(down, 1, 1), beyond), down)
    beyond = pltpu.roll(pltpu.roll(fy["yz"][1][side], 7, 0), 1, 1)
    high = jnp.where(sub == 7, jnp.where(odd, beyond, pltpu.roll(up, 127, 1)), up)
    total = total + comb(low, high)
    outer, own = fz["zp2"][side], fz["own_z"][side]
    total = total + (comb(outer, own) if side == 0 else comb(own, outer))
    return jnp.where(lane < 32, total, 0.0)


def solve(
    sizes, here, s_ref, ov_ref, u_ref, halo_ref, uz_ref,
    m_ref, zs_ref, sx, sy, sxy, sz,
    z5, xa, xb, ya, yb, exy, za, exz, eyz,
    pw, rw, z3, px, rx, py, py2, ry, pxy, pz, pxz, pyz, inv_ref, diag_ref, plane_ref, uzp,
    fx, fy, fxy, fz, s_send, s_recv, g_send, g_recv, h_send, h_recv, f_send, f_recv,
):
    lower = [here[a] > 0 for a in range(3)]
    upper = [here[a] < sizes[a] - 1 for a in range(3)]

    def present(step):
        wanted = [(upper if step[a] > 0 else lower)[a] for a in range(3) if step[a]]
        return functools.reduce(jnp.logical_and, wanted)

    def opposite(step):
        return tuple(-v for v in step)

    def message(step, source, target, send, recv):
        copy = pltpu.make_async_remote_copy(
            src_ref=source, dst_ref=target, send_sem=send, recv_sem=recv,
            device_id=tuple(here[a] + step[a] for a in range(3)), device_id_type=MESH,
        )
        return step, copy

    def start(messages):
        for step, copy in messages:
            @pl.when(present(step))
            def _(copy=copy):
                copy.start()

    def receive(messages):
        for step, copy in messages:
            @pl.when(present(opposite(step)))
            def _(copy=copy):
                copy.wait_recv()

    def drain(messages):
        for step, copy in messages:
            @pl.when(present(step))
            def _(copy=copy):
                copy.wait_send()

    lane, sub = grid_iotas()
    zero = jnp.zeros((8, 128), F32)

    for part, tiles in ((0, 32), (1, 5)):
        packed = zero
        for i in range(tiles):
            tile = ov_ref[pl.ds(256 * part + 8 * i, 8), :]
            tile = tile + pltpu.roll(tile, 124, 1)
            here_lanes = jnp.logical_and(lane >= 4 * i, lane < 4 * i + 4)
            packed = jnp.where(here_lanes, roll_to(tile, 0, 4 * i), packed)
        zs_ref[part] = packed
    sources = [s_ref.at[256:272], s_ref.at[272:288], zs_ref.at[0], s_ref.at[288:289]] + [zs_ref.at[1]] * 3
    targets = [sx, sy, sz.at[0], sxy, sz.at[1], sz.at[2], sz.at[3]]
    mass = [message(UPPER[i], sources[i], targets[i], s_send.at[i], s_recv.at[i]) for i in range(7)]
    start(mass[::-1])
    for c in range(4):
        m_ref[c] = s_ref[0:256, 128 * c : 128 * c + 128].reshape(16, 2, 8, 128)
    receive(mass)
    for c in range(4):
        columns = slice(128 * c, 128 * c + 128)
        m_ref[c, 0] += sx[:, columns].reshape(2, 8, 128)
        from_y = sy[:, columns]
        near_z = [roll_to(sz[2], 8 + 4 * t + c, 0) for t in range(2)]
        for x in range(16):
            row = from_y[x : x + 1, :] + jnp.where(lane[0:1] == 0, near_z[x // 8][x % 8 : x % 8 + 1, :], 0.0)
            m_ref[c, x, 0, 0:1, :] += row
        for i in range(32):
            m_ref[c, i // 2, i % 2] += jnp.where(lane == 0, roll_to(sz[0], 4 * i + c, 0), 0.0)
        for t in range(2):
            m_ref[c, 0, t] += jnp.where(lane == 0, roll_to(sz[1], 4 * t + c, 0), 0.0)
        corner = sxy[:, columns] + jnp.where(lane[0:1] == 0, roll_to(sz[3], 16 + c, 0)[0:1], 0.0)
        m_ref[c, 0, 0, 0:1, :] += corner

    def end(side, depth, size):
        return size - 1 - depth if side == 0 else depth

    def toward(side):
        return 1 if side == 0 else -1

    def mesh_step(**sides):
        return tuple(toward(sides[name]) if name in sides else 0 for name in "xyz")

    def numbered(entries, send, recv):
        return [message(step, a, b, send.at[i], recv.at[i]) for i, (step, a, b) in enumerate(entries)]

    for side in range(2):
        for i, (c, depth) in enumerate(((0, 0), (2, 0), (1, 0), (3, 0), (2, 1))):
            z5[side, i] = pack(lambda k, c=c: m_ref[c, k // 2, k % 2], end(side, depth, 128))
    entries = []
    for a in range(2):
        for b in range(2):
            entries.append((mesh_step(x=a, y=b), m_ref.at[0:2, end(a, 0, 16), 1 - b, 7 - 7 * b, :], exy.at[a, b]))
            entries.append((mesh_step(x=a, z=b), z5.at[b, 0:2], exz.at[a, b]))
            entries.append((mesh_step(y=a, z=b), z5.at[b, 1:3], eyz.at[a, b]))
    for a in range(2):
        first = 14 if a == 0 else 0
        entries.append((mesh_step(x=a), m_ref.at[0, first : first + 2], xa.at[a]))
        entries.append((mesh_step(x=a), m_ref.at[1:4, end(a, 0, 16)], xb.at[a]))
        entries.append((mesh_step(y=a), m_ref.at[:, :, 1 - a, 7 - 7 * a, :], ya.at[a]))
        entries.append((mesh_step(y=a), m_ref.at[1, :, 1 - a, 6 - 5 * a, :], yb.at[a]))
        entries.append((mesh_step(z=a), z5.at[a], za.at[a]))
    ghost = numbered(entries, g_send, g_recv)
    start(ghost)
    receive(ghost)

    def tiles_of(zp, xz):
        def tiles(side, i, t):
            at = 0 if side == 0 else 127
            if i == 0:
                return roll_to(xz[0][side], 30 + t, at)
            if i == 17:
                return roll_to(xz[1][side], t, at)
            return roll_to(zp[side], 2 * (i - 1) + t, at)
        return tiles

    def rows_of(row, xy):
        def rows(side, i):
            value = xy[0][side] if i == 0 else xy[1][side] if i == 17 else row(side, i - 1)
            return jnp.broadcast_to(value, (8, 128))
        return rows

    def both(get):
        return [get(0), get(1)]

    def grid2(get):
        return [[get(a, b) for b in range(2)] for a in range(2)]

    def difference(low, high):
        return high - low

    def plus(low, high):
        return low + high

    nx = {
        "plane": both(lambda a: ya[a, 0]), "xy": grid2(lambda a, b: exy[a, b, 0:1]),
        "zp": both(lambda a: za[a, 0]), "xz": grid2(lambda a, b: exz[a, b, 0]),
    }
    ny = {
        "plane2": both(lambda a: yb[a]), "own_row": both(lambda a: m_ref[1, :, a, 7 * a, :]),
        "zp": both(lambda a: za[a, 2]), "yz": grid2(lambda a, b: eyz[a, b, 1]),
    }
    nz = {
        "plane": both(lambda a: ya[a, 2]), "yz": grid2(lambda a, b: eyz[a, b, 0]),
        "zp2": both(lambda a: za[a, 4]), "own_z": both(lambda a: z5[1 - a, 1]),
    }
    along_x = jnp.concatenate([xa[0], m_ref[0], xa[1]], axis=0)
    along_y = jnp.concatenate([xb[0, 0:1], m_ref[1], xb[1, 0:1]], axis=0)
    along_z = jnp.concatenate([xb[0, 1:2], m_ref[2], xb[1, 1:2]], axis=0)
    rows = rows_of(lambda side, x: ya[side, 1, x : x + 1, :], grid2(lambda a, b: exy[a, b, 1:2]))
    tiles = tiles_of(both(lambda a: za[a, 1]), grid2(lambda a, b: exz[a, b, 1]))
    source = -0.5 * slab_star(difference, along_x, along_y, along_z, rows, tiles)

    def shift_diagonal(mass_part):
        return 6.0 + base_screen + point_screen * mass_part

    def inverse(diagonal, exists):
        return jnp.where(exists, 1.0 / diagonal, 0.0)

    slabs = shift_diagonal(jnp.concatenate([xb[0, 2:3], m_ref[3], xb[1, 2:3]], axis=0))
    diag_ref[...] = slabs
    inv_ref[0] = inverse(slabs[0], lower[0])
    inv_ref[1:17] = 1.0 / slabs[1:17]
    inv_ref[17] = inverse(slabs[17], upper[0])
    exists = lambda axis, side: (lower, upper)[side][axis]
    diag_y = both(lambda a: shift_diagonal(ya[a, 3]))
    inv_y = both(lambda a: inverse(diag_y[a], exists(1, a)))
    diag_z = both(lambda a: shift_diagonal(za[a, 3]))
    inv_z = both(lambda a: inverse(diag_z[a], exists(2, a)))

    def second_sweep(round_index, slabs, planes, layers, residual, keep, push):
        for side in range(2):
            plane_ref[round_index, side] = planes[side]
        own = slabs[1:17]
        around = slab_star(
            plus, slabs, own, own,
            lambda side, i: jnp.broadcast_to(plane_ref[round_index, side, i : i + 1, :], (8, 128)),
            lambda side, i, t: roll_to(layers[side], 2 * i + t, 0 if side == 0 else 127),
        )
        residual = residual - (diag_ref[1:17] * own - around)
        return residual, keep * own + push * (residual * inv_ref[1:17])

    factors = sweep_factors()
    slabs = source * inv_ref[...]
    planes = both(lambda a: -0.5 * layer_star_y(difference, a, nx, ny, nz) * inv_y[a])
    layers = both(lambda a: -0.5 * layer_star_z(difference, a, nx, ny, nz) * inv_z[a])
    u_ref[...] = slabs[1:17]
    residual, following = second_sweep(0, slabs, planes, layers, source[1:17], *factors[0])

    rounds = []
    for e in range(2):
        pw[e] = following
        rw[e] = residual
        for side in range(2):
            for i, (ref, depth) in enumerate(((pw, 0), (pw, 1), (rw, 0))):
                z3[e, side, i] = pack(lambda k, ref=ref: ref[e, k // 2, k % 2], end(side, depth, 128))
        entries = []
        for a in range(2):
            for b in range(2):
                row = pw.at[e, end(a, 0, 16), 1 - b, 7 - 7 * b : 8 - 7 * b, :]
                entries.append((mesh_step(x=a, y=b), row, pxy.at[e, a, b]))
                entries.append((mesh_step(x=a, z=b), z3.at[e, b, 0], pxz.at[e, a, b]))
                entries.append((mesh_step(y=a, z=b), z3.at[e, b, 0], pyz.at[e, a, b]))
        for a in range(2):
            first = 14 if a == 0 else 0
            entries.append((mesh_step(x=a), pw.at[e, first : first + 2], px.at[e, a]))
            entries.append((mesh_step(x=a), rw.at[e, end(a, 0, 16)], rx.at[e, a]))
            entries.append((mesh_step(y=a), pw.at[e, :, 1 - a, 7 - 7 * a, :], py.at[e, a]))
            entries.append((mesh_step(y=a), pw.at[e, :, 1 - a, 6 - 5 * a, :], py2.at[e, a]))
            entries.append((mesh_step(y=a), rw.at[e, :, 1 - a, 7 - 7 * a, :], ry.at[e, a]))
            entries.append((mesh_step(z=a), z3.at[e, a], pz.at[e, a]))
        ghosts = numbered(entries, h_send.at[e], h_recv.at[e])
        rounds.append(ghosts)
        start(ghosts)
        u_ref[...] += following
        receive(ghosts)
        p = {
            "plane": both(lambda a: py[e, a]), "plane2": both(lambda a: py2[e, a]),
            "own_row": both(lambda a: pw[e, :, a, 7 * a, :]), "xy": grid2(lambda a, b: pxy[e, a, b]),
            "zp": both(lambda a: pz[e, a, 0]), "zp2": both(lambda a: pz[e, a, 1]),
            "own_z": both(lambda a: z3[e, 1 - a, 0]),
            "xz": grid2(lambda a, b: pxz[e, a, b]), "yz": grid2(lambda a, b: pyz[e, a, b]),
        }
        wide = jnp.concatenate([px[e, 0], pw[e], px[e, 1]], axis=0)
        middle = wide[1:19]
        rows = rows_of(lambda side, x: py[e, side, x : x + 1, :], p["xy"])
        around = slab_star(plus, wide, middle, middle, rows, tiles_of(p["zp"], p["xz"]))
        residual = jnp.concatenate([rx[e, 0][None], rw[e], rx[e, 1][None]], axis=0)
        residual = residual - (diag_ref[...] * middle - around)
        keep, push = factors[2 * e + 1]
        slabs = keep * middle + push * (residual * inv_ref[...])

        def outside(own, rest, diagonal, inverse_diagonal, star):
            rest = rest - (diagonal * own - star)
            return keep * own + push * (rest * inverse_diagonal)

        planes = both(lambda a: outside(p["plane"][a], ry[e, a], diag_y[a], inv_y[a], layer_star_y(plus, a, p, p, p)))
        layers = both(lambda a: outside(p["zp"][a], pz[e, a, 2], diag_z[a], inv_z[a], layer_star_z(plus, a, p, p, p)))
        u_ref[...] += slabs[1:17]
        residual, following = second_sweep(e + 1, slabs, planes, layers, residual[1:17], *factors[2 * e + 2])
    u_ref[...] += following

    uzp[...] = pack(lambda i: u_ref[i // 2, i % 2], 0)
    sources = [u_ref.at[0], u_ref.at[:, 0, 0, :], uzp, u_ref.at[0, 0, 0:1]] + [uzp] * 3
    targets = [fx, fy, fz.at[0], fxy, fz.at[1], fz.at[2], fz.at[3]]
    layer = [message(opposite(UPPER[i]), sources[i], targets[i], f_send.at[i], f_recv.at[i]) for i in range(7)]
    start(layer[::-1])
    receive(layer)
    halo_ref[0:16] = fx[...].reshape(16, 128)
    halo_ref[16:32] = fy[...]
    halo_ref[32:40] = jnp.where(sub == 0, jnp.broadcast_to(fxy[...], (8, 128)), 0.0)
    halo_ref[40:48] = zero
    for i in range(32):
        uz_ref[8 * i : 8 * i + 8] = roll_to(fz[0], i, 0)
    for t in range(2):
        uz_ref[256 + 8 * t : 264 + 8 * t] = roll_to(fz[1], t, 0)
        picked = jnp.where(lane == 2 * (8 * t + sub), jnp.broadcast_to(fz[2, 0:1], (8, 128)), 0.0)
        column = jnp.sum(picked, axis=1, keepdims=True)
        uz_ref[272 + 8 * t : 280 + 8 * t] = jnp.broadcast_to(column, (8, 128))
    uz_ref[288:296] = jnp.where(sub == 0, fz[3], 0.0)
    uz_ref[296:304] = zero
    for messages in (mass, ghost, *rounds, layer):
        drain(messages)


FIELD = (16, 2, 8, 128)
SOLVE_SHAPES = [
    (4, *FIELD), (2, 8, 128), (16, 512), (16, 512), (1, 512), (4, 8, 128),
    (2, 5, 8, 128), (2, 2, 2, 8, 128), (2, 3, 2, 8, 128), (2, 4, 16, 128), (2, 16, 128), (2, 2, 2, 128),
    (2, 5, 8, 128), (2, 2, 2, 8, 128), (2, 2, 2, 8, 128),
    (2, *FIELD), (2, *FIELD), (2, 2, 3, 8, 128), (2, 2, 2, 2, 8, 128), (2, 2, 2, 8, 128),
    (2, 2, 16, 128), (2, 2, 16, 128), (2, 2, 16, 128), (2, 2, 2, 1, 128), (2, 2, 3, 8, 128),
    (2, 2, 2, 8, 128), (2, 2, 2, 8, 128), (18, 2, 8, 128), (18, 2, 8, 128), (3, 2, 16, 128), (8, 128),
    (2, 8, 128), (16, 128), (1, 128), (4, 8, 128),
]
LANDING = [2, 3, 4, 5, 7, 8, 9, 10, 11, 12, 13, 14, 18, 19, 20, 21, 22, 23, 24, 25, 26, 31, 32, 33, 34]


def kernel(sizes, data_hbm, cells_hbm, counts_hbm, u_ref, out_ref, *scratch):
    (data_ref, cells_ref, counts_ref, send, recv, sent, d_ref, a0, b0, a1, b1, acc_ref, ov_ref,
     l_ref, r_ref, halo_ref, uz_ref, val_ref, back_send, back_recv, back_sent,
     in_sem, send_sem, recv_sem, *rest) = scratch
    here = position(sizes)
    me = (here[0] * sizes[1] + here[1]) * sizes[2] + here[2]
    for at in LANDING:
        rest[at][...] = jnp.zeros(rest[at].shape, F32)
    loads = [
        pltpu.make_async_copy(source, target, in_sem.at[i])
        for i, (source, target) in enumerate(((data_hbm, data_ref), (cells_hbm, cells_ref), (counts_hbm, counts_ref)))
    ]
    for load in loads:
        load.start()

    def meanwhile():
        for load in loads:
            load.wait()
        prepare_rows(data_ref, cells_ref, counts_ref, send)

    greet(me, meanwhile)
    exchange_rows(me, send, recv, sent, send_sem.at[0], recv_sem.at[0])
    d_ref[...] = recv[...].T[: CAP * CHANNELS].reshape(CHANNELS, CAP, DEVICES)
    splat_points(d_ref, acc_ref, ov_ref, a0, b0, a1, b1)
    solve(sizes, here, acc_ref, ov_ref, u_ref, halo_ref, uz_ref, *rest)
    interpolate(d_ref, u_ref, halo_ref, uz_ref, val_ref, l_ref, r_ref)
    padded = jnp.concatenate([val_ref[...], jnp.zeros((DEVICES - CAP, DEVICES), F32)], axis=0)
    back_send[...] = padded.T
    exchange_rows(me, back_send, back_recv, back_sent, send_sem.at[1], recv_sem.at[1])
    slot = lax.broadcasted_iota(jnp.int32, (CAP, DEVICES), 0)
    out_ref[...] = jnp.where(slot < counts_ref[...], back_recv[...].T[:CAP], 0.0)
    pltpu.make_async_copy(send, recv, send_sem.at[0]).wait()
    pltpu.make_async_copy(back_send, back_recv, send_sem.at[1]).wait()


def on_device(sizes, point_data, point_cells, send_counts):
    data = jnp.transpose(point_data[0], (1, 2, 0))
    cells = jnp.transpose(point_cells[0], (1, 2, 0))
    dma = pltpu.SemaphoreType.DMA
    shapes = [
        ((7, CAP, DEVICES), F32), ((3, CAP, DEVICES), jnp.int32), ((1, DEVICES), jnp.int32),
        ((DEVICES, WIDTH), F32), ((DEVICES, WIDTH), F32), ((1, WIDTH), F32), ((CHANNELS, CAP, DEVICES), F32),
        ((ROWS, 3 * POINTS), BF16), ((528, 3 * POINTS), BF16), ((ROWS, 3 * POINTS), BF16), ((528, 3 * POINTS), BF16),
        ((ROWS, 512), F32), ((ROWS, 128), F32), ((ROWS, 512), BF16), ((512, POINTS), BF16),
        ((48, 128), F32), ((ROWS, 128), F32), ((CAP, DEVICES), F32),
        ((DEVICES, DEVICES), F32), ((DEVICES, DEVICES), F32), ((1, DEVICES), F32),
    ]
    u, returned = pl.pallas_call(
        functools.partial(kernel, sizes),
        out_shape=[jax.ShapeDtypeStruct(s, F32) for s in (FIELD, (CAP, DEVICES))],
        in_specs=[pl.BlockSpec(memory_space=pltpu.HBM)] * 3,
        out_specs=[vmem()] * 2,
        scratch_shapes=[pltpu.VMEM(*s) for s in shapes]
        + [dma((3,)), dma((2,)), dma((2,))]
        + [pltpu.VMEM(s, F32) for s in SOLVE_SHAPES]
        + [dma((7,)), dma((7,)), dma((22,)), dma((22,)), dma((2, 24)), dma((2, 24)), dma((7,)), dma((7,))],
        compiler_params=pltpu.CompilerParams(
            vmem_limit_bytes=24 * 1024 * 1024, collective_id=0, has_side_effects=True
        ),
        name="reconstruct",
    )(*[pltpu.with_memory_space_constraint(v, pltpu.HBM) for v in (data, cells, send_counts)])
    return u.reshape(16, 16, 128), returned.T[None]


def solution(mesh):
    sizes = tuple(mesh.shape[name] for name in ("gx", "gy", "gz"))
    spread_over = ("gx", "gy", "gz")
    in_specs = (P(spread_over, None, None, None), P(spread_over, None, None, None), P(spread_over, None))
    out_specs = (P("gx", "gy", "gz"), P(spread_over, None, None))
    return jax.shard_map(
        functools.partial(on_device, sizes), mesh=mesh, in_specs=in_specs, out_specs=out_specs, check_vma=False
    )
```

```python
import functools

import jax
import jax.numpy as jnp
from jax import lax
from jax.experimental import pallas as pl
from jax.experimental.pallas import tpu as pltpu
from jax.sharding import PartitionSpec as P

MESH = pl.DeviceIdType.MESH
F32 = jnp.float32
BF16 = jnp.bfloat16

DEVICES = 128
CAP = 32
CHANNELS = 10
WIDTH = 384
POINTS = 512
ROWS = 304
ITERS = 6
GROUPS = CAP * DEVICES // POINTS

base_screen = 0.25
point_screen = 4.0


def sweep_factors():
    half_width = 6.0 / (6.0 + base_screen)
    rho_prev = half_width
    factors = []
    for _ in range(ITERS - 1):
        rho_next = 1.0 / (2.0 / half_width - rho_prev)
        factors.append((rho_next * rho_prev, 2.0 * rho_next / half_width))
        rho_prev = rho_next
    return factors


def position(sizes):
    return tuple(lax.axis_index(name) for name in ("gx", "gy", "gz"))


def vmem():
    return pl.BlockSpec(memory_space=pltpu.VMEM)


def greet(me, meanwhile):
    barrier = pltpu.get_barrier_semaphore()

    @pl.loop(0, DEVICES - 8, step=8)
    def _(step):
        for q in range(8):
            pl.semaphore_signal(barrier, inc=1, device_id=me ^ (step + q + 1), device_id_type=pl.DeviceIdType.LOGICAL)

    for q in range(DEVICES - 7, DEVICES):
        pl.semaphore_signal(barrier, inc=1, device_id=me ^ q, device_id_type=pl.DeviceIdType.LOGICAL)
    meanwhile()
    pl.semaphore_wait(barrier, DEVICES - 1)


def exchange_rows(me, send, recv, sent, send_sem, recv_sem):
    def post(step):
        other = me ^ ((step * 37) & (DEVICES - 1))
        pltpu.make_async_remote_copy(
            src_ref=send.at[pl.ds(other, 1)],
            dst_ref=recv.at[pl.ds(me, 1)],
            send_sem=send_sem,
            recv_sem=recv_sem,
            device_id=other,
            device_id_type=pl.DeviceIdType.LOGICAL,
        ).start()

    @pl.loop(0, DEVICES - 8, step=8)
    def _(step):
        for q in range(8):
            post(step + q + 1)

    for q in range(DEVICES - 7, DEVICES):
        post(q)
    pltpu.make_async_copy(send.at[pl.ds(me, 1)], recv.at[pl.ds(me, 1)], recv_sem).start()
    pltpu.make_async_copy(send.at[pl.ds(me, 1)], sent, send_sem).start()
    pltpu.make_async_copy(send, recv, recv_sem).wait()


def prepare_rows(data_ref, cells_ref, counts_ref, send):
    slot = lax.broadcasted_iota(jnp.int32, (CAP, DEVICES), 0)
    weight = jnp.where(slot < counts_ref[...], data_ref[3], 0.0)
    parts = [data_ref[c] * weight for c in range(3)] + [weight]
    parts += [data_ref[4 + c] for c in range(3)] + [cells_ref[c].astype(F32) for c in range(3)]
    parts += [jnp.zeros((WIDTH - CAP * CHANNELS, DEVICES), F32)]
    send[...] = jnp.concatenate(parts, axis=0).T


def split(value):
    high = value.astype(BF16)
    return high, (value - high.astype(F32)).astype(BF16)


WIDE = 256


def lane_rows(d_ref, group, block, channels):
    first = (group * POINTS + block * WIDE) // DEVICES
    wide = lambda c, q: jnp.broadcast_to(d_ref[c, pl.ds(first + q, 1), :], (16, DEVICES))
    return [jnp.concatenate([wide(c, q) for q in range(WIDE // DEVICES)], axis=1) for c in channels]


def tile_iota():
    return lax.broadcasted_iota(jnp.int32, (16, WIDE), 0).astype(F32).astype(BF16)


def build_block(d_ref, group, block, a_ref, b_ref):
    iota = tile_iota()
    zero = jnp.zeros((16, WIDE), BF16)
    lanes = slice(block * WIDE, (block + 1) * WIDE)
    v = lane_rows(d_ref, group, block, range(4))
    fx, fy, fz, cx, cy, cz = lane_rows(d_ref, group, block, range(4, 10))
    bz = cz.astype(BF16)
    bz1 = (cz + 1.0).astype(BF16)
    g0 = [split(v[c] * (1.0 - fz)) for c in range(4)]
    g1 = [split(v[c] * fz) for c in range(4)]
    for t in range(8):
        at = iota + jnp.asarray(16 * t, BF16)
        z0, z1 = bz == at, bz1 == at
        for c in range(4):
            for part in range(2):
                value = jnp.where(z0, g0[c][part], jnp.where(z1, g1[c][part], zero))
                b_ref[512 * part + 128 * c + 16 * t : 512 * part + 128 * c + 16 * t + 16, lanes] = value
    top = bz == 127
    both = zero
    for c in range(4):
        for part in range(2):
            both = jnp.where(iota == c + 4 * part, g1[c][part], both)
    b_ref[1024:1040, lanes] = jnp.where(top, both, zero)
    by, by1 = cy.astype(BF16), (cy + 1.0).astype(BF16)
    y0, y1 = by == iota, by1 == iota
    near, far = [], []
    for along, out in ((1.0 - fx, near), (fx, far)):
        w0, w1 = split(along * (1.0 - fy)), split(along * fy)
        for part in range(2):
            out.append(jnp.where(y0, w0[part], jnp.where(y1, w1[part], zero)))
    bx = cx.astype(BF16)
    below = None
    for x in range(17):
        here = bx == x
        for part in range(2):
            value = near[part] if below is None else jnp.where(below, far[part], zero)
            value = jnp.where(here, near[part], zero if below is None else value)
            first = (256 * part + 16 * x) if x < 16 else 512 + 48 * part
            a_ref[first : first + 16, lanes] = value
        below = here
    bx1 = (cx + 1.0).astype(BF16)
    edge = jnp.where(cy == 15.0, fy, 0.0)
    e0, e1 = split((1.0 - fx) * edge), split(fx * edge)
    for t in range(2):
        at = iota + jnp.asarray(16 * t, BF16)
        x0, x1 = bx == at, bx1 == at
        for part in range(2):
            first = 528 + 48 * part + 16 * t
            a_ref[first : first + 16, lanes] = jnp.where(x0, e0[part], jnp.where(x1, e1[part], zero))


ROW_DIMS = (((1,), (1,)), ((), ()))


def rows_by_rows(left, right):
    return lax.dot_general(left, right, ROW_DIMS, preferred_element_type=F32)


def multiply_outside(piece, a_ref, b_ref, acc_ref, ov_ref):
    if piece == 0:
        acc_ref[512:608, 0:256] += rows_by_rows(a_ref[512:608, :], b_ref[0:256, :])
    elif piece == 1:
        acc_ref[512:608, 256:512] += rows_by_rows(a_ref[512:608, :], b_ref[256:512, :])
    elif piece == 2:
        acc_ref[512:560, :] += rows_by_rows(a_ref[512:560, :], b_ref[512:1024, :])
    else:
        ov_ref[:, 0:16] += rows_by_rows(a_ref[...], b_ref[1024:1040, :])


def splat_outside(d_ref, acc_ref, ov_ref, a_refs, b_refs):
    acc_ref[...] = jnp.zeros_like(acc_ref)
    ov_ref[...] = jnp.zeros_like(ov_ref)
    for block in range(POINTS // WIDE):
        build_block(d_ref, 0, block, a_refs[0], b_refs[0])
    for group in range(GROUPS):
        for block in range(4):
            if group + 1 < GROUPS and block < POINTS // WIDE:
                build_block(d_ref, group + 1, block, a_refs[group + 1], b_refs[group + 1])
            multiply_outside(block, a_refs[group], b_refs[group], acc_ref, ov_ref)


def splat_inside(acc_ref, a_refs, b_refs):
    for a_ref, b_ref in zip(a_refs, b_refs):
        acc_ref[0:512, :] += rows_by_rows(a_ref[0:512, :], b_ref[0:512, :])
        acc_ref[0:256, :] += rows_by_rows(a_ref[0:256, :], b_ref[512:1024, :])


def interpolation_tables(d_ref, r_ref, w_ref):
    iota = tile_iota()
    iota_f = iota.astype(F32)
    zero = jnp.zeros((16, WIDE), BF16)

    @pl.loop(0, GROUPS)
    def _(group):
        r_ref[group, 400:512, :] = jnp.zeros((112, POINTS), BF16)
        for block in range(POINTS // WIDE):
            lanes = slice(block * WIDE, (block + 1) * WIDE)
            fx, fy, fz, cx, cy, cz = lane_rows(d_ref, group, block, range(4, 10))
            bz, bz1 = cz.astype(BF16), (cz + 1.0).astype(BF16)
            g0, g1 = split(1.0 - fz), split(fz)
            for t in range(8):
                at = iota + jnp.asarray(16 * t, BF16)
                z0, z1 = bz == at, bz1 == at
                high, low = [jnp.where(z0, g0[part], jnp.where(z1, g1[part], zero)) for part in range(2)]
                r_ref[group, 16 * t : 16 * t + 16, lanes] = high
                r_ref[group, 128 + 16 * t : 144 + 16 * t, lanes] = high
                r_ref[group, 256 + 16 * t : 272 + 16 * t, lanes] = low
            picked = jnp.where(iota <= 1, g1[0], jnp.where(iota == 2, g1[1], zero))
            r_ref[group, 384:400, lanes] = jnp.where(bz == 127, picked, zero)
            hat_y = jnp.where(cy == iota_f, 1.0 - fy, jnp.where(cy + 1.0 == iota_f, fy, 0.0))
            near, far = (1.0 - fx) * hat_y, fx * hat_y
            for x in range(17):
                w_ref[group, 16 * x : 16 * x + 16, lanes] = jnp.where(cx == x, near, jnp.where(cx == x - 1, far, 0.0))
            edge = jnp.where(cy == 15.0, fy, 0.0)
            for t in range(2):
                at = iota_f + 16.0 * t
                hat = jnp.where(cx == at, 1.0 - fx, jnp.where(cx + 1.0 == at, fx, 0.0))
                w_ref[group, 272 + 16 * t : 288 + 16 * t, lanes] = hat * edge


def weighted(g, w_ref, group, first):
    rows = g.shape[0]
    total = g[0:8] * w_ref[group, first : first + 8]
    for i in range(1, rows // 8):
        total = total + g[8 * i : 8 * i + 8] * w_ref[group, first + 8 * i : first + 8 * i + 8]
    return total


def high_and_low(l_ref, first, value):
    rows = pl.ds(first, value.shape[0])
    high, low = split(value)
    l_ref[rows, 0:128] = high
    l_ref[rows, 128:256] = low
    l_ref[rows, 256:384] = high


def interpolate_inside(u_ref, part_ref, l_ref, r_ref, w_ref):
    high_and_low(l_ref, 0, u_ref[...].reshape(256, 128))

    @pl.loop(0, GROUPS, step=4)
    def _(first):
        for step in range(4):
            group = first + step
            g = jnp.dot(l_ref[0:256, 0:384], r_ref[group, 0:384], preferred_element_type=F32)
            part_ref[group] = weighted(g, w_ref, group, 0)


def interpolate(halo_ref, uz_ref, part_ref, out_ref, l_ref, r_ref, w_ref):
    high_and_low(l_ref, 256, halo_ref[...])
    top = jnp.broadcast_to(uz_ref[:, 0:1], (ROWS, 128))
    high = top.astype(BF16).astype(F32)
    lane = lax.broadcasted_iota(jnp.int32, (ROWS, 128), 1)
    low = jnp.where(lane == 1, top - high, 0.0)
    l_ref[:, 384:512] = jnp.where(jnp.logical_or(lane == 0, lane == 2), high, low).astype(BF16)

    @pl.loop(0, GROUPS, step=4)
    def _(first):
        for step in range(4):
            group = first + step
            g = jnp.dot(l_ref[256:ROWS, :], r_ref[group], preferred_element_type=F32)
            total = part_ref[group] + weighted(g, w_ref, group, 256)
            g = jnp.dot(l_ref[0:256, 384:512], r_ref[group, 384:512], preferred_element_type=F32)
            value = jnp.sum(total + weighted(g, w_ref, group, 0), axis=0, keepdims=True)
            count = POINTS // DEVICES
            for q in range(count):
                out_ref[pl.ds(group * count + q, 1), :] = value[:, q * DEVICES : (q + 1) * DEVICES]


FACES = [(1, 0, 0), (0, 1, 0), (0, 0, 1)]
UPPER = FACES + [(1, 1, 0), (1, 0, 1), (0, 1, 1), (1, 1, 1)]


def roll_to(tile, source, target):
    shift = (target - source) % 128
    return pltpu.roll(tile, shift, 1) if shift else tile


def grid_iotas():
    lane = lax.broadcasted_iota(jnp.int32, (8, 128), 1)
    sub = lax.broadcasted_iota(jnp.int32, (8, 128), 0)
    return lane, sub


def pack(read, source):
    lane, _ = grid_iotas()
    packed = jnp.zeros((8, 128), F32)
    for i in range(32):
        packed = jnp.where(lane == i, roll_to(read(i), source, i), packed)
    return packed


def slab_star(comb, along_x, along_y, along_z, rows, tiles):
    n = along_y.shape[0]
    total = comb(along_x[0:n], along_x[2 : n + 2])
    sub3 = lax.broadcasted_iota(jnp.int32, (n, 8, 128), 1)
    down = pltpu.roll(along_y.reshape(2 * n, 8, 128), 1, 1).reshape(n, 2, 8, 128)
    up = pltpu.roll(along_y.reshape(2 * n, 8, 128), 7, 1).reshape(n, 2, 8, 128)
    edge = [jnp.stack([rows(side, i) for i in range(n)]) for side in range(2)]
    first, last = sub3 == 0, sub3 == 7
    low = jnp.stack([jnp.where(first, edge[0], down[:, 0]), jnp.where(first, down[:, 0], down[:, 1])], axis=1)
    high = jnp.stack([jnp.where(last, up[:, 1], up[:, 0]), jnp.where(last, edge[1], up[:, 1])], axis=1)
    total = total + comb(low, high)
    lanes = lax.broadcasted_iota(jnp.int32, (2 * n, 8, 128), 2)
    flat = along_z.reshape(16 * n, 128)
    sides = []
    for side, shift, at in ((0, 1, 0), (1, 127, 127)):
        edge = jnp.stack([tiles(side, i, t) for i in range(n) for t in range(2)])
        sides.append(jnp.where(lanes == at, edge, pltpu.roll(flat, shift, 1).reshape(2 * n, 8, 128)))
    return total + comb(*sides).reshape(n, 2, 8, 128)


def layer_star_y(comb, side, fx, fy, fz):
    row = lax.broadcasted_iota(jnp.int32, (16, 128), 0)
    lane16 = lax.broadcasted_iota(jnp.int32, (16, 128), 1)
    plane = fx["plane"][side]
    low = jnp.where(row == 0, jnp.broadcast_to(fx["xy"][0][side], (16, 128)), pltpu.roll(plane, 1, 0))
    high = jnp.where(row == 15, jnp.broadcast_to(fx["xy"][1][side], (16, 128)), pltpu.roll(plane, 15, 0))
    total = comb(low, high)
    outer, own = fy["plane2"][side], fy["own_row"][side]
    total = total + (comb(outer, own) if side == 0 else comb(own, outer))
    plane = fz["plane"][side]
    parity, source = (1, 7) if side == 0 else (0, 0)
    sides = []
    for z_side, shift, at in ((0, 1, 0), (1, 127, 127)):
        values = jnp.broadcast_to(fz["yz"][side][z_side][source : source + 1], (16, 128))
        column = jnp.sum(jnp.where(lane16 == 2 * row + parity, values, 0.0), axis=1, keepdims=True)
        sides.append(jnp.where(lane16 == at, jnp.broadcast_to(column, (16, 128)), pltpu.roll(plane, shift, 1)))
    return total + comb(*sides)


def layer_star_z(comb, side, fx, fy, fz):
    lane, sub = grid_iotas()
    layer = fx["zp"][side]
    low = jnp.where(lane < 2, roll_to(fx["xz"][0][side], 30, 0), pltpu.roll(layer, 2, 1))
    high = jnp.where(lane >= 30, roll_to(fx["xz"][1][side], 0, 30), pltpu.roll(layer, 126, 1))
    total = comb(low, high)
    layer = fy["zp"][side]
    down, up = pltpu.roll(layer, 1, 0), pltpu.roll(layer, 7, 0)
    odd = lax.rem(lane, 2) == 1
    beyond = pltpu.roll(pltpu.roll(fy["yz"][0][side], 1, 0), 127, 1)
    low = jnp.where(sub == 0, jnp.where(odd, pltpu.roll(down, 1, 1), beyond), down)
    beyond = pltpu.roll(pltpu.roll(fy["yz"][1][side], 7, 0), 1, 1)
    high = jnp.where(sub == 7, jnp.where(odd, beyond, pltpu.roll(up, 127, 1)), up)
    total = total + comb(low, high)
    outer, own = fz["zp2"][side], fz["own_z"][side]
    total = total + (comb(outer, own) if side == 0 else comb(own, outer))
    return jnp.where(lane < 32, total, 0.0)


def solve(
    sizes, here, own_rows, tables, own_values, s_ref, ov_ref, out_ref, u_ref, halo_ref, uz_ref,
    m_ref, zs_ref, sx, sy, sxy, sz,
    z5, xa, xb, ya, yb, exy, za, exz, eyz,
    pw, rw, z3, px, rx, py, py2, ry, pxy, pz, pxz, pyz, inv_ref, diag_ref, plane_ref, uzp,
    fx, fy, fxy, fz, s_send, s_recv, g_send, g_recv, h_send, h_recv, f_send, f_recv,
):
    lower = [here[a] > 0 for a in range(3)]
    upper = [here[a] < sizes[a] - 1 for a in range(3)]

    def present(step):
        wanted = [(upper if step[a] > 0 else lower)[a] for a in range(3) if step[a]]
        return functools.reduce(jnp.logical_and, wanted)

    def opposite(step):
        return tuple(-v for v in step)

    def message(step, source, target, send, recv):
        copy = pltpu.make_async_remote_copy(
            src_ref=source, dst_ref=target, send_sem=send, recv_sem=recv,
            device_id=tuple(here[a] + step[a] for a in range(3)), device_id_type=MESH,
        )
        return step, copy

    def start(messages):
        for step, copy in messages:
            @pl.when(present(step))
            def _(copy=copy):
                copy.start()

    def receive(messages):
        for step, copy in messages:
            @pl.when(present(opposite(step)))
            def _(copy=copy):
                copy.wait_recv()

    def drain(messages):
        for step, copy in messages:
            @pl.when(present(step))
            def _(copy=copy):
                copy.wait_send()

    lane, sub = grid_iotas()
    zero = jnp.zeros((8, 128), F32)

    for part, tiles in ((0, 32), (1, 5)):
        packed = zero
        for i in range(tiles):
            first = 512 * part + 8 * i
            tile = ov_ref[pl.ds(first, 8), :] + ov_ref[pl.ds(first + (48 if part else 256), 8), :]
            tile = tile + pltpu.roll(tile, 124, 1)
            here_lanes = jnp.logical_and(lane >= 4 * i, lane < 4 * i + 4)
            packed = jnp.where(here_lanes, roll_to(tile, 0, 4 * i), packed)
        zs_ref[part] = packed
    out_ref[...] = s_ref[512:560, :] + s_ref[560:608, :]
    sources = [out_ref.at[0:16], out_ref.at[16:32], zs_ref.at[0], out_ref.at[32:33]] + [zs_ref.at[1]] * 3
    targets = [sx, sy, sz.at[0], sxy, sz.at[1], sz.at[2], sz.at[3]]
    mass = [message(UPPER[i], sources[i], targets[i], s_send.at[i], s_recv.at[i]) for i in range(7)]
    start(mass[::-1])
    own_rows()
    for c in range(4):
        columns = slice(128 * c, 128 * c + 128)
        m_ref[c] = (s_ref[0:256, columns] + s_ref[256:512, columns]).reshape(16, 2, 8, 128)
    receive(mass)
    for c in range(4):
        columns = slice(128 * c, 128 * c + 128)
        m_ref[c, 0] += sx[:, columns].reshape(2, 8, 128)
        from_y = sy[:, columns]
        near_z = [roll_to(sz[2], 8 + 4 * t + c, 0) for t in range(2)]
        for x in range(16):
            row = from_y[x : x + 1, :] + jnp.where(lane[0:1] == 0, near_z[x // 8][x % 8 : x % 8 + 1, :], 0.0)
            m_ref[c, x, 0, 0:1, :] += row
        for i in range(32):
            m_ref[c, i // 2, i % 2] += jnp.where(lane == 0, roll_to(sz[0], 4 * i + c, 0), 0.0)
        for t in range(2):
            m_ref[c, 0, t] += jnp.where(lane == 0, roll_to(sz[1], 4 * t + c, 0), 0.0)
        corner = sxy[:, columns] + jnp.where(lane[0:1] == 0, roll_to(sz[3], 16 + c, 0)[0:1], 0.0)
        m_ref[c, 0, 0, 0:1, :] += corner

    def end(side, depth, size):
        return size - 1 - depth if side == 0 else depth

    def toward(side):
        return 1 if side == 0 else -1

    def mesh_step(**sides):
        return tuple(toward(sides[name]) if name in sides else 0 for name in "xyz")

    def numbered(entries, send, recv):
        return [message(step, a, b, send.at[i], recv.at[i]) for i, (step, a, b) in enumerate(entries)]

    for side in range(2):
        for i, (c, depth) in enumerate(((0, 0), (2, 0), (1, 0), (3, 0), (2, 1))):
            z5[side, i] = pack(lambda k, c=c: m_ref[c, k // 2, k % 2], end(side, depth, 128))
    entries = []
    for a in range(2):
        for b in range(2):
            entries.append((mesh_step(x=a, y=b), m_ref.at[0:2, end(a, 0, 16), 1 - b, 7 - 7 * b, :], exy.at[a, b]))
            entries.append((mesh_step(x=a, z=b), z5.at[b, 0:2], exz.at[a, b]))
            entries.append((mesh_step(y=a, z=b), z5.at[b, 1:3], eyz.at[a, b]))
    for a in range(2):
        first = 14 if a == 0 else 0
        entries.append((mesh_step(x=a), m_ref.at[0, first : first + 2], xa.at[a]))
        entries.append((mesh_step(x=a), m_ref.at[1:4, end(a, 0, 16)], xb.at[a]))
        entries.append((mesh_step(y=a), m_ref.at[:, :, 1 - a, 7 - 7 * a, :], ya.at[a]))
        entries.append((mesh_step(y=a), m_ref.at[1, :, 1 - a, 6 - 5 * a, :], yb.at[a]))
        entries.append((mesh_step(z=a), z5.at[a], za.at[a]))
    ghost = numbered(entries, g_send, g_recv)
    start(ghost)
    tables()
    receive(ghost)

    def tiles_of(zp, xz):
        def tiles(side, i, t):
            at = 0 if side == 0 else 127
            if i == 0:
                return roll_to(xz[0][side], 30 + t, at)
            if i == 17:
                return roll_to(xz[1][side], t, at)
            return roll_to(zp[side], 2 * (i - 1) + t, at)
        return tiles

    def rows_of(row, xy):
        def rows(side, i):
            value = xy[0][side] if i == 0 else xy[1][side] if i == 17 else row(side, i - 1)
            return jnp.broadcast_to(value, (8, 128))
        return rows

    def both(get):
        return [get(0), get(1)]

    def grid2(get):
        return [[get(a, b) for b in range(2)] for a in range(2)]

    def difference(low, high):
        return high - low

    def plus(low, high):
        return low + high

    nx = {
        "plane": both(lambda a: ya[a, 0]), "xy": grid2(lambda a, b: exy[a, b, 0:1]),
        "zp": both(lambda a: za[a, 0]), "xz": grid2(lambda a, b: exz[a, b, 0]),
    }
    ny = {
        "plane2": both(lambda a: yb[a]), "own_row": both(lambda a: m_ref[1, :, a, 7 * a, :]),
        "zp": both(lambda a: za[a, 2]), "yz": grid2(lambda a, b: eyz[a, b, 1]),
    }
    nz = {
        "plane": both(lambda a: ya[a, 2]), "yz": grid2(lambda a, b: eyz[a, b, 0]),
        "zp2": both(lambda a: za[a, 4]), "own_z": both(lambda a: z5[1 - a, 1]),
    }
    along_x = jnp.concatenate([xa[0], m_ref[0], xa[1]], axis=0)
    along_y = jnp.concatenate([xb[0, 0:1], m_ref[1], xb[1, 0:1]], axis=0)
    along_z = jnp.concatenate([xb[0, 1:2], m_ref[2], xb[1, 1:2]], axis=0)
    rows = rows_of(lambda side, x: ya[side, 1, x : x + 1, :], grid2(lambda a, b: exy[a, b, 1:2]))
    tiles = tiles_of(both(lambda a: za[a, 1]), grid2(lambda a, b: exz[a, b, 1]))
    source = -0.5 * slab_star(difference, along_x, along_y, along_z, rows, tiles)

    def shift_diagonal(mass_part):
        return 6.0 + base_screen + point_screen * mass_part

    def inverse(diagonal, exists):
        return jnp.where(exists, 1.0 / diagonal, 0.0)

    slabs = shift_diagonal(jnp.concatenate([xb[0, 2:3], m_ref[3], xb[1, 2:3]], axis=0))
    diag_ref[...] = slabs
    inv_ref[0] = inverse(slabs[0], lower[0])
    inv_ref[1:17] = 1.0 / slabs[1:17]
    inv_ref[17] = inverse(slabs[17], upper[0])
    exists = lambda axis, side: (lower, upper)[side][axis]
    diag_y = both(lambda a: shift_diagonal(ya[a, 3]))
    inv_y = both(lambda a: inverse(diag_y[a], exists(1, a)))
    diag_z = both(lambda a: shift_diagonal(za[a, 3]))
    inv_z = both(lambda a: inverse(diag_z[a], exists(2, a)))

    def second_sweep(round_index, slabs, planes, layers, residual, keep, push):
        for side in range(2):
            plane_ref[round_index, side] = planes[side]
        own = slabs[1:17]
        around = slab_star(
            plus, slabs, own, own,
            lambda side, i: jnp.broadcast_to(plane_ref[round_index, side, i : i + 1, :], (8, 128)),
            lambda side, i, t: roll_to(layers[side], 2 * i + t, 0 if side == 0 else 127),
        )
        residual = residual - (diag_ref[1:17] * own - around)
        return residual, keep * own + push * (residual * inv_ref[1:17])

    factors = sweep_factors()
    slabs = source * inv_ref[...]
    planes = both(lambda a: -0.5 * layer_star_y(difference, a, nx, ny, nz) * inv_y[a])
    layers = both(lambda a: -0.5 * layer_star_z(difference, a, nx, ny, nz) * inv_z[a])
    u_ref[...] = slabs[1:17]
    residual, following = second_sweep(0, slabs, planes, layers, source[1:17], *factors[0])

    rounds = []
    for e in range(2):
        pw[e] = following
        rw[e] = residual
        for side in range(2):
            for i, (ref, depth) in enumerate(((pw, 0), (pw, 1), (rw, 0))):
                z3[e, side, i] = pack(lambda k, ref=ref: ref[e, k // 2, k % 2], end(side, depth, 128))
        entries = []
        for a in range(2):
            for b in range(2):
                row = pw.at[e, end(a, 0, 16), 1 - b, 7 - 7 * b : 8 - 7 * b, :]
                entries.append((mesh_step(x=a, y=b), row, pxy.at[e, a, b]))
                entries.append((mesh_step(x=a, z=b), z3.at[e, b, 0], pxz.at[e, a, b]))
                entries.append((mesh_step(y=a, z=b), z3.at[e, b, 0], pyz.at[e, a, b]))
        for a in range(2):
            first = 14 if a == 0 else 0
            entries.append((mesh_step(x=a), pw.at[e, first : first + 2], px.at[e, a]))
            entries.append((mesh_step(x=a), rw.at[e, end(a, 0, 16)], rx.at[e, a]))
            entries.append((mesh_step(y=a), pw.at[e, :, 1 - a, 7 - 7 * a, :], py.at[e, a]))
            entries.append((mesh_step(y=a), pw.at[e, :, 1 - a, 6 - 5 * a, :], py2.at[e, a]))
            entries.append((mesh_step(y=a), rw.at[e, :, 1 - a, 7 - 7 * a, :], ry.at[e, a]))
            entries.append((mesh_step(z=a), z3.at[e, a], pz.at[e, a]))
        ghosts = numbered(entries, h_send.at[e], h_recv.at[e])
        rounds.append(ghosts)
        start(ghosts)
        u_ref[...] += following
        receive(ghosts)
        p = {
            "plane": both(lambda a: py[e, a]), "plane2": both(lambda a: py2[e, a]),
            "own_row": both(lambda a: pw[e, :, a, 7 * a, :]), "xy": grid2(lambda a, b: pxy[e, a, b]),
            "zp": both(lambda a: pz[e, a, 0]), "zp2": both(lambda a: pz[e, a, 1]),
            "own_z": both(lambda a: z3[e, 1 - a, 0]),
            "xz": grid2(lambda a, b: pxz[e, a, b]), "yz": grid2(lambda a, b: pyz[e, a, b]),
        }
        wide = jnp.concatenate([px[e, 0], pw[e], px[e, 1]], axis=0)
        middle = wide[1:19]
        rows = rows_of(lambda side, x: py[e, side, x : x + 1, :], p["xy"])
        around = slab_star(plus, wide, middle, middle, rows, tiles_of(p["zp"], p["xz"]))
        residual = jnp.concatenate([rx[e, 0][None], rw[e], rx[e, 1][None]], axis=0)
        residual = residual - (diag_ref[...] * middle - around)
        keep, push = factors[2 * e + 1]
        slabs = keep * middle + push * (residual * inv_ref[...])

        def outside(own, rest, diagonal, inverse_diagonal, star):
            rest = rest - (diagonal * own - star)
            return keep * own + push * (rest * inverse_diagonal)

        planes = both(lambda a: outside(p["plane"][a], ry[e, a], diag_y[a], inv_y[a], layer_star_y(plus, a, p, p, p)))
        layers = both(lambda a: outside(p["zp"][a], pz[e, a, 2], diag_z[a], inv_z[a], layer_star_z(plus, a, p, p, p)))
        u_ref[...] += slabs[1:17]
        residual, following = second_sweep(e + 1, slabs, planes, layers, residual[1:17], *factors[2 * e + 2])
    u_ref[...] += following

    uzp[...] = pack(lambda i: u_ref[i // 2, i % 2], 0)
    sources = [u_ref.at[0], u_ref.at[:, 0, 0, :], uzp, u_ref.at[0, 0, 0:1]] + [uzp] * 3
    targets = [fx, fy, fz.at[0], fxy, fz.at[1], fz.at[2], fz.at[3]]
    layer = [message(opposite(UPPER[i]), sources[i], targets[i], f_send.at[i], f_recv.at[i]) for i in range(7)]
    start(layer[::-1])
    own_values()
    receive(layer)
    halo_ref[0:16] = fx[...].reshape(16, 128)
    halo_ref[16:32] = fy[...]
    halo_ref[32:40] = jnp.where(sub == 0, jnp.broadcast_to(fxy[...], (8, 128)), 0.0)
    halo_ref[40:48] = zero
    for i in range(32):
        uz_ref[8 * i : 8 * i + 8] = roll_to(fz[0], i, 0)
    for t in range(2):
        uz_ref[256 + 8 * t : 264 + 8 * t] = roll_to(fz[1], t, 0)
        picked = jnp.where(lane == 2 * (8 * t + sub), jnp.broadcast_to(fz[2, 0:1], (8, 128)), 0.0)
        column = jnp.sum(picked, axis=1, keepdims=True)
        uz_ref[272 + 8 * t : 280 + 8 * t] = jnp.broadcast_to(column, (8, 128))
    uz_ref[288:296] = jnp.where(sub == 0, fz[3], 0.0)
    uz_ref[296:304] = zero

    def finish():
        for messages in (mass, ghost, *rounds, layer):
            drain(messages)

    return finish


FIELD = (16, 2, 8, 128)
SOLVE_SHAPES = [
    (4, *FIELD), (2, 8, 128), (16, 512), (16, 512), (1, 512), (4, 8, 128),
    (2, 5, 8, 128), (2, 2, 2, 8, 128), (2, 3, 2, 8, 128), (2, 4, 16, 128), (2, 16, 128), (2, 2, 2, 128),
    (2, 5, 8, 128), (2, 2, 2, 8, 128), (2, 2, 2, 8, 128),
    (2, *FIELD), (2, *FIELD), (2, 2, 3, 8, 128), (2, 2, 2, 2, 8, 128), (2, 2, 2, 8, 128),
    (2, 2, 16, 128), (2, 2, 16, 128), (2, 2, 16, 128), (2, 2, 2, 1, 128), (2, 2, 3, 8, 128),
    (2, 2, 2, 8, 128), (2, 2, 2, 8, 128), (18, 2, 8, 128), (18, 2, 8, 128), (3, 2, 16, 128), (8, 128),
    (2, 8, 128), (16, 128), (1, 128), (4, 8, 128),
]
LANDING = [2, 3, 4, 5, 7, 8, 9, 10, 11, 12, 13, 14, 18, 19, 20, 21, 22, 23, 24, 25, 26, 31, 32, 33, 34]


def kernel(sizes, data_hbm, cells_hbm, counts_hbm, u_ref, out_ref, *scratch):
    a_refs, b_refs, scratch = scratch[:GROUPS], scratch[GROUPS : 2 * GROUPS], scratch[2 * GROUPS :]
    (data_ref, cells_ref, counts_ref, send, recv, sent, d_ref, acc_ref, ov_ref, face_ref,
     l_ref, r_ref, w_ref, part_ref, halo_ref, uz_ref, val_ref, back_send, back_recv, back_sent,
     in_sem, send_sem, recv_sem, *rest) = scratch
    here = position(sizes)
    me = (here[0] * sizes[1] + here[1]) * sizes[2] + here[2]
    for at in LANDING:
        rest[at][...] = jnp.zeros(rest[at].shape, F32)
    loads = [
        pltpu.make_async_copy(source, target, in_sem.at[i])
        for i, (source, target) in enumerate(((data_hbm, data_ref), (cells_hbm, cells_ref), (counts_hbm, counts_ref)))
    ]
    for load in loads:
        load.start()

    def meanwhile():
        for load in loads:
            load.wait()
        prepare_rows(data_ref, cells_ref, counts_ref, send)

    greet(me, meanwhile)
    exchange_rows(me, send, recv, sent, send_sem.at[0], recv_sem.at[0])
    d_ref[...] = recv[...].T[: CAP * CHANNELS].reshape(CHANNELS, CAP, DEVICES)
    splat_outside(d_ref, acc_ref, ov_ref, a_refs, b_refs)
    finish = solve(
        sizes, here, lambda: splat_inside(acc_ref, a_refs, b_refs), lambda: interpolation_tables(d_ref, r_ref, w_ref),
        lambda: interpolate_inside(u_ref, part_ref, l_ref, r_ref, w_ref),
        acc_ref, ov_ref, face_ref, u_ref, halo_ref, uz_ref, *rest,
    )
    interpolate(halo_ref, uz_ref, part_ref, val_ref, l_ref, r_ref, w_ref)
    padded = jnp.concatenate([val_ref[...], jnp.zeros((DEVICES - CAP, DEVICES), F32)], axis=0)
    back_send[...] = padded.T
    exchange_rows(me, back_send, back_recv, back_sent, send_sem.at[1], recv_sem.at[1])
    slot = lax.broadcasted_iota(jnp.int32, (CAP, DEVICES), 0)
    out_ref[...] = jnp.where(slot < counts_ref[...], back_recv[...].T[:CAP], 0.0)
    finish()
    pltpu.make_async_copy(send, recv, send_sem.at[0]).wait()
    pltpu.make_async_copy(back_send, back_recv, send_sem.at[1]).wait()


def on_device(sizes, point_data, point_cells, send_counts):
    data = jnp.transpose(point_data[0], (1, 2, 0))
    cells = jnp.transpose(point_cells[0], (1, 2, 0))
    dma = pltpu.SemaphoreType.DMA
    shapes = [((608, POINTS), BF16)] * GROUPS + [((1040, POINTS), BF16)] * GROUPS + [
        ((7, CAP, DEVICES), F32), ((3, CAP, DEVICES), jnp.int32), ((1, DEVICES), jnp.int32),
        ((DEVICES, WIDTH), F32), ((DEVICES, WIDTH), F32), ((1, WIDTH), F32), ((CHANNELS, CAP, DEVICES), F32),
        ((608, 512), F32), ((608, 128), F32), ((48, 512), F32), ((ROWS, 512), BF16),
        ((GROUPS, 512, POINTS), BF16), ((GROUPS, ROWS, POINTS), F32), ((GROUPS, 8, POINTS), F32),
        ((48, 128), F32), ((ROWS, 128), F32), ((CAP, DEVICES), F32),
        ((DEVICES, DEVICES), F32), ((DEVICES, DEVICES), F32), ((1, DEVICES), F32),
    ]
    u, returned = pl.pallas_call(
        functools.partial(kernel, sizes),
        out_shape=[jax.ShapeDtypeStruct(s, F32) for s in (FIELD, (CAP, DEVICES))],
        in_specs=[pl.BlockSpec(memory_space=pltpu.HBM)] * 3,
        out_specs=[vmem()] * 2,
        scratch_shapes=[pltpu.VMEM(*s) for s in shapes]
        + [dma((3,)), dma((2,)), dma((2,))]
        + [pltpu.VMEM(s, F32) for s in SOLVE_SHAPES]
        + [dma((7,)), dma((7,)), dma((22,)), dma((22,)), dma((2, 24)), dma((2, 24)), dma((7,)), dma((7,))],
        compiler_params=pltpu.CompilerParams(
            vmem_limit_bytes=48 * 1024 * 1024, collective_id=0, has_side_effects=True
        ),
        name="reconstruct",
    )(*[pltpu.with_memory_space_constraint(v, pltpu.HBM) for v in (data, cells, send_counts)])
    u, returned = pl.pallas_call(
        put_out,
        out_shape=[jax.ShapeDtypeStruct(s, F32) for s in (FIELD, (CAP, DEVICES))],
        in_specs=[vmem()] * 2,
        out_specs=[pl.BlockSpec(memory_space=pl.ANY)] * 2,
        scratch_shapes=[dma((2,))],
        compiler_params=pltpu.CompilerParams(vmem_limit_bytes=1024 * 1024),
        name="put_out",
    )(u, returned)
    return u.reshape(16, 16, 128), returned.T[None]


def put_out(u_ref, value_ref, u_out, value_out, sems):
    copies = [
        pltpu.make_async_copy(u_ref, u_out, sems.at[0]),
        pltpu.make_async_copy(value_ref, value_out, sems.at[1]),
    ]
    for copy in copies:
        copy.start()
    for copy in copies:
        copy.wait()


def solution(mesh):
    sizes = tuple(mesh.shape[name] for name in ("gx", "gy", "gz"))
    spread_over = ("gx", "gy", "gz")
    in_specs = (P(spread_over, None, None, None), P(spread_over, None, None, None), P(spread_over, None))
    out_specs = (P("gx", "gy", "gz"), P(spread_over, None, None))
    return jax.shard_map(
        functools.partial(on_device, sizes), mesh=mesh, in_specs=in_specs, out_specs=out_specs, check_vma=False
    )
```

```python
import functools

import jax
import jax.numpy as jnp
from jax import lax
from jax.experimental import pallas as pl
from jax.experimental.pallas import tpu as pltpu
from jax.sharding import PartitionSpec as P

MESH = pl.DeviceIdType.MESH
F32 = jnp.float32
BF16 = jnp.bfloat16

DEVICES = 128
CAP = 32
CHANNELS = 10
WIDTH = 384
POINTS = 512
ROWS = 304
ITERS = 6
GROUPS = CAP * DEVICES // POINTS

base_screen = 0.25
point_screen = 4.0


def sweep_factors():
    half_width = 6.0 / (6.0 + base_screen)
    rho_prev = half_width
    factors = []
    for _ in range(ITERS - 1):
        rho_next = 1.0 / (2.0 / half_width - rho_prev)
        factors.append((rho_next * rho_prev, 2.0 * rho_next / half_width))
        rho_prev = rho_next
    return factors


def position(sizes):
    return tuple(lax.axis_index(name) for name in ("gx", "gy", "gz"))


def vmem():
    return pl.BlockSpec(memory_space=pltpu.VMEM)


def greet(me, meanwhile):
    barrier = pltpu.get_barrier_semaphore()

    @pl.loop(0, DEVICES - 8, step=8)
    def _(step):
        for q in range(8):
            pl.semaphore_signal(barrier, inc=1, device_id=me ^ (step + q + 1), device_id_type=pl.DeviceIdType.LOGICAL)

    for q in range(DEVICES - 7, DEVICES):
        pl.semaphore_signal(barrier, inc=1, device_id=me ^ q, device_id_type=pl.DeviceIdType.LOGICAL)
    meanwhile()
    pl.semaphore_wait(barrier, DEVICES - 1)


def exchange_rows(me, send, recv, sent, send_sem, recv_sem):
    def post(step):
        other = me ^ ((step * 37) & (DEVICES - 1))
        pltpu.make_async_remote_copy(
            src_ref=send.at[pl.ds(other, 1)],
            dst_ref=recv.at[pl.ds(me, 1)],
            send_sem=send_sem,
            recv_sem=recv_sem,
            device_id=other,
            device_id_type=pl.DeviceIdType.LOGICAL,
        ).start()

    @pl.loop(0, DEVICES - 8, step=8)
    def _(step):
        for q in range(8):
            post(step + q + 1)

    for q in range(DEVICES - 7, DEVICES):
        post(q)
    pltpu.make_async_copy(send.at[pl.ds(me, 1)], recv.at[pl.ds(me, 1)], recv_sem).start()
    pltpu.make_async_copy(send.at[pl.ds(me, 1)], sent, send_sem).start()
    pltpu.make_async_copy(send, recv, recv_sem).wait()


def prepare_rows(data_ref, cells_ref, counts_ref, send):
    slot = lax.broadcasted_iota(jnp.int32, (CAP, DEVICES), 0)
    weight = jnp.where(slot < counts_ref[...], data_ref[3], 0.0)
    parts = [data_ref[c] * weight for c in range(3)] + [weight]
    parts += [data_ref[4 + c] for c in range(3)] + [cells_ref[c].astype(F32) for c in range(3)]
    parts += [jnp.zeros((WIDTH - CAP * CHANNELS, DEVICES), F32)]
    send[...] = jnp.concatenate(parts, axis=0).T


def split(value):
    high = value.astype(BF16)
    return high, (value - high.astype(F32)).astype(BF16)


WIDE = 256


def lane_rows(d_ref, group, block, channels):
    first = (group * POINTS + block * WIDE) // DEVICES
    wide = lambda c, q: jnp.broadcast_to(d_ref[c, pl.ds(first + q, 1), :], (16, DEVICES))
    return [jnp.concatenate([wide(c, q) for q in range(WIDE // DEVICES)], axis=1) for c in channels]


def tile_iota():
    return lax.broadcasted_iota(jnp.int32, (16, WIDE), 0).astype(F32).astype(BF16)


def build_block(d_ref, group, block, a_ref, b_ref, c_ref, x_ref):
    iota = tile_iota()
    zero = jnp.zeros((16, WIDE), BF16)
    lanes = slice(block * WIDE, (block + 1) * WIDE)
    v = lane_rows(d_ref, group, block, range(4))
    fx, fy, fz, cx, cy, cz = lane_rows(d_ref, group, block, range(4, 10))
    bz = cz.astype(BF16)
    bz1 = (cz + 1.0).astype(BF16)
    g0 = [split(v[c] * (1.0 - fz)) for c in range(4)]
    g1 = [split(v[c] * fz) for c in range(4)]
    for t in range(8):
        at = iota + jnp.asarray(16 * t, BF16)
        z0, z1 = bz == at, bz1 == at
        for c in range(4):
            for part in range(2):
                value = jnp.where(z0, g0[c][part], jnp.where(z1, g1[c][part], zero))
                b_ref[512 * part + 128 * c + 16 * t : 512 * part + 128 * c + 16 * t + 16, lanes] = value
    by, by1 = cy.astype(BF16), (cy + 1.0).astype(BF16)
    y0, y1 = by == iota, by1 == iota
    near, far = [], []
    for along, out in ((1.0 - fx, near), (fx, far)):
        w0, w1 = split(along * (1.0 - fy)), split(along * fy)
        for part in range(2):
            out.append(jnp.where(y0, w0[part], jnp.where(y1, w1[part], zero)))
    bx = cx.astype(BF16)
    below = None
    for x in range(17):
        here = bx == x
        for part in range(2):
            value = near[part] if below is None else jnp.where(below, far[part], zero)
            value = jnp.where(here, near[part], zero if below is None else value)
            first = (352 * part + 16 * x) if x < 16 else 256 + 48 * part
            a_ref[first : first + 16, lanes] = value
        below = here
    bx1 = (cx + 1.0).astype(BF16)
    edge = jnp.where(cy == 15.0, fy, 0.0)
    e0, e1 = split((1.0 - fx) * edge), split(fx * edge)
    for t in range(2):
        at = iota + jnp.asarray(16 * t, BF16)
        x0, x1 = bx == at, bx1 == at
        for part in range(2):
            first = 272 + 48 * part + 16 * t
            a_ref[first : first + 16, lanes] = jnp.where(x0, e0[part], jnp.where(x1, e1[part], zero))
    x_near, x_far = split(1.0 - fx), split(fx)
    for t in range(2):
        at = iota + jnp.asarray(16 * t, BF16)
        x0, x1 = bx == at, bx1 == at
        for part in range(2):
            first = 32 * part + 16 * t
            x_ref[first : first + 16, lanes] = jnp.where(x0, x_near[part], jnp.where(x1, x_far[part], zero))
    over = jnp.where(cz == 127.0, fz, 0.0)
    over0, over1 = over * (1.0 - fy), over * fy
    last = [zero, zero]
    for c in range(4):
        w0, w1 = split(v[c] * over0), split(v[c] * over1)
        for part in range(2):
            first = 80 * part + 16 * c
            c_ref[first : first + 16, lanes] = jnp.where(y0, w0[part], jnp.where(y1, w1[part], zero))
            last[part] = jnp.where(iota == c, w1[part], last[part])
    for part in range(2):
        c_ref[80 * part + 64 : 80 * part + 80, lanes] = jnp.where(by == 15, last[part], zero)


ROW_DIMS = (((1,), (1,)), ((), ()))


def rows_by_rows(left, right):
    return lax.dot_general(left, right, ROW_DIMS, preferred_element_type=F32)


def multiply_outside(piece, a_ref, b_ref, c_ref, x_ref, acc_ref, ov_ref):
    if piece == 0:
        acc_ref[0:352, 0:256] += rows_by_rows(a_ref[0:352, :], b_ref[0:256, :])
    elif piece == 1:
        acc_ref[0:352, 256:512] += rows_by_rows(a_ref[0:352, :], b_ref[256:512, :])
    elif piece == 2:
        acc_ref[256:304, :] += rows_by_rows(a_ref[256:304, :], b_ref[512:1024, :])
    else:
        ov_ref[:, 0:64] += rows_by_rows(c_ref[...], x_ref[...])


def splat_outside(d_ref, acc_ref, ov_ref, tiles):
    acc_ref[...] = jnp.zeros_like(acc_ref)
    ov_ref[...] = jnp.zeros_like(ov_ref)
    blocks = POINTS // WIDE
    for block in range(blocks):
        build_block(d_ref, 0, block, *tiles[0])
    for group in range(GROUPS):
        for piece in range(4):
            if group + 1 < GROUPS and piece < blocks:
                build_block(d_ref, group + 1, piece, *tiles[group + 1])
            multiply_outside(piece, *tiles[group], acc_ref, ov_ref)


def splat_inside(acc_ref, tiles):
    for a_ref, b_ref, _, _ in tiles:
        acc_ref[352:608, :] += rows_by_rows(a_ref[352:608, :], b_ref[0:512, :])
        acc_ref[0:256, :] += rows_by_rows(a_ref[0:256, :], b_ref[512:1024, :])


def interpolation_tables(d_ref, r_ref, w_ref):
    iota = tile_iota()
    iota_f = iota.astype(F32)
    zero = jnp.zeros((16, WIDE), BF16)

    @pl.loop(0, GROUPS)
    def _(group):
        r_ref[group, 400:512, :] = jnp.zeros((112, POINTS), BF16)
        for block in range(POINTS // WIDE):
            lanes = slice(block * WIDE, (block + 1) * WIDE)
            fx, fy, fz, cx, cy, cz = lane_rows(d_ref, group, block, range(4, 10))
            bz, bz1 = cz.astype(BF16), (cz + 1.0).astype(BF16)
            g0, g1 = split(1.0 - fz), split(fz)
            for t in range(8):
                at = iota + jnp.asarray(16 * t, BF16)
                z0, z1 = bz == at, bz1 == at
                high, low = [jnp.where(z0, g0[part], jnp.where(z1, g1[part], zero)) for part in range(2)]
                r_ref[group, 16 * t : 16 * t + 16, lanes] = high
                r_ref[group, 128 + 16 * t : 144 + 16 * t, lanes] = high
                r_ref[group, 256 + 16 * t : 272 + 16 * t, lanes] = low
            picked = jnp.where(iota <= 1, g1[0], jnp.where(iota == 2, g1[1], zero))
            r_ref[group, 384:400, lanes] = jnp.where(bz == 127, picked, zero)
            hat_y = jnp.where(cy == iota_f, 1.0 - fy, jnp.where(cy + 1.0 == iota_f, fy, 0.0))
            near, far = (1.0 - fx) * hat_y, fx * hat_y
            for x in range(17):
                w_ref[group, 16 * x : 16 * x + 16, lanes] = jnp.where(cx == x, near, jnp.where(cx == x - 1, far, 0.0))
            edge = jnp.where(cy == 15.0, fy, 0.0)
            for t in range(2):
                at = iota_f + 16.0 * t
                hat = jnp.where(cx == at, 1.0 - fx, jnp.where(cx + 1.0 == at, fx, 0.0))
                w_ref[group, 272 + 16 * t : 288 + 16 * t, lanes] = hat * edge


def weighted(g, w_ref, group, first):
    rows = g.shape[0]
    total = g[0:8] * w_ref[group, first : first + 8]
    for i in range(1, rows // 8):
        total = total + g[8 * i : 8 * i + 8] * w_ref[group, first + 8 * i : first + 8 * i + 8]
    return total


def high_and_low(l_ref, first, value):
    rows = pl.ds(first, value.shape[0])
    high, low = split(value)
    l_ref[rows, 0:128] = high
    l_ref[rows, 128:256] = low
    l_ref[rows, 256:384] = high


def interpolate_inside(u_ref, part_ref, l_ref, r_ref, w_ref):
    high_and_low(l_ref, 0, u_ref[...].reshape(256, 128))

    @pl.loop(0, GROUPS, step=4)
    def _(first):
        for step in range(4):
            group = first + step
            g = jnp.dot(l_ref[0:256, 0:384], r_ref[group, 0:384], preferred_element_type=F32)
            part_ref[group] = weighted(g, w_ref, group, 0)


def interpolate(halo_ref, uz_ref, part_ref, out_ref, l_ref, r_ref, w_ref):
    high_and_low(l_ref, 256, halo_ref[...])
    top = jnp.broadcast_to(uz_ref[:, 0:1], (ROWS, 128))
    high = top.astype(BF16).astype(F32)
    lane = lax.broadcasted_iota(jnp.int32, (ROWS, 128), 1)
    low = jnp.where(lane == 1, top - high, 0.0)
    l_ref[:, 384:512] = jnp.where(jnp.logical_or(lane == 0, lane == 2), high, low).astype(BF16)

    @pl.loop(0, GROUPS, step=4)
    def _(first):
        for step in range(4):
            group = first + step
            g = jnp.dot(l_ref[256:ROWS, :], r_ref[group], preferred_element_type=F32)
            total = part_ref[group] + weighted(g, w_ref, group, 256)
            g = jnp.dot(l_ref[0:256, 384:512], r_ref[group, 384:512], preferred_element_type=F32)
            value = jnp.sum(total + weighted(g, w_ref, group, 0), axis=0, keepdims=True)
            count = POINTS // DEVICES
            for q in range(count):
                out_ref[pl.ds(group * count + q, 1), :] = value[:, q * DEVICES : (q + 1) * DEVICES]


FACES = [(1, 0, 0), (0, 1, 0), (0, 0, 1)]
UPPER = FACES + [(1, 1, 0), (1, 0, 1), (0, 1, 1), (1, 1, 1)]


def roll_to(tile, source, target):
    shift = (target - source) % 128
    return pltpu.roll(tile, shift, 1) if shift else tile


def grid_iotas():
    lane = lax.broadcasted_iota(jnp.int32, (8, 128), 1)
    sub = lax.broadcasted_iota(jnp.int32, (8, 128), 0)
    return lane, sub


def pack(read, source):
    lane, _ = grid_iotas()
    packed = jnp.zeros((8, 128), F32)
    for i in range(32):
        packed = jnp.where(lane == i, roll_to(read(i), source, i), packed)
    return packed


def slab_star(comb, along_x, along_y, along_z, rows, tiles):
    n = along_y.shape[0]
    total = comb(along_x[0:n], along_x[2 : n + 2])
    sub3 = lax.broadcasted_iota(jnp.int32, (n, 8, 128), 1)
    down = pltpu.roll(along_y.reshape(2 * n, 8, 128), 1, 1).reshape(n, 2, 8, 128)
    up = pltpu.roll(along_y.reshape(2 * n, 8, 128), 7, 1).reshape(n, 2, 8, 128)
    edge = [jnp.stack([rows(side, i) for i in range(n)]) for side in range(2)]
    first, last = sub3 == 0, sub3 == 7
    low = jnp.stack([jnp.where(first, edge[0], down[:, 0]), jnp.where(first, down[:, 0], down[:, 1])], axis=1)
    high = jnp.stack([jnp.where(last, up[:, 1], up[:, 0]), jnp.where(last, edge[1], up[:, 1])], axis=1)
    total = total + comb(low, high)
    lanes = lax.broadcasted_iota(jnp.int32, (2 * n, 8, 128), 2)
    flat = along_z.reshape(16 * n, 128)
    sides = []
    for side, shift, at in ((0, 1, 0), (1, 127, 127)):
        edge = jnp.stack([tiles(side, i, t) for i in range(n) for t in range(2)])
        sides.append(jnp.where(lanes == at, edge, pltpu.roll(flat, shift, 1).reshape(2 * n, 8, 128)))
    return total + comb(*sides).reshape(n, 2, 8, 128)


def layer_star_y(comb, side, fx, fy, fz):
    row = lax.broadcasted_iota(jnp.int32, (16, 128), 0)
    lane16 = lax.broadcasted_iota(jnp.int32, (16, 128), 1)
    plane = fx["plane"][side]
    low = jnp.where(row == 0, jnp.broadcast_to(fx["xy"][0][side], (16, 128)), pltpu.roll(plane, 1, 0))
    high = jnp.where(row == 15, jnp.broadcast_to(fx["xy"][1][side], (16, 128)), pltpu.roll(plane, 15, 0))
    total = comb(low, high)
    outer, own = fy["plane2"][side], fy["own_row"][side]
    total = total + (comb(outer, own) if side == 0 else comb(own, outer))
    plane = fz["plane"][side]
    parity, source = (1, 7) if side == 0 else (0, 0)
    sides = []
    for z_side, shift, at in ((0, 1, 0), (1, 127, 127)):
        values = jnp.broadcast_to(fz["yz"][side][z_side][source : source + 1], (16, 128))
        column = jnp.sum(jnp.where(lane16 == 2 * row + parity, values, 0.0), axis=1, keepdims=True)
        sides.append(jnp.where(lane16 == at, jnp.broadcast_to(column, (16, 128)), pltpu.roll(plane, shift, 1)))
    return total + comb(*sides)


def layer_star_z(comb, side, fx, fy, fz):
    lane, sub = grid_iotas()
    layer = fx["zp"][side]
    low = jnp.where(lane < 2, roll_to(fx["xz"][0][side], 30, 0), pltpu.roll(layer, 2, 1))
    high = jnp.where(lane >= 30, roll_to(fx["xz"][1][side], 0, 30), pltpu.roll(layer, 126, 1))
    total = comb(low, high)
    layer = fy["zp"][side]
    down, up = pltpu.roll(layer, 1, 0), pltpu.roll(layer, 7, 0)
    odd = lax.rem(lane, 2) == 1
    beyond = pltpu.roll(pltpu.roll(fy["yz"][0][side], 1, 0), 127, 1)
    low = jnp.where(sub == 0, jnp.where(odd, pltpu.roll(down, 1, 1), beyond), down)
    beyond = pltpu.roll(pltpu.roll(fy["yz"][1][side], 7, 0), 1, 1)
    high = jnp.where(sub == 7, jnp.where(odd, beyond, pltpu.roll(up, 127, 1)), up)
    total = total + comb(low, high)
    outer, own = fz["zp2"][side], fz["own_z"][side]
    total = total + (comb(outer, own) if side == 0 else comb(own, outer))
    return jnp.where(lane < 32, total, 0.0)


def solve(
    sizes, here, own_rows, tables, own_values, s_ref, ov_ref, out_ref, u_ref, halo_ref, uz_ref,
    m_ref, zs_ref, sx, sy, sxy, sz,
    z5, xa, xb, ya, yb, exy, za, exz, eyz,
    pw, rw, z3, px, rx, py, py2, ry, pxy, pz, pxz, pyz, inv_ref, diag_ref, plane_ref, uzp,
    fx, fy, fxy, fz, s_send, s_recv, g_send, g_recv, h_send, h_recv, f_send, f_recv,
):
    lower = [here[a] > 0 for a in range(3)]
    upper = [here[a] < sizes[a] - 1 for a in range(3)]

    def present(step):
        wanted = [(upper if step[a] > 0 else lower)[a] for a in range(3) if step[a]]
        return functools.reduce(jnp.logical_and, wanted)

    def opposite(step):
        return tuple(-v for v in step)

    def message(step, source, target, send, recv):
        copy = pltpu.make_async_remote_copy(
            src_ref=source, dst_ref=target, send_sem=send, recv_sem=recv,
            device_id=tuple(here[a] + step[a] for a in range(3)), device_id_type=MESH,
        )
        return step, copy

    def start(messages):
        for step, copy in messages:
            @pl.when(present(step))
            def _(copy=copy):
                copy.start()

    def receive(messages):
        for step, copy in messages:
            @pl.when(present(opposite(step)))
            def _(copy=copy):
                copy.wait_recv()

    def drain(messages):
        for step, copy in messages:
            @pl.when(present(step))
            def _(copy=copy):
                copy.wait_send()

    lane, sub = grid_iotas()
    zero = jnp.zeros((8, 128), F32)

    def over(first):
        tile = ov_ref[pl.ds(first, 8), :] + ov_ref[pl.ds(first + 80, 8), :]
        return tile + pltpu.roll(tile, 96, 1)

    packed = zero
    rest = roll_to(over(64), 0, 32)
    for c in range(4):
        for t in range(2):
            tile = over(16 * c + 8 * t)
            at = 32 * c + 16 * t
            packed = jnp.where(jnp.logical_and(lane >= at, lane < at + 16), roll_to(tile, 0, at), packed)
            rest = jnp.where(lane == 4 * t + c, roll_to(tile, 16, 4 * t + c), rest)
    zs_ref[0] = packed
    zs_ref[1] = rest
    out_ref[...] = s_ref[256:304, :] + s_ref[304:352, :]
    sources = [out_ref.at[0:16], out_ref.at[16:32], zs_ref.at[0], out_ref.at[32:33]] + [zs_ref.at[1]] * 3
    targets = [sx, sy, sz.at[0], sxy, sz.at[1], sz.at[2], sz.at[3]]
    mass = [message(UPPER[i], sources[i], targets[i], s_send.at[i], s_recv.at[i]) for i in range(7)]
    start(mass[::-1])
    own_rows()
    for c in range(4):
        columns = slice(128 * c, 128 * c + 128)
        m_ref[c] = (s_ref[0:256, columns] + s_ref[352:608, columns]).reshape(16, 2, 8, 128)
    receive(mass)
    for c in range(4):
        columns = slice(128 * c, 128 * c + 128)
        m_ref[c, 0] += sx[:, columns].reshape(2, 8, 128)
        from_y = sy[:, columns]
        for x in range(16):
            row = from_y[x : x + 1, :] + jnp.where(lane == 0, roll_to(sz[2], 32 + x, 0), 0.0)[c : c + 1, :]
            m_ref[c, x, 0, 0:1, :] += row
        for i in range(32):
            m_ref[c, i // 2, i % 2] += jnp.where(lane == 0, roll_to(sz[0], 32 * c + 16 * (i % 2) + i // 2, 0), 0.0)
        for t in range(2):
            m_ref[c, 0, t] += jnp.where(lane == 0, roll_to(sz[1], 4 * t + c, 0), 0.0)
        corner = sxy[:, columns] + jnp.where(lane == 0, roll_to(sz[3], 48, 0), 0.0)[c : c + 1, :]
        m_ref[c, 0, 0, 0:1, :] += corner

    def end(side, depth, size):
        return size - 1 - depth if side == 0 else depth

    def toward(side):
        return 1 if side == 0 else -1

    def mesh_step(**sides):
        return tuple(toward(sides[name]) if name in sides else 0 for name in "xyz")

    def numbered(entries, send, recv):
        return [message(step, a, b, send.at[i], recv.at[i]) for i, (step, a, b) in enumerate(entries)]

    for side in range(2):
        for i, (c, depth) in enumerate(((0, 0), (2, 0), (1, 0), (3, 0), (2, 1))):
            z5[side, i] = pack(lambda k, c=c: m_ref[c, k // 2, k % 2], end(side, depth, 128))
    entries = []
    for a in range(2):
        for b in range(2):
            entries.append((mesh_step(x=a, y=b), m_ref.at[0:2, end(a, 0, 16), 1 - b, 7 - 7 * b, :], exy.at[a, b]))
            entries.append((mesh_step(x=a, z=b), z5.at[b, 0:2], exz.at[a, b]))
            entries.append((mesh_step(y=a, z=b), z5.at[b, 1:3], eyz.at[a, b]))
    for a in range(2):
        first = 14 if a == 0 else 0
        entries.append((mesh_step(x=a), m_ref.at[0, first : first + 2], xa.at[a]))
        entries.append((mesh_step(x=a), m_ref.at[1:4, end(a, 0, 16)], xb.at[a]))
        entries.append((mesh_step(y=a), m_ref.at[:, :, 1 - a, 7 - 7 * a, :], ya.at[a]))
        entries.append((mesh_step(y=a), m_ref.at[1, :, 1 - a, 6 - 5 * a, :], yb.at[a]))
        entries.append((mesh_step(z=a), z5.at[a], za.at[a]))
    ghost = numbered(entries, g_send, g_recv)
    start(ghost)
    tables()
    receive(ghost)

    def tiles_of(zp, xz):
        def tiles(side, i, t):
            at = 0 if side == 0 else 127
            if i == 0:
                return roll_to(xz[0][side], 30 + t, at)
            if i == 17:
                return roll_to(xz[1][side], t, at)
            return roll_to(zp[side], 2 * (i - 1) + t, at)
        return tiles

    def rows_of(row, xy):
        def rows(side, i):
            value = xy[0][side] if i == 0 else xy[1][side] if i == 17 else row(side, i - 1)
            return jnp.broadcast_to(value, (8, 128))
        return rows

    def both(get):
        return [get(0), get(1)]

    def grid2(get):
        return [[get(a, b) for b in range(2)] for a in range(2)]

    def difference(low, high):
        return high - low

    def plus(low, high):
        return low + high

    nx = {
        "plane": both(lambda a: ya[a, 0]), "xy": grid2(lambda a, b: exy[a, b, 0:1]),
        "zp": both(lambda a: za[a, 0]), "xz": grid2(lambda a, b: exz[a, b, 0]),
    }
    ny = {
        "plane2": both(lambda a: yb[a]), "own_row": both(lambda a: m_ref[1, :, a, 7 * a, :]),
        "zp": both(lambda a: za[a, 2]), "yz": grid2(lambda a, b: eyz[a, b, 1]),
    }
    nz = {
        "plane": both(lambda a: ya[a, 2]), "yz": grid2(lambda a, b: eyz[a, b, 0]),
        "zp2": both(lambda a: za[a, 4]), "own_z": both(lambda a: z5[1 - a, 1]),
    }
    along_x = jnp.concatenate([xa[0], m_ref[0], xa[1]], axis=0)
    along_y = jnp.concatenate([xb[0, 0:1], m_ref[1], xb[1, 0:1]], axis=0)
    along_z = jnp.concatenate([xb[0, 1:2], m_ref[2], xb[1, 1:2]], axis=0)
    rows = rows_of(lambda side, x: ya[side, 1, x : x + 1, :], grid2(lambda a, b: exy[a, b, 1:2]))
    tiles = tiles_of(both(lambda a: za[a, 1]), grid2(lambda a, b: exz[a, b, 1]))
    source = -0.5 * slab_star(difference, along_x, along_y, along_z, rows, tiles)

    def shift_diagonal(mass_part):
        return 6.0 + base_screen + point_screen * mass_part

    def inverse(diagonal, exists):
        return jnp.where(exists, 1.0 / diagonal, 0.0)

    slabs = shift_diagonal(jnp.concatenate([xb[0, 2:3], m_ref[3], xb[1, 2:3]], axis=0))
    diag_ref[...] = slabs
    inv_ref[0] = inverse(slabs[0], lower[0])
    inv_ref[1:17] = 1.0 / slabs[1:17]
    inv_ref[17] = inverse(slabs[17], upper[0])
    exists = lambda axis, side: (lower, upper)[side][axis]
    diag_y = both(lambda a: shift_diagonal(ya[a, 3]))
    inv_y = both(lambda a: inverse(diag_y[a], exists(1, a)))
    diag_z = both(lambda a: shift_diagonal(za[a, 3]))
    inv_z = both(lambda a: inverse(diag_z[a], exists(2, a)))

    def second_sweep(round_index, slabs, planes, layers, residual, keep, push):
        for side in range(2):
            plane_ref[round_index, side] = planes[side]
        own = slabs[1:17]
        around = slab_star(
            plus, slabs, own, own,
            lambda side, i: jnp.broadcast_to(plane_ref[round_index, side, i : i + 1, :], (8, 128)),
            lambda side, i, t: roll_to(layers[side], 2 * i + t, 0 if side == 0 else 127),
        )
        residual = residual - (diag_ref[1:17] * own - around)
        return residual, keep * own + push * (residual * inv_ref[1:17])

    factors = sweep_factors()
    slabs = source * inv_ref[...]
    planes = both(lambda a: -0.5 * layer_star_y(difference, a, nx, ny, nz) * inv_y[a])
    layers = both(lambda a: -0.5 * layer_star_z(difference, a, nx, ny, nz) * inv_z[a])
    u_ref[...] = slabs[1:17]
    residual, following = second_sweep(0, slabs, planes, layers, source[1:17], *factors[0])

    rounds = []
    for e in range(2):
        pw[e] = following
        rw[e] = residual
        for side in range(2):
            for i, (ref, depth) in enumerate(((pw, 0), (pw, 1), (rw, 0))):
                z3[e, side, i] = pack(lambda k, ref=ref: ref[e, k // 2, k % 2], end(side, depth, 128))
        entries = []
        for a in range(2):
            for b in range(2):
                row = pw.at[e, end(a, 0, 16), 1 - b, 7 - 7 * b : 8 - 7 * b, :]
                entries.append((mesh_step(x=a, y=b), row, pxy.at[e, a, b]))
                entries.append((mesh_step(x=a, z=b), z3.at[e, b, 0], pxz.at[e, a, b]))
                entries.append((mesh_step(y=a, z=b), z3.at[e, b, 0], pyz.at[e, a, b]))
        for a in range(2):
            first = 14 if a == 0 else 0
            entries.append((mesh_step(x=a), pw.at[e, first : first + 2], px.at[e, a]))
            entries.append((mesh_step(x=a), rw.at[e, end(a, 0, 16)], rx.at[e, a]))
            entries.append((mesh_step(y=a), pw.at[e, :, 1 - a, 7 - 7 * a, :], py.at[e, a]))
            entries.append((mesh_step(y=a), pw.at[e, :, 1 - a, 6 - 5 * a, :], py2.at[e, a]))
            entries.append((mesh_step(y=a), rw.at[e, :, 1 - a, 7 - 7 * a, :], ry.at[e, a]))
            entries.append((mesh_step(z=a), z3.at[e, a], pz.at[e, a]))
        ghosts = numbered(entries, h_send.at[e], h_recv.at[e])
        rounds.append(ghosts)
        start(ghosts)
        u_ref[...] += following
        receive(ghosts)
        p = {
            "plane": both(lambda a: py[e, a]), "plane2": both(lambda a: py2[e, a]),
            "own_row": both(lambda a: pw[e, :, a, 7 * a, :]), "xy": grid2(lambda a, b: pxy[e, a, b]),
            "zp": both(lambda a: pz[e, a, 0]), "zp2": both(lambda a: pz[e, a, 1]),
            "own_z": both(lambda a: z3[e, 1 - a, 0]),
            "xz": grid2(lambda a, b: pxz[e, a, b]), "yz": grid2(lambda a, b: pyz[e, a, b]),
        }
        wide = jnp.concatenate([px[e, 0], pw[e], px[e, 1]], axis=0)
        middle = wide[1:19]
        rows = rows_of(lambda side, x: py[e, side, x : x + 1, :], p["xy"])
        around = slab_star(plus, wide, middle, middle, rows, tiles_of(p["zp"], p["xz"]))
        residual = jnp.concatenate([rx[e, 0][None], rw[e], rx[e, 1][None]], axis=0)
        residual = residual - (diag_ref[...] * middle - around)
        keep, push = factors[2 * e + 1]
        slabs = keep * middle + push * (residual * inv_ref[...])

        def outside(own, rest, diagonal, inverse_diagonal, star):
            rest = rest - (diagonal * own - star)
            return keep * own + push * (rest * inverse_diagonal)

        planes = both(lambda a: outside(p["plane"][a], ry[e, a], diag_y[a], inv_y[a], layer_star_y(plus, a, p, p, p)))
        layers = both(lambda a: outside(p["zp"][a], pz[e, a, 2], diag_z[a], inv_z[a], layer_star_z(plus, a, p, p, p)))
        u_ref[...] += slabs[1:17]
        residual, following = second_sweep(e + 1, slabs, planes, layers, residual[1:17], *factors[2 * e + 2])
    u_ref[...] += following

    uzp[...] = pack(lambda i: u_ref[i // 2, i % 2], 0)
    sources = [u_ref.at[0], u_ref.at[:, 0, 0, :], uzp, u_ref.at[0, 0, 0:1]] + [uzp] * 3
    targets = [fx, fy, fz.at[0], fxy, fz.at[1], fz.at[2], fz.at[3]]
    layer = [message(opposite(UPPER[i]), sources[i], targets[i], f_send.at[i], f_recv.at[i]) for i in range(7)]
    start(layer[::-1])
    own_values()
    receive(layer)
    halo_ref[0:16] = fx[...].reshape(16, 128)
    halo_ref[16:32] = fy[...]
    halo_ref[32:40] = jnp.where(sub == 0, jnp.broadcast_to(fxy[...], (8, 128)), 0.0)
    halo_ref[40:48] = zero
    for i in range(32):
        uz_ref[8 * i : 8 * i + 8] = roll_to(fz[0], i, 0)
    for t in range(2):
        uz_ref[256 + 8 * t : 264 + 8 * t] = roll_to(fz[1], t, 0)
        picked = jnp.where(lane == 2 * (8 * t + sub), jnp.broadcast_to(fz[2, 0:1], (8, 128)), 0.0)
        column = jnp.sum(picked, axis=1, keepdims=True)
        uz_ref[272 + 8 * t : 280 + 8 * t] = jnp.broadcast_to(column, (8, 128))
    uz_ref[288:296] = jnp.where(sub == 0, fz[3], 0.0)
    uz_ref[296:304] = zero

    def finish():
        for messages in (mass, ghost, *rounds, layer):
            drain(messages)

    return finish


FIELD = (16, 2, 8, 128)
SOLVE_SHAPES = [
    (4, *FIELD), (2, 8, 128), (16, 512), (16, 512), (1, 512), (4, 8, 128),
    (2, 5, 8, 128), (2, 2, 2, 8, 128), (2, 3, 2, 8, 128), (2, 4, 16, 128), (2, 16, 128), (2, 2, 2, 128),
    (2, 5, 8, 128), (2, 2, 2, 8, 128), (2, 2, 2, 8, 128),
    (2, *FIELD), (2, *FIELD), (2, 2, 3, 8, 128), (2, 2, 2, 2, 8, 128), (2, 2, 2, 8, 128),
    (2, 2, 16, 128), (2, 2, 16, 128), (2, 2, 16, 128), (2, 2, 2, 1, 128), (2, 2, 3, 8, 128),
    (2, 2, 2, 8, 128), (2, 2, 2, 8, 128), (18, 2, 8, 128), (18, 2, 8, 128), (3, 2, 16, 128), (8, 128),
    (2, 8, 128), (16, 128), (1, 128), (4, 8, 128),
]
LANDING = [2, 3, 4, 5, 7, 8, 9, 10, 11, 12, 13, 14, 18, 19, 20, 21, 22, 23, 24, 25, 26, 31, 32, 33, 34]


def kernel(sizes, data_hbm, cells_hbm, counts_hbm, u_ref, out_ref, *scratch):
    tiles, scratch = [scratch[i::GROUPS][:4] for i in range(GROUPS)], scratch[4 * GROUPS :]
    (data_ref, cells_ref, counts_ref, send, recv, sent, d_ref, acc_ref, ov_ref, face_ref,
     l_ref, r_ref, w_ref, part_ref, halo_ref, uz_ref, val_ref, back_send, back_recv, back_sent,
     in_sem, send_sem, recv_sem, *rest) = scratch
    here = position(sizes)
    me = (here[0] * sizes[1] + here[1]) * sizes[2] + here[2]
    for at in LANDING:
        rest[at][...] = jnp.zeros(rest[at].shape, F32)
    loads = [
        pltpu.make_async_copy(source, target, in_sem.at[i])
        for i, (source, target) in enumerate(((data_hbm, data_ref), (cells_hbm, cells_ref), (counts_hbm, counts_ref)))
    ]
    for load in loads:
        load.start()

    def meanwhile():
        for load in loads:
            load.wait()
        prepare_rows(data_ref, cells_ref, counts_ref, send)

    greet(me, meanwhile)
    exchange_rows(me, send, recv, sent, send_sem.at[0], recv_sem.at[0])
    d_ref[...] = recv[...].T[: CAP * CHANNELS].reshape(CHANNELS, CAP, DEVICES)
    splat_outside(d_ref, acc_ref, ov_ref, tiles)
    finish = solve(
        sizes, here, lambda: splat_inside(acc_ref, tiles), lambda: interpolation_tables(d_ref, r_ref, w_ref),
        lambda: interpolate_inside(u_ref, part_ref, l_ref, r_ref, w_ref),
        acc_ref, ov_ref, face_ref, u_ref, halo_ref, uz_ref, *rest,
    )
    interpolate(halo_ref, uz_ref, part_ref, val_ref, l_ref, r_ref, w_ref)
    padded = jnp.concatenate([val_ref[...], jnp.zeros((DEVICES - CAP, DEVICES), F32)], axis=0)
    back_send[...] = padded.T
    exchange_rows(me, back_send, back_recv, back_sent, send_sem.at[1], recv_sem.at[1])
    slot = lax.broadcasted_iota(jnp.int32, (CAP, DEVICES), 0)
    out_ref[...] = jnp.where(slot < counts_ref[...], back_recv[...].T[:CAP], 0.0)
    finish()
    pltpu.make_async_copy(send, recv, send_sem.at[0]).wait()
    pltpu.make_async_copy(back_send, back_recv, send_sem.at[1]).wait()


def on_device(sizes, point_data, point_cells, send_counts):
    data = jnp.transpose(point_data[0], (1, 2, 0))
    cells = jnp.transpose(point_cells[0], (1, 2, 0))
    dma = pltpu.SemaphoreType.DMA
    tile_rows = (608, 1024, 160, 64)
    shapes = [((rows, POINTS), BF16) for rows in tile_rows for _ in range(GROUPS)] + [
        ((7, CAP, DEVICES), F32), ((3, CAP, DEVICES), jnp.int32), ((1, DEVICES), jnp.int32),
        ((DEVICES, WIDTH), F32), ((DEVICES, WIDTH), F32), ((1, WIDTH), F32), ((CHANNELS, CAP, DEVICES), F32),
        ((608, 512), F32), ((160, 128), F32), ((48, 512), F32), ((ROWS, 512), BF16),
        ((GROUPS, 512, POINTS), BF16), ((GROUPS, ROWS, POINTS), F32), ((GROUPS, 8, POINTS), F32),
        ((48, 128), F32), ((ROWS, 128), F32), ((CAP, DEVICES), F32),
        ((DEVICES, DEVICES), F32), ((DEVICES, DEVICES), F32), ((1, DEVICES), F32),
    ]
    u, returned = pl.pallas_call(
        functools.partial(kernel, sizes),
        out_shape=[jax.ShapeDtypeStruct(s, F32) for s in (FIELD, (CAP, DEVICES))],
        in_specs=[pl.BlockSpec(memory_space=pltpu.HBM)] * 3,
        out_specs=[vmem()] * 2,
        scratch_shapes=[pltpu.VMEM(*s) for s in shapes]
        + [dma((3,)), dma((2,)), dma((2,))]
        + [pltpu.VMEM(s, F32) for s in SOLVE_SHAPES]
        + [dma((7,)), dma((7,)), dma((22,)), dma((22,)), dma((2, 24)), dma((2, 24)), dma((7,)), dma((7,))],
        compiler_params=pltpu.CompilerParams(
            vmem_limit_bytes=48 * 1024 * 1024, collective_id=0, has_side_effects=True
        ),
        name="reconstruct",
    )(*[pltpu.with_memory_space_constraint(v, pltpu.HBM) for v in (data, cells, send_counts)])
    u, returned = pl.pallas_call(
        put_out,
        out_shape=[jax.ShapeDtypeStruct(s, F32) for s in (FIELD, (CAP, DEVICES))],
        in_specs=[vmem()] * 2,
        out_specs=[pl.BlockSpec(memory_space=pl.ANY)] * 2,
        scratch_shapes=[dma((2,))],
        compiler_params=pltpu.CompilerParams(vmem_limit_bytes=1024 * 1024),
        name="put_out",
    )(u, returned)
    return u.reshape(16, 16, 128), returned.T[None]


def put_out(u_ref, value_ref, u_out, value_out, sems):
    copies = [
        pltpu.make_async_copy(u_ref, u_out, sems.at[0]),
        pltpu.make_async_copy(value_ref, value_out, sems.at[1]),
    ]
    for copy in copies:
        copy.start()
    for copy in copies:
        copy.wait()


def solution(mesh):
    sizes = tuple(mesh.shape[name] for name in ("gx", "gy", "gz"))
    spread_over = ("gx", "gy", "gz")
    in_specs = (P(spread_over, None, None, None), P(spread_over, None, None, None), P(spread_over, None))
    out_specs = (P("gx", "gy", "gz"), P(spread_over, None, None))
    return jax.shard_map(
        functools.partial(on_device, sizes), mesh=mesh, in_specs=in_specs, out_specs=out_specs, check_vma=False
    )
```

```python
import functools

import jax
import jax.numpy as jnp
from jax import lax
from jax.experimental import pallas as pl
from jax.experimental.pallas import tpu as pltpu
from jax.sharding import PartitionSpec as P

MESH = pl.DeviceIdType.MESH
F32 = jnp.float32
BF16 = jnp.bfloat16

DEVICES = 128
CAP = 32
CHANNELS = 10
WIDTH = 384
POINTS = 512
ROWS = 304
ITERS = 6
GROUPS = CAP * DEVICES // POINTS

base_screen = 0.25
point_screen = 4.0


def sweep_factors():
    half_width = 6.0 / (6.0 + base_screen)
    rho_prev = half_width
    factors = []
    for _ in range(ITERS - 1):
        rho_next = 1.0 / (2.0 / half_width - rho_prev)
        factors.append((rho_next * rho_prev, 2.0 * rho_next / half_width))
        rho_prev = rho_next
    return factors


def position(sizes):
    return tuple(lax.axis_index(name) for name in ("gx", "gy", "gz"))


def vmem():
    return pl.BlockSpec(memory_space=pltpu.VMEM)


def far_first():
    def hops(offset):
        fields = (offset >> 5) & 3, (offset >> 3) & 3, offset & 3
        return sum((0, 1, 2, 1)[field] for field in fields) + 0.5 * ((offset >> 2) & 1)

    return sorted(range(1, DEVICES), key=lambda offset: (-hops(offset), offset * 37 % DEVICES))


def greet(me, meanwhile):
    barrier = pltpu.get_barrier_semaphore()
    for offset in far_first():
        pl.semaphore_signal(barrier, inc=1, device_id=me ^ offset, device_id_type=pl.DeviceIdType.LOGICAL)
    meanwhile()
    pl.semaphore_wait(barrier, DEVICES - 1)


def exchange_rows(me, send, recv, sent, send_sem, recv_sem):
    for offset in far_first():
        other = me ^ offset
        pltpu.make_async_remote_copy(
            src_ref=send.at[pl.ds(other, 1)],
            dst_ref=recv.at[pl.ds(me, 1)],
            send_sem=send_sem,
            recv_sem=recv_sem,
            device_id=other,
            device_id_type=pl.DeviceIdType.LOGICAL,
        ).start()
    pltpu.make_async_copy(send.at[pl.ds(me, 1)], recv.at[pl.ds(me, 1)], recv_sem).start()
    pltpu.make_async_copy(send.at[pl.ds(me, 1)], sent, send_sem).start()
    pltpu.make_async_copy(send, recv, recv_sem).wait()


def prepare_rows(data_ref, cells_ref, counts_ref, send):
    slot = lax.broadcasted_iota(jnp.int32, (CAP, DEVICES), 0)
    weight = jnp.where(slot < counts_ref[...], data_ref[3], 0.0)
    parts = [data_ref[c] * weight for c in range(3)] + [weight]
    parts += [data_ref[4 + c] for c in range(3)] + [cells_ref[c].astype(F32) for c in range(3)]
    parts += [jnp.zeros((WIDTH - CAP * CHANNELS, DEVICES), F32)]
    send[...] = jnp.concatenate(parts, axis=0).T


def split(value):
    high = value.astype(BF16)
    return high, (value - high.astype(F32)).astype(BF16)


WIDE = 256


def tile(value):
    return jnp.concatenate([value, value], axis=0).astype(BF16)


def split_tile(value):
    high = tile(value)
    return high, tile(value - high[0:8].astype(F32))


def lane_rows(d_ref, group, block, channels, rows):
    first = (group * POINTS + block * WIDE) // DEVICES
    wide = lambda c, q: jnp.broadcast_to(d_ref[c, pl.ds(first + q, 1), :], (rows, DEVICES))
    return [jnp.concatenate([wide(c, q) for q in range(WIDE // DEVICES)], axis=1) for c in channels]


def tile_iota():
    return lax.broadcasted_iota(jnp.int32, (16, WIDE), 0).astype(F32).astype(BF16)


def build_block(d_ref, group, block, a_ref, b_ref, c_ref, x_ref):
    iota = tile_iota()
    zero = jnp.zeros((16, WIDE), BF16)
    lanes = slice(block * WIDE, (block + 1) * WIDE)
    v = lane_rows(d_ref, group, block, range(4), 8)
    fx, fy, fz, cx, cy, cz = lane_rows(d_ref, group, block, range(4, 10), 8)
    bz = tile(cz)
    bz1 = tile(cz + 1.0)
    g0 = [split_tile(v[c] * (1.0 - fz)) for c in range(4)]
    g1 = [split_tile(v[c] * fz) for c in range(4)]
    for t in range(8):
        at = iota + jnp.asarray(16 * t, BF16)
        z0, z1 = bz == at, bz1 == at
        for c in range(4):
            for part in range(2):
                value = jnp.where(z0, g0[c][part], jnp.where(z1, g1[c][part], zero))
                b_ref[512 * part + 128 * c + 16 * t : 512 * part + 128 * c + 16 * t + 16, lanes] = value
    by, by1 = tile(cy), tile(cy + 1.0)
    y0, y1 = by == iota, by1 == iota
    near, far = [], []
    for along, out in ((1.0 - fx, near), (fx, far)):
        w0, w1 = split_tile(along * (1.0 - fy)), split_tile(along * fy)
        for part in range(2):
            out.append(jnp.where(y0, w0[part], jnp.where(y1, w1[part], zero)))
    bx = tile(cx)
    below = None
    for x in range(17):
        here = bx == x
        for part in range(2):
            value = near[part] if below is None else jnp.where(below, far[part], zero)
            value = jnp.where(here, near[part], zero if below is None else value)
            first = (352 * part + 16 * x) if x < 16 else 256 + 48 * part
            a_ref[first : first + 16, lanes] = value
        below = here
    bx1 = tile(cx + 1.0)
    edge = jnp.where(cy == 15.0, fy, 0.0)
    e0, e1 = split_tile((1.0 - fx) * edge), split_tile(fx * edge)
    for t in range(2):
        at = iota + jnp.asarray(16 * t, BF16)
        x0, x1 = bx == at, bx1 == at
        for part in range(2):
            first = 272 + 48 * part + 16 * t
            a_ref[first : first + 16, lanes] = jnp.where(x0, e0[part], jnp.where(x1, e1[part], zero))
    x_near, x_far = split_tile(1.0 - fx), split_tile(fx)
    for t in range(2):
        at = iota + jnp.asarray(16 * t, BF16)
        x0, x1 = bx == at, bx1 == at
        for part in range(2):
            first = 32 * part + 16 * t
            x_ref[first : first + 16, lanes] = jnp.where(x0, x_near[part], jnp.where(x1, x_far[part], zero))
    over = jnp.where(cz == 127.0, fz, 0.0)
    over0, over1 = over * (1.0 - fy), over * fy
    last = [zero, zero]
    for c in range(4):
        w0, w1 = split_tile(v[c] * over0), split_tile(v[c] * over1)
        for part in range(2):
            first = 80 * part + 16 * c
            c_ref[first : first + 16, lanes] = jnp.where(y0, w0[part], jnp.where(y1, w1[part], zero))
            last[part] = jnp.where(iota == c, w1[part], last[part])
    for part in range(2):
        c_ref[80 * part + 64 : 80 * part + 80, lanes] = jnp.where(by == 15, last[part], zero)


ROW_DIMS = (((1,), (1,)), ((), ()))


def rows_by_rows(left, right):
    return lax.dot_general(left, right, ROW_DIMS, preferred_element_type=F32)


def multiply_outside(piece, a_ref, b_ref, c_ref, x_ref, acc_ref, ov_ref):
    if piece == 0:
        acc_ref[0:352, 0:256] += rows_by_rows(a_ref[0:352, :], b_ref[0:256, :])
    elif piece == 1:
        acc_ref[0:352, 256:512] += rows_by_rows(a_ref[0:352, :], b_ref[256:512, :])
    elif piece == 2:
        acc_ref[256:304, :] += rows_by_rows(a_ref[256:304, :], b_ref[512:1024, :])
    else:
        ov_ref[:, 0:64] += rows_by_rows(c_ref[...], x_ref[...])


def splat_outside(d_ref, acc_ref, ov_ref, tiles):
    acc_ref[...] = jnp.zeros_like(acc_ref)
    ov_ref[...] = jnp.zeros_like(ov_ref)
    blocks = POINTS // WIDE
    for block in range(blocks):
        build_block(d_ref, 0, block, *tiles[0])
    for group in range(GROUPS):
        for piece in range(4):
            if group + 1 < GROUPS and piece < blocks:
                build_block(d_ref, group + 1, piece, *tiles[group + 1])
            multiply_outside(piece, *tiles[group], acc_ref, ov_ref)


def splat_inside(acc_ref, tiles):
    for a_ref, b_ref, _, _ in tiles:
        acc_ref[352:608, :] += rows_by_rows(a_ref[352:608, :], b_ref[0:512, :])
        acc_ref[0:256, :] += rows_by_rows(a_ref[0:256, :], b_ref[512:1024, :])


def interpolation_tables(d_ref, r_ref, w_ref):
    iota = tile_iota()
    iota_f = iota.astype(F32)
    zero = jnp.zeros((16, WIDE), BF16)

    @pl.loop(0, GROUPS)
    def _(group):
        r_ref[group, 400:512, :] = jnp.zeros((112, POINTS), BF16)
        for block in range(POINTS // WIDE):
            lanes = slice(block * WIDE, (block + 1) * WIDE)
            fx, fy, fz, cx, cy, cz = lane_rows(d_ref, group, block, range(4, 10), 16)
            bz, bz1 = cz.astype(BF16), (cz + 1.0).astype(BF16)
            g0, g1 = split(1.0 - fz), split(fz)
            for t in range(8):
                at = iota + jnp.asarray(16 * t, BF16)
                z0, z1 = bz == at, bz1 == at
                high, low = [jnp.where(z0, g0[part], jnp.where(z1, g1[part], zero)) for part in range(2)]
                r_ref[group, 16 * t : 16 * t + 16, lanes] = high
                r_ref[group, 128 + 16 * t : 144 + 16 * t, lanes] = high
                r_ref[group, 256 + 16 * t : 272 + 16 * t, lanes] = low
            picked = jnp.where(iota <= 1, g1[0], jnp.where(iota == 2, g1[1], zero))
            r_ref[group, 384:400, lanes] = jnp.where(bz == 127, picked, zero)
            hat_y = jnp.where(cy == iota_f, 1.0 - fy, jnp.where(cy + 1.0 == iota_f, fy, 0.0))
            near, far = (1.0 - fx) * hat_y, fx * hat_y
            for x in range(17):
                w_ref[group, 16 * x : 16 * x + 16, lanes] = jnp.where(cx == x, near, jnp.where(cx == x - 1, far, 0.0))
            edge = jnp.where(cy == 15.0, fy, 0.0)
            for t in range(2):
                at = iota_f + 16.0 * t
                hat = jnp.where(cx == at, 1.0 - fx, jnp.where(cx + 1.0 == at, fx, 0.0))
                w_ref[group, 272 + 16 * t : 288 + 16 * t, lanes] = hat * edge


def weighted(g, w_ref, group, first):
    rows = g.shape[0]
    total = g[0:8] * w_ref[group, first : first + 8]
    for i in range(1, rows // 8):
        total = total + g[8 * i : 8 * i + 8] * w_ref[group, first + 8 * i : first + 8 * i + 8]
    return total


def high_and_low(l_ref, first, value):
    rows = pl.ds(first, value.shape[0])
    high, low = split(value)
    l_ref[rows, 0:128] = high
    l_ref[rows, 128:256] = low
    l_ref[rows, 256:384] = high


def interpolate_inside(u_ref, part_ref, l_ref, r_ref, w_ref):
    high_and_low(l_ref, 0, u_ref[...].reshape(256, 128))

    @pl.loop(0, GROUPS, step=4)
    def _(first):
        for step in range(4):
            group = first + step
            g = jnp.dot(l_ref[0:256, 0:384], r_ref[group, 0:384], preferred_element_type=F32)
            part_ref[group] = weighted(g, w_ref, group, 0)


def interpolate(halo_ref, uz_ref, part_ref, out_ref, l_ref, r_ref, w_ref):
    high_and_low(l_ref, 256, halo_ref[...])
    top = jnp.broadcast_to(uz_ref[:, 0:1], (ROWS, 128))
    high = top.astype(BF16).astype(F32)
    lane = lax.broadcasted_iota(jnp.int32, (ROWS, 128), 1)
    low = jnp.where(lane == 1, top - high, 0.0)
    l_ref[:, 384:512] = jnp.where(jnp.logical_or(lane == 0, lane == 2), high, low).astype(BF16)

    @pl.loop(0, GROUPS, step=4)
    def _(first):
        for step in range(4):
            group = first + step
            g = jnp.dot(l_ref[256:ROWS, :], r_ref[group], preferred_element_type=F32)
            total = part_ref[group] + weighted(g, w_ref, group, 256)
            g = jnp.dot(l_ref[0:256, 384:512], r_ref[group, 384:512], preferred_element_type=F32)
            value = jnp.sum(total + weighted(g, w_ref, group, 0), axis=0, keepdims=True)
            count = POINTS // DEVICES
            for q in range(count):
                out_ref[pl.ds(group * count + q, 1), :] = value[:, q * DEVICES : (q + 1) * DEVICES]


FACES = [(1, 0, 0), (0, 1, 0), (0, 0, 1)]
UPPER = FACES + [(1, 1, 0), (1, 0, 1), (0, 1, 1), (1, 1, 1)]


def roll_to(tile, source, target):
    shift = (target - source) % 128
    return pltpu.roll(tile, shift, 1) if shift else tile


def grid_iotas():
    lane = lax.broadcasted_iota(jnp.int32, (8, 128), 1)
    sub = lax.broadcasted_iota(jnp.int32, (8, 128), 0)
    return lane, sub


def pack(read, source):
    lane, _ = grid_iotas()
    packed = jnp.zeros((8, 128), F32)
    for i in range(32):
        packed = jnp.where(lane == i, roll_to(read(i), source, i), packed)
    return packed


def slab_star(comb, along_x, along_y, along_z, rows, tiles):
    n = along_y.shape[0]
    total = comb(along_x[0:n], along_x[2 : n + 2])
    sub3 = lax.broadcasted_iota(jnp.int32, (n, 8, 128), 1)
    down = pltpu.roll(along_y.reshape(2 * n, 8, 128), 1, 1).reshape(n, 2, 8, 128)
    up = pltpu.roll(along_y.reshape(2 * n, 8, 128), 7, 1).reshape(n, 2, 8, 128)
    edge = [jnp.stack([rows(side, i) for i in range(n)]) for side in range(2)]
    first, last = sub3 == 0, sub3 == 7
    low = jnp.stack([jnp.where(first, edge[0], down[:, 0]), jnp.where(first, down[:, 0], down[:, 1])], axis=1)
    high = jnp.stack([jnp.where(last, up[:, 1], up[:, 0]), jnp.where(last, edge[1], up[:, 1])], axis=1)
    total = total + comb(low, high)
    lanes = lax.broadcasted_iota(jnp.int32, (2 * n, 8, 128), 2)
    flat = along_z.reshape(16 * n, 128)
    sides = []
    for side, shift, at in ((0, 1, 0), (1, 127, 127)):
        edge = jnp.stack([tiles(side, i, t) for i in range(n) for t in range(2)])
        sides.append(jnp.where(lanes == at, edge, pltpu.roll(flat, shift, 1).reshape(2 * n, 8, 128)))
    return total + comb(*sides).reshape(n, 2, 8, 128)


def own_star(comb, along_x, along_y, along_z):
    nothing = jnp.zeros((8, 128), F32)
    end_slab = jnp.zeros((1, 2, 8, 128), F32)
    wide = jnp.concatenate([end_slab, along_x, end_slab], axis=0)
    return slab_star(comb, wide, along_y, along_z, lambda side, i: nothing, lambda side, i, t: nothing)


def add_outside(total, low_sign, x_low, x_high, rows, tiles):
    sub3 = lax.broadcasted_iota(jnp.int32, (16, 8, 128), 1)
    lanes = lax.broadcasted_iota(jnp.int32, (32, 8, 128), 2)
    edge = [jnp.stack([rows(side, i + 1) for i in range(16)]) for side in range(2)]
    along_y = jnp.stack([jnp.where(sub3 == 0, low_sign * edge[0], 0.0), jnp.where(sub3 == 7, edge[1], 0.0)], axis=1)
    edge = [jnp.stack([tiles(side, i + 1, t) for i in range(16) for t in range(2)]) for side in range(2)]
    along_z = jnp.where(lanes == 0, low_sign * edge[0], jnp.where(lanes == 127, edge[1], 0.0))
    total = total + (along_y + along_z.reshape(16, 2, 8, 128))
    return jnp.concatenate(
        [total[0:1] + low_sign * x_low[None], total[1:15], total[15:16] + x_high[None]], axis=0
    )


def layer_star_y(comb, side, fx, fy, fz):
    row = lax.broadcasted_iota(jnp.int32, (16, 128), 0)
    lane16 = lax.broadcasted_iota(jnp.int32, (16, 128), 1)
    plane = fx["plane"][side]
    low = jnp.where(row == 0, jnp.broadcast_to(fx["xy"][0][side], (16, 128)), pltpu.roll(plane, 1, 0))
    high = jnp.where(row == 15, jnp.broadcast_to(fx["xy"][1][side], (16, 128)), pltpu.roll(plane, 15, 0))
    total = comb(low, high)
    outer, own = fy["plane2"][side], fy["own_row"][side]
    total = total + (comb(outer, own) if side == 0 else comb(own, outer))
    plane = fz["plane"][side]
    parity, source = (1, 7) if side == 0 else (0, 0)
    sides = []
    for z_side, shift, at in ((0, 1, 0), (1, 127, 127)):
        values = jnp.broadcast_to(fz["yz"][side][z_side][source : source + 1], (16, 128))
        column = jnp.sum(jnp.where(lane16 == 2 * row + parity, values, 0.0), axis=1, keepdims=True)
        sides.append(jnp.where(lane16 == at, jnp.broadcast_to(column, (16, 128)), pltpu.roll(plane, shift, 1)))
    return total + comb(*sides)


def layer_star_z(comb, side, fx, fy, fz):
    lane, sub = grid_iotas()
    layer = fx["zp"][side]
    low = jnp.where(lane < 2, roll_to(fx["xz"][0][side], 30, 0), pltpu.roll(layer, 2, 1))
    high = jnp.where(lane >= 30, roll_to(fx["xz"][1][side], 0, 30), pltpu.roll(layer, 126, 1))
    total = comb(low, high)
    layer = fy["zp"][side]
    down, up = pltpu.roll(layer, 1, 0), pltpu.roll(layer, 7, 0)
    odd = lax.rem(lane, 2) == 1
    beyond = pltpu.roll(pltpu.roll(fy["yz"][0][side], 1, 0), 127, 1)
    low = jnp.where(sub == 0, jnp.where(odd, pltpu.roll(down, 1, 1), beyond), down)
    beyond = pltpu.roll(pltpu.roll(fy["yz"][1][side], 7, 0), 1, 1)
    high = jnp.where(sub == 7, jnp.where(odd, beyond, pltpu.roll(up, 127, 1)), up)
    total = total + comb(low, high)
    outer, own = fz["zp2"][side], fz["own_z"][side]
    total = total + (comb(outer, own) if side == 0 else comb(own, outer))
    return jnp.where(lane < 32, total, 0.0)


def solve(
    sizes, here, own_rows, tables, own_values, s_ref, ov_ref, out_ref, u_ref, halo_ref, uz_ref,
    m_ref, zs_ref, sx, sy, sxy, sz,
    z5, xa, xb, ya, yb, exy, za, exz, eyz,
    pw, rw, z3, px, rx, py, py2, ry, pxy, pz, pxz, pyz, inv_ref, diag_ref, plane_ref, uzp, pre_ref,
    fx, fy, fxy, fz, s_send, s_recv, g_send, g_recv, h_send, h_recv, f_send, f_recv,
):
    lower = [here[a] > 0 for a in range(3)]
    upper = [here[a] < sizes[a] - 1 for a in range(3)]

    def present(step):
        wanted = [(upper if step[a] > 0 else lower)[a] for a in range(3) if step[a]]
        return functools.reduce(jnp.logical_and, wanted)

    def opposite(step):
        return tuple(-v for v in step)

    def message(step, source, target, send, recv):
        copy = pltpu.make_async_remote_copy(
            src_ref=source, dst_ref=target, send_sem=send, recv_sem=recv,
            device_id=tuple(here[a] + step[a] for a in range(3)), device_id_type=MESH,
        )
        return step, copy

    def start(messages):
        for step, copy in messages:
            @pl.when(present(step))
            def _(copy=copy):
                copy.start()

    def receive(messages):
        for step, copy in messages:
            @pl.when(present(opposite(step)))
            def _(copy=copy):
                copy.wait_recv()

    def drain(messages):
        for step, copy in messages:
            @pl.when(present(step))
            def _(copy=copy):
                copy.wait_send()

    lane, sub = grid_iotas()
    zero = jnp.zeros((8, 128), F32)

    def over(first):
        tile = ov_ref[pl.ds(first, 8), :] + ov_ref[pl.ds(first + 80, 8), :]
        return tile + pltpu.roll(tile, 96, 1)

    packed = zero
    rest = roll_to(over(64), 0, 32)
    for c in range(4):
        for t in range(2):
            tile = over(16 * c + 8 * t)
            at = 32 * c + 16 * t
            packed = jnp.where(jnp.logical_and(lane >= at, lane < at + 16), roll_to(tile, 0, at), packed)
            rest = jnp.where(lane == 4 * t + c, roll_to(tile, 16, 4 * t + c), rest)
    zs_ref[0] = packed
    zs_ref[1] = rest
    out_ref[...] = s_ref[256:304, :] + s_ref[304:352, :]
    sources = [out_ref.at[0:16], out_ref.at[16:32], zs_ref.at[0], out_ref.at[32:33]] + [zs_ref.at[1]] * 3
    targets = [sx, sy, sz.at[0], sxy, sz.at[1], sz.at[2], sz.at[3]]
    mass = [message(UPPER[i], sources[i], targets[i], s_send.at[i], s_recv.at[i]) for i in range(7)]
    start(mass[::-1])
    own_rows()
    for c in range(4):
        columns = slice(128 * c, 128 * c + 128)
        m_ref[c] = (s_ref[0:256, columns] + s_ref[352:608, columns]).reshape(16, 2, 8, 128)
    receive(mass)
    for c in range(4):
        columns = slice(128 * c, 128 * c + 128)
        m_ref[c, 0] += sx[:, columns].reshape(2, 8, 128)
        from_y = sy[:, columns]
        for x in range(16):
            row = from_y[x : x + 1, :] + jnp.where(lane == 0, roll_to(sz[2], 32 + x, 0), 0.0)[c : c + 1, :]
            m_ref[c, x, 0, 0:1, :] += row
        for i in range(32):
            m_ref[c, i // 2, i % 2] += jnp.where(lane == 0, roll_to(sz[0], 32 * c + 16 * (i % 2) + i // 2, 0), 0.0)
        for t in range(2):
            m_ref[c, 0, t] += jnp.where(lane == 0, roll_to(sz[1], 4 * t + c, 0), 0.0)
        corner = sxy[:, columns] + jnp.where(lane == 0, roll_to(sz[3], 48, 0), 0.0)[c : c + 1, :]
        m_ref[c, 0, 0, 0:1, :] += corner

    def end(side, depth, size):
        return size - 1 - depth if side == 0 else depth

    def toward(side):
        return 1 if side == 0 else -1

    def mesh_step(**sides):
        return tuple(toward(sides[name]) if name in sides else 0 for name in "xyz")

    def numbered(entries, send, recv):
        return [message(step, a, b, send.at[i], recv.at[i]) for i, (step, a, b) in enumerate(entries)]

    def difference(low, high):
        return high - low

    def plus(low, high):
        return low + high

    for side in range(2):
        for i, (c, depth) in enumerate(((0, 0), (2, 0), (1, 0), (3, 0), (2, 1))):
            z5[side, i] = pack(lambda k, c=c: m_ref[c, k // 2, k % 2], end(side, depth, 128))
    entries = []
    for a in range(2):
        for b in range(2):
            entries.append((mesh_step(x=a, y=b), m_ref.at[0:2, end(a, 0, 16), 1 - b, 7 - 7 * b, :], exy.at[a, b]))
            entries.append((mesh_step(x=a, z=b), z5.at[b, 0:2], exz.at[a, b]))
            entries.append((mesh_step(y=a, z=b), z5.at[b, 1:3], eyz.at[a, b]))
    for a in range(2):
        first = 14 if a == 0 else 0
        entries.append((mesh_step(x=a), m_ref.at[0, first : first + 2], xa.at[a]))
        entries.append((mesh_step(x=a), m_ref.at[1:4, end(a, 0, 16)], xb.at[a]))
        entries.append((mesh_step(y=a), m_ref.at[:, :, 1 - a, 7 - 7 * a, :], ya.at[a]))
        entries.append((mesh_step(y=a), m_ref.at[1, :, 1 - a, 6 - 5 * a, :], yb.at[a]))
        entries.append((mesh_step(z=a), z5.at[a], za.at[a]))
    ghost = numbered(entries, g_send, g_recv)
    start(ghost)
    pre_ref[...] = own_star(difference, m_ref[0], m_ref[1], m_ref[2])
    tables()
    receive(ghost)

    def tiles_of(zp, xz):
        def tiles(side, i, t):
            at = 0 if side == 0 else 127
            if i == 0:
                return roll_to(xz[0][side], 30 + t, at)
            if i == 17:
                return roll_to(xz[1][side], t, at)
            return roll_to(zp[side], 2 * (i - 1) + t, at)
        return tiles

    def rows_of(row, xy):
        def rows(side, i):
            value = xy[0][side] if i == 0 else xy[1][side] if i == 17 else row(side, i - 1)
            return jnp.broadcast_to(value, (8, 128))
        return rows

    def both(get):
        return [get(0), get(1)]

    def grid2(get):
        return [[get(a, b) for b in range(2)] for a in range(2)]

    nx = {
        "plane": both(lambda a: ya[a, 0]), "xy": grid2(lambda a, b: exy[a, b, 0:1]),
        "zp": both(lambda a: za[a, 0]), "xz": grid2(lambda a, b: exz[a, b, 0]),
    }
    ny = {
        "plane2": both(lambda a: yb[a]), "own_row": both(lambda a: m_ref[1, :, a, 7 * a, :]),
        "zp": both(lambda a: za[a, 2]), "yz": grid2(lambda a, b: eyz[a, b, 1]),
    }
    nz = {
        "plane": both(lambda a: ya[a, 2]), "yz": grid2(lambda a, b: eyz[a, b, 0]),
        "zp2": both(lambda a: za[a, 4]), "own_z": both(lambda a: z5[1 - a, 1]),
    }
    rows = rows_of(lambda side, x: ya[side, 1, x : x + 1, :], grid2(lambda a, b: exy[a, b, 1:2]))
    tiles = tiles_of(both(lambda a: za[a, 1]), grid2(lambda a, b: exz[a, b, 1]))

    def end_star(comb, a, three, along_y, along_z, rows, tiles):
        at = 17 * a
        return slab_star(
            comb, jnp.stack(three), along_y[None], along_z[None],
            lambda side, i: rows(side, at), lambda side, i, t: tiles(side, at, t),
        )

    ends = [
        end_star(difference, 0, [xa[0, 0], xa[0, 1], m_ref[0, 0]], xb[0, 0], xb[0, 1], rows, tiles),
        end_star(difference, 1, [m_ref[0, 15], xa[1, 0], xa[1, 1]], xb[1, 0], xb[1, 1], rows, tiles),
    ]
    inside = add_outside(pre_ref[...], -1.0, xa[0, 1], xa[1, 0], rows, tiles)
    source = -0.5 * jnp.concatenate([ends[0], inside, ends[1]], axis=0)

    def shift_diagonal(mass_part):
        return 6.0 + base_screen + point_screen * mass_part

    def inverse(diagonal, exists):
        return jnp.where(exists, 1.0 / diagonal, 0.0)

    slabs = shift_diagonal(jnp.concatenate([xb[0, 2:3], m_ref[3], xb[1, 2:3]], axis=0))
    diag_ref[...] = slabs
    inv_ref[0] = inverse(slabs[0], lower[0])
    inv_ref[1:17] = 1.0 / slabs[1:17]
    inv_ref[17] = inverse(slabs[17], upper[0])
    exists = lambda axis, side: (lower, upper)[side][axis]
    diag_y = both(lambda a: shift_diagonal(ya[a, 3]))
    inv_y = both(lambda a: inverse(diag_y[a], exists(1, a)))
    diag_z = both(lambda a: shift_diagonal(za[a, 3]))
    inv_z = both(lambda a: inverse(diag_z[a], exists(2, a)))

    def second_sweep(round_index, slabs, planes, layers, residual, keep, push):
        for side in range(2):
            plane_ref[round_index, side] = planes[side]
        own = slabs[1:17]
        around = slab_star(
            plus, slabs, own, own,
            lambda side, i: jnp.broadcast_to(plane_ref[round_index, side, i : i + 1, :], (8, 128)),
            lambda side, i, t: roll_to(layers[side], 2 * i + t, 0 if side == 0 else 127),
        )
        residual = residual - (diag_ref[1:17] * own - around)
        return residual, keep * own + push * (residual * inv_ref[1:17])

    factors = sweep_factors()
    slabs = source * inv_ref[...]
    planes = both(lambda a: -0.5 * layer_star_y(difference, a, nx, ny, nz) * inv_y[a])
    layers = both(lambda a: -0.5 * layer_star_z(difference, a, nx, ny, nz) * inv_z[a])
    u_ref[...] = slabs[1:17]
    residual, following = second_sweep(0, slabs, planes, layers, source[1:17], *factors[0])

    rounds = []
    for e in range(2):
        pw[e] = following
        rw[e] = residual
        for side in range(2):
            for i, (ref, depth) in enumerate(((pw, 0), (pw, 1), (rw, 0))):
                z3[e, side, i] = pack(lambda k, ref=ref: ref[e, k // 2, k % 2], end(side, depth, 128))
        entries = []
        for a in range(2):
            for b in range(2):
                row = pw.at[e, end(a, 0, 16), 1 - b, 7 - 7 * b : 8 - 7 * b, :]
                entries.append((mesh_step(x=a, y=b), row, pxy.at[e, a, b]))
                entries.append((mesh_step(x=a, z=b), z3.at[e, b, 0], pxz.at[e, a, b]))
                entries.append((mesh_step(y=a, z=b), z3.at[e, b, 0], pyz.at[e, a, b]))
        for a in range(2):
            first = 14 if a == 0 else 0
            entries.append((mesh_step(x=a), pw.at[e, first : first + 2], px.at[e, a]))
            entries.append((mesh_step(x=a), rw.at[e, end(a, 0, 16)], rx.at[e, a]))
            entries.append((mesh_step(y=a), pw.at[e, :, 1 - a, 7 - 7 * a, :], py.at[e, a]))
            entries.append((mesh_step(y=a), pw.at[e, :, 1 - a, 6 - 5 * a, :], py2.at[e, a]))
            entries.append((mesh_step(y=a), rw.at[e, :, 1 - a, 7 - 7 * a, :], ry.at[e, a]))
            entries.append((mesh_step(z=a), z3.at[e, a], pz.at[e, a]))
        ghosts = numbered(entries, h_send.at[e], h_recv.at[e])
        rounds.append(ghosts)
        start(ghosts)
        u_ref[...] += following
        own = pw[e]
        pre_ref[...] = rw[e] - (diag_ref[1:17] * own - own_star(plus, own, own, own))
        receive(ghosts)
        p = {
            "plane": both(lambda a: py[e, a]), "plane2": both(lambda a: py2[e, a]),
            "own_row": both(lambda a: pw[e, :, a, 7 * a, :]), "xy": grid2(lambda a, b: pxy[e, a, b]),
            "zp": both(lambda a: pz[e, a, 0]), "zp2": both(lambda a: pz[e, a, 1]),
            "own_z": both(lambda a: z3[e, 1 - a, 0]),
            "xz": grid2(lambda a, b: pxz[e, a, b]), "yz": grid2(lambda a, b: pyz[e, a, b]),
        }
        rows = rows_of(lambda side, x: py[e, side, x : x + 1, :], p["xy"])
        tiles = tiles_of(p["zp"], p["xz"])
        inside = add_outside(pre_ref[...], 1.0, px[e, 0, 1], px[e, 1, 0], rows, tiles)
        ends = []
        for a, three in enumerate(([px[e, 0, 0], px[e, 0, 1], pw[e, 0]], [pw[e, 15], px[e, 1, 0], px[e, 1, 1]])):
            around = end_star(plus, a, three, three[1], three[1], rows, tiles)
            ends.append(rx[e, a][None] - (diag_ref[17 * a][None] * three[1][None] - around))
        middle = jnp.concatenate([px[e, 0, 1][None], pw[e], px[e, 1, 0][None]], axis=0)
        residual = jnp.concatenate([ends[0], inside, ends[1]], axis=0)
        keep, push = factors[2 * e + 1]
        slabs = keep * middle + push * (residual * inv_ref[...])

        def outside(own, rest, diagonal, inverse_diagonal, star):
            rest = rest - (diagonal * own - star)
            return keep * own + push * (rest * inverse_diagonal)

        planes = both(lambda a: outside(p["plane"][a], ry[e, a], diag_y[a], inv_y[a], layer_star_y(plus, a, p, p, p)))
        layers = both(lambda a: outside(p["zp"][a], pz[e, a, 2], diag_z[a], inv_z[a], layer_star_z(plus, a, p, p, p)))
        u_ref[...] += slabs[1:17]
        residual, following = second_sweep(e + 1, slabs, planes, layers, residual[1:17], *factors[2 * e + 2])
    u_ref[...] += following

    uzp[...] = pack(lambda i: u_ref[i // 2, i % 2], 0)
    sources = [u_ref.at[0], u_ref.at[:, 0, 0, :], uzp, u_ref.at[0, 0, 0:1]] + [uzp] * 3
    targets = [fx, fy, fz.at[0], fxy, fz.at[1], fz.at[2], fz.at[3]]
    layer = [message(opposite(UPPER[i]), sources[i], targets[i], f_send.at[i], f_recv.at[i]) for i in range(7)]
    start(layer[::-1])
    own_values()
    receive(layer)
    halo_ref[0:16] = fx[...].reshape(16, 128)
    halo_ref[16:32] = fy[...]
    halo_ref[32:40] = jnp.where(sub == 0, jnp.broadcast_to(fxy[...], (8, 128)), 0.0)
    halo_ref[40:48] = zero
    for i in range(32):
        uz_ref[8 * i : 8 * i + 8] = roll_to(fz[0], i, 0)
    for t in range(2):
        uz_ref[256 + 8 * t : 264 + 8 * t] = roll_to(fz[1], t, 0)
        picked = jnp.where(lane == 2 * (8 * t + sub), jnp.broadcast_to(fz[2, 0:1], (8, 128)), 0.0)
        column = jnp.sum(picked, axis=1, keepdims=True)
        uz_ref[272 + 8 * t : 280 + 8 * t] = jnp.broadcast_to(column, (8, 128))
    uz_ref[288:296] = jnp.where(sub == 0, fz[3], 0.0)
    uz_ref[296:304] = zero

    def finish():
        for messages in (mass, ghost, *rounds, layer):
            drain(messages)

    return finish


FIELD = (16, 2, 8, 128)
SOLVE_SHAPES = [
    (4, *FIELD), (2, 8, 128), (16, 512), (16, 512), (1, 512), (4, 8, 128),
    (2, 5, 8, 128), (2, 2, 2, 8, 128), (2, 3, 2, 8, 128), (2, 4, 16, 128), (2, 16, 128), (2, 2, 2, 128),
    (2, 5, 8, 128), (2, 2, 2, 8, 128), (2, 2, 2, 8, 128),
    (2, *FIELD), (2, *FIELD), (2, 2, 3, 8, 128), (2, 2, 2, 2, 8, 128), (2, 2, 2, 8, 128),
    (2, 2, 16, 128), (2, 2, 16, 128), (2, 2, 16, 128), (2, 2, 2, 1, 128), (2, 2, 3, 8, 128),
    (2, 2, 2, 8, 128), (2, 2, 2, 8, 128), (18, 2, 8, 128), (18, 2, 8, 128), (3, 2, 16, 128), (8, 128), FIELD,
    (2, 8, 128), (16, 128), (1, 128), (4, 8, 128),
]
LANDING = [2, 3, 4, 5, 7, 8, 9, 10, 11, 12, 13, 14, 18, 19, 20, 21, 22, 23, 24, 25, 26, 32, 33, 34, 35]


def kernel(sizes, data_hbm, cells_hbm, counts_hbm, u_ref, out_ref, *scratch):
    tiles, scratch = [scratch[i::GROUPS][:4] for i in range(GROUPS)], scratch[4 * GROUPS :]
    (data_ref, cells_ref, counts_ref, send, recv, sent, d_ref, acc_ref, ov_ref, face_ref,
     l_ref, r_ref, w_ref, part_ref, halo_ref, uz_ref, val_ref, back_send, back_recv, back_sent,
     in_sem, send_sem, recv_sem, *rest) = scratch
    here = position(sizes)
    me = (here[0] * sizes[1] + here[1]) * sizes[2] + here[2]
    for at in LANDING:
        rest[at][...] = jnp.zeros(rest[at].shape, F32)
    loads = [
        pltpu.make_async_copy(source, target, in_sem.at[i])
        for i, (source, target) in enumerate(((data_hbm, data_ref), (cells_hbm, cells_ref), (counts_hbm, counts_ref)))
    ]
    for load in loads:
        load.start()

    def meanwhile():
        for load in loads:
            load.wait()
        prepare_rows(data_ref, cells_ref, counts_ref, send)

    greet(me, meanwhile)
    exchange_rows(me, send, recv, sent, send_sem.at[0], recv_sem.at[0])
    d_ref[...] = recv[...].T[: CAP * CHANNELS].reshape(CHANNELS, CAP, DEVICES)
    splat_outside(d_ref, acc_ref, ov_ref, tiles)
    finish = solve(
        sizes, here, lambda: splat_inside(acc_ref, tiles), lambda: interpolation_tables(d_ref, r_ref, w_ref),
        lambda: interpolate_inside(u_ref, part_ref, l_ref, r_ref, w_ref),
        acc_ref, ov_ref, face_ref, u_ref, halo_ref, uz_ref, *rest,
    )
    interpolate(halo_ref, uz_ref, part_ref, val_ref, l_ref, r_ref, w_ref)
    padded = jnp.concatenate([val_ref[...], jnp.zeros((DEVICES - CAP, DEVICES), F32)], axis=0)
    back_send[...] = padded.T
    exchange_rows(me, back_send, back_recv, back_sent, send_sem.at[1], recv_sem.at[1])
    slot = lax.broadcasted_iota(jnp.int32, (CAP, DEVICES), 0)
    out_ref[...] = jnp.where(slot < counts_ref[...], back_recv[...].T[:CAP], 0.0)
    finish()
    pltpu.make_async_copy(send, recv, send_sem.at[0]).wait()
    pltpu.make_async_copy(back_send, back_recv, send_sem.at[1]).wait()


def on_device(sizes, point_data, point_cells, send_counts):
    data = jnp.transpose(point_data[0], (1, 2, 0))
    cells = jnp.transpose(point_cells[0], (1, 2, 0))
    dma = pltpu.SemaphoreType.DMA
    tile_rows = (608, 1024, 160, 64)
    shapes = [((rows, POINTS), BF16) for rows in tile_rows for _ in range(GROUPS)] + [
        ((7, CAP, DEVICES), F32), ((3, CAP, DEVICES), jnp.int32), ((1, DEVICES), jnp.int32),
        ((DEVICES, WIDTH), F32), ((DEVICES, WIDTH), F32), ((1, WIDTH), F32), ((CHANNELS, CAP, DEVICES), F32),
        ((608, 512), F32), ((160, 128), F32), ((48, 512), F32), ((ROWS, 512), BF16),
        ((GROUPS, 512, POINTS), BF16), ((GROUPS, ROWS, POINTS), F32), ((GROUPS, 8, POINTS), F32),
        ((48, 128), F32), ((ROWS, 128), F32), ((CAP, DEVICES), F32),
        ((DEVICES, DEVICES), F32), ((DEVICES, DEVICES), F32), ((1, DEVICES), F32),
    ]
    u, returned = pl.pallas_call(
        functools.partial(kernel, sizes),
        out_shape=[jax.ShapeDtypeStruct(s, F32) for s in (FIELD, (CAP, DEVICES))],
        in_specs=[pl.BlockSpec(memory_space=pltpu.HBM)] * 3,
        out_specs=[vmem()] * 2,
        scratch_shapes=[pltpu.VMEM(*s) for s in shapes]
        + [dma((3,)), dma((2,)), dma((2,))]
        + [pltpu.VMEM(s, F32) for s in SOLVE_SHAPES]
        + [dma((7,)), dma((7,)), dma((22,)), dma((22,)), dma((2, 24)), dma((2, 24)), dma((7,)), dma((7,))],
        compiler_params=pltpu.CompilerParams(
            vmem_limit_bytes=48 * 1024 * 1024, collective_id=0, has_side_effects=True
        ),
        name="reconstruct",
    )(*[pltpu.with_memory_space_constraint(v, pltpu.HBM) for v in (data, cells, send_counts)])
    u, returned = pl.pallas_call(
        put_out,
        out_shape=[jax.ShapeDtypeStruct(s, F32) for s in (FIELD, (CAP, DEVICES))],
        in_specs=[vmem()] * 2,
        out_specs=[pl.BlockSpec(memory_space=pl.ANY)] * 2,
        scratch_shapes=[dma((2,))],
        compiler_params=pltpu.CompilerParams(vmem_limit_bytes=1024 * 1024),
        name="put_out",
    )(u, returned)
    return u.reshape(16, 16, 128), returned.T[None]


def put_out(u_ref, value_ref, u_out, value_out, sems):
    copies = [
        pltpu.make_async_copy(u_ref, u_out, sems.at[0]),
        pltpu.make_async_copy(value_ref, value_out, sems.at[1]),
    ]
    for copy in copies:
        copy.start()
    for copy in copies:
        copy.wait()


def solution(mesh):
    sizes = tuple(mesh.shape[name] for name in ("gx", "gy", "gz"))
    spread_over = ("gx", "gy", "gz")
    in_specs = (P(spread_over, None, None, None), P(spread_over, None, None, None), P(spread_over, None))
    out_specs = (P("gx", "gy", "gz"), P(spread_over, None, None))
    return jax.shard_map(
        functools.partial(on_device, sizes), mesh=mesh, in_specs=in_specs, out_specs=out_specs, check_vma=False
    )
```

```python
import functools

import jax
import jax.numpy as jnp
from jax import lax
from jax.experimental import pallas as pl
from jax.experimental.pallas import tpu as pltpu
from jax.sharding import PartitionSpec as P

MESH = pl.DeviceIdType.MESH
F32 = jnp.float32
BF16 = jnp.bfloat16

DEVICES = 128
CAP = 32
CHANNELS = 10
WIDTH = 384
POINTS = 512
ROWS = 304
ITERS = 6
GROUPS = CAP * DEVICES // POINTS

base_screen = 0.25
point_screen = 4.0


def sweep_factors():
    half_width = 6.0 / (6.0 + base_screen)
    rho_prev = half_width
    factors = []
    for _ in range(ITERS - 1):
        rho_next = 1.0 / (2.0 / half_width - rho_prev)
        factors.append((rho_next * rho_prev, 2.0 * rho_next / half_width))
        rho_prev = rho_next
    return factors


def position(sizes):
    return tuple(lax.axis_index(name) for name in ("gx", "gy", "gz"))


def vmem():
    return pl.BlockSpec(memory_space=pltpu.VMEM)


def far_first():
    def hops(offset):
        fields = (offset >> 5) & 3, (offset >> 3) & 3, offset & 3
        return sum((0, 1, 2, 1)[field] for field in fields) + 0.5 * ((offset >> 2) & 1)

    return sorted(range(1, DEVICES), key=lambda offset: (-hops(offset), offset * 37 % DEVICES))


def greet(me, meanwhile):
    barrier = pltpu.get_barrier_semaphore()
    for offset in far_first():
        pl.semaphore_signal(barrier, inc=1, device_id=me ^ offset, device_id_type=pl.DeviceIdType.LOGICAL)
    meanwhile()
    pl.semaphore_wait(barrier, DEVICES - 1)


def exchange_rows(me, send, recv, sent, send_sem, recv_sem):
    for offset in far_first():
        other = me ^ offset
        pltpu.make_async_remote_copy(
            src_ref=send.at[pl.ds(other, 1)],
            dst_ref=recv.at[pl.ds(me, 1)],
            send_sem=send_sem,
            recv_sem=recv_sem,
            device_id=other,
            device_id_type=pl.DeviceIdType.LOGICAL,
        ).start()
    pltpu.make_async_copy(send.at[pl.ds(me, 1)], recv.at[pl.ds(me, 1)], recv_sem).start()
    pltpu.make_async_copy(send.at[pl.ds(me, 1)], sent, send_sem).start()
    pltpu.make_async_copy(send, recv, recv_sem).wait()


def prepare_rows(data_ref, cells_ref, counts_ref, send):
    slot = lax.broadcasted_iota(jnp.int32, (CAP, DEVICES), 0)
    weight = jnp.where(slot < counts_ref[...], data_ref[3], 0.0)
    parts = [data_ref[c] * weight for c in range(3)] + [weight]
    parts += [data_ref[4 + c] for c in range(3)] + [cells_ref[c].astype(F32) for c in range(3)]
    parts += [jnp.zeros((WIDTH - CAP * CHANNELS, DEVICES), F32)]
    send[...] = jnp.concatenate(parts, axis=0).T


def split(value):
    high = value.astype(BF16)
    return high, (value - high.astype(F32)).astype(BF16)


WIDE = 256


def tile(value):
    return jnp.concatenate([value, value], axis=0).astype(BF16)


def split_tile(value):
    high = tile(value)
    return high, tile(value - high[0:8].astype(F32))


def lane_rows(d_ref, group, block, channels, rows):
    first = (group * POINTS + block * WIDE) // DEVICES
    wide = lambda c, q: jnp.broadcast_to(d_ref[c, pl.ds(first + q, 1), :], (rows, DEVICES))
    return [jnp.concatenate([wide(c, q) for q in range(WIDE // DEVICES)], axis=1) for c in channels]


def tile_iota():
    return lax.broadcasted_iota(jnp.int32, (16, WIDE), 0).astype(F32).astype(BF16)


def build_block(d_ref, group, block, a_ref, b_ref, c_ref, x_ref):
    iota = tile_iota()
    zero = jnp.zeros((16, WIDE), BF16)
    lanes = slice(block * WIDE, (block + 1) * WIDE)
    v = lane_rows(d_ref, group, block, range(4), 8)
    fx, fy, fz, cx, cy, cz = lane_rows(d_ref, group, block, range(4, 10), 8)
    bz = tile(cz)
    bz1 = tile(cz + 1.0)
    g0 = [split_tile(v[c] * (1.0 - fz)) for c in range(4)]
    g1 = [split_tile(v[c] * fz) for c in range(4)]
    for t in range(8):
        at = iota + jnp.asarray(16 * t, BF16)
        z0, z1 = bz == at, bz1 == at
        for c in range(4):
            for part in range(2):
                value = jnp.where(z0, g0[c][part], jnp.where(z1, g1[c][part], zero))
                b_ref[512 * part + 128 * c + 16 * t : 512 * part + 128 * c + 16 * t + 16, lanes] = value
    by, by1 = tile(cy), tile(cy + 1.0)
    y0, y1 = by == iota, by1 == iota
    near, far = [], []
    for along, out in ((1.0 - fx, near), (fx, far)):
        w0, w1 = split_tile(along * (1.0 - fy)), split_tile(along * fy)
        for part in range(2):
            out.append(jnp.where(y0, w0[part], jnp.where(y1, w1[part], zero)))
    bx = tile(cx)
    below = None
    for x in range(17):
        here = bx == x
        for part in range(2):
            value = near[part] if below is None else jnp.where(below, far[part], zero)
            value = jnp.where(here, near[part], zero if below is None else value)
            first = (352 * part + 16 * x) if x < 16 else 256 + 48 * part
            a_ref[first : first + 16, lanes] = value
        below = here
    bx1 = tile(cx + 1.0)
    edge = jnp.where(cy == 15.0, fy, 0.0)
    e0, e1 = split_tile((1.0 - fx) * edge), split_tile(fx * edge)
    for t in range(2):
        at = iota + jnp.asarray(16 * t, BF16)
        x0, x1 = bx == at, bx1 == at
        for part in range(2):
            first = 272 + 48 * part + 16 * t
            a_ref[first : first + 16, lanes] = jnp.where(x0, e0[part], jnp.where(x1, e1[part], zero))
    x_near, x_far = split_tile(1.0 - fx), split_tile(fx)
    for t in range(2):
        at = iota + jnp.asarray(16 * t, BF16)
        x0, x1 = bx == at, bx1 == at
        for part in range(2):
            first = 32 * part + 16 * t
            x_ref[first : first + 16, lanes] = jnp.where(x0, x_near[part], jnp.where(x1, x_far[part], zero))
    over = jnp.where(cz == 127.0, fz, 0.0)
    over0, over1 = over * (1.0 - fy), over * fy
    last = [zero, zero]
    for c in range(4):
        w0, w1 = split_tile(v[c] * over0), split_tile(v[c] * over1)
        for part in range(2):
            first = 80 * part + 16 * c
            c_ref[first : first + 16, lanes] = jnp.where(y0, w0[part], jnp.where(y1, w1[part], zero))
            last[part] = jnp.where(iota == c, w1[part], last[part])
    for part in range(2):
        c_ref[80 * part + 64 : 80 * part + 80, lanes] = jnp.where(by == 15, last[part], zero)


ROW_DIMS = (((1,), (1,)), ((), ()))


def rows_by_rows(left, right):
    return lax.dot_general(left, right, ROW_DIMS, preferred_element_type=F32)


def multiply_outside(piece, a_ref, b_ref, c_ref, x_ref, acc_ref, ov_ref):
    if piece == 0:
        acc_ref[0:352, 0:256] += rows_by_rows(a_ref[0:352, :], b_ref[0:256, :])
    elif piece == 1:
        acc_ref[0:352, 256:512] += rows_by_rows(a_ref[0:352, :], b_ref[256:512, :])
    elif piece == 2:
        acc_ref[256:304, :] += rows_by_rows(a_ref[256:304, :], b_ref[512:1024, :])
    else:
        ov_ref[:, 0:64] += rows_by_rows(c_ref[...], x_ref[...])


def splat_outside(d_ref, acc_ref, ov_ref, tiles):
    blocks = POINTS // WIDE
    for block in range(blocks):
        build_block(d_ref, 0, block, *tiles[0])
    for group in range(GROUPS):
        for piece in range(4):
            if group + 1 < GROUPS and piece < blocks:
                build_block(d_ref, group + 1, piece, *tiles[group + 1])
            multiply_outside(piece, *tiles[group], acc_ref, ov_ref)


def splat_inside(acc_ref, tiles):
    for a_ref, b_ref, _, _ in tiles:
        acc_ref[352:608, :] += rows_by_rows(a_ref[352:608, :], b_ref[0:512, :])
        acc_ref[0:256, :] += rows_by_rows(a_ref[0:256, :], b_ref[512:1024, :])


def interpolation_tables(d_ref, r_ref, w_ref):
    iota = tile_iota()
    iota_f = iota.astype(F32)
    zero = jnp.zeros((16, WIDE), BF16)

    @pl.loop(0, GROUPS)
    def _(group):
        r_ref[group, 400:512, :] = jnp.zeros((112, POINTS), BF16)
        for block in range(POINTS // WIDE):
            lanes = slice(block * WIDE, (block + 1) * WIDE)
            fx, fy, fz, cx, cy, cz = lane_rows(d_ref, group, block, range(4, 10), 16)
            bz, bz1 = cz.astype(BF16), (cz + 1.0).astype(BF16)
            g0, g1 = split(1.0 - fz), split(fz)
            for t in range(8):
                at = iota + jnp.asarray(16 * t, BF16)
                z0, z1 = bz == at, bz1 == at
                high, low = [jnp.where(z0, g0[part], jnp.where(z1, g1[part], zero)) for part in range(2)]
                r_ref[group, 16 * t : 16 * t + 16, lanes] = high
                r_ref[group, 128 + 16 * t : 144 + 16 * t, lanes] = high
                r_ref[group, 256 + 16 * t : 272 + 16 * t, lanes] = low
            picked = jnp.where(iota <= 1, g1[0], jnp.where(iota == 2, g1[1], zero))
            r_ref[group, 384:400, lanes] = jnp.where(bz == 127, picked, zero)
            hat_y = jnp.where(cy == iota_f, 1.0 - fy, jnp.where(cy + 1.0 == iota_f, fy, 0.0))
            near, far = (1.0 - fx) * hat_y, fx * hat_y
            for x in range(17):
                w_ref[group, 16 * x : 16 * x + 16, lanes] = jnp.where(cx == x, near, jnp.where(cx == x - 1, far, 0.0))
            edge = jnp.where(cy == 15.0, fy, 0.0)
            for t in range(2):
                at = iota_f + 16.0 * t
                hat = jnp.where(cx == at, 1.0 - fx, jnp.where(cx + 1.0 == at, fx, 0.0))
                w_ref[group, 272 + 16 * t : 288 + 16 * t, lanes] = hat * edge


def weighted(g, w_ref, group, first):
    rows = g.shape[0]
    total = g[0:8] * w_ref[group, first : first + 8]
    for i in range(1, rows // 8):
        total = total + g[8 * i : 8 * i + 8] * w_ref[group, first + 8 * i : first + 8 * i + 8]
    return total


def high_and_low(l_ref, first, value):
    rows = pl.ds(first, value.shape[0])
    high, low = split(value)
    l_ref[rows, 0:128] = high
    l_ref[rows, 128:256] = low
    l_ref[rows, 256:384] = high


def interpolate_inside(u_ref, part_ref, l_ref, r_ref, w_ref):
    high_and_low(l_ref, 0, u_ref[...].reshape(256, 128))

    @pl.loop(0, GROUPS, step=8)
    def _(first):
        for step in range(8):
            group = first + step
            g = jnp.dot(l_ref[0:256, 0:384], r_ref[group, 0:384], preferred_element_type=F32)
            part_ref[group] = weighted(g, w_ref, group, 0)


def interpolate(halo_ref, uz_ref, part_ref, out_ref, l_ref, r_ref, w_ref):
    high_and_low(l_ref, 256, halo_ref[...])
    top = jnp.broadcast_to(uz_ref[:, 0:1], (ROWS, 128))
    high = top.astype(BF16).astype(F32)
    lane = lax.broadcasted_iota(jnp.int32, (ROWS, 128), 1)
    low = jnp.where(lane == 1, top - high, 0.0)
    l_ref[:, 384:512] = jnp.where(jnp.logical_or(lane == 0, lane == 2), high, low).astype(BF16)

    @pl.loop(0, GROUPS, step=8)
    def _(first):
        for step in range(8):
            group = first + step
            g = jnp.dot(l_ref[256:ROWS, :], r_ref[group], preferred_element_type=F32)
            total = part_ref[group] + weighted(g, w_ref, group, 256)
            g = jnp.dot(l_ref[0:256, 384:512], r_ref[group, 384:512], preferred_element_type=F32)
            value = jnp.sum(total + weighted(g, w_ref, group, 0), axis=0, keepdims=True)
            count = POINTS // DEVICES
            for q in range(count):
                out_ref[pl.ds(group * count + q, 1), :] = value[:, q * DEVICES : (q + 1) * DEVICES]


FACES = [(1, 0, 0), (0, 1, 0), (0, 0, 1)]
UPPER = FACES + [(1, 1, 0), (1, 0, 1), (0, 1, 1), (1, 1, 1)]


def roll_to(tile, source, target):
    shift = (target - source) % 128
    return pltpu.roll(tile, shift, 1) if shift else tile


def grid_iotas():
    lane = lax.broadcasted_iota(jnp.int32, (8, 128), 1)
    sub = lax.broadcasted_iota(jnp.int32, (8, 128), 0)
    return lane, sub


def pack(read, source):
    lane, _ = grid_iotas()
    packed = jnp.zeros((8, 128), F32)
    for i in range(32):
        packed = jnp.where(lane == i, roll_to(read(i), source, i), packed)
    return packed


def slab_star(comb, along_x, along_y, along_z, rows, tiles):
    n = along_y.shape[0]
    total = comb(along_x[0:n], along_x[2 : n + 2])
    sub3 = lax.broadcasted_iota(jnp.int32, (n, 8, 128), 1)
    down = pltpu.roll(along_y.reshape(2 * n, 8, 128), 1, 1).reshape(n, 2, 8, 128)
    up = pltpu.roll(along_y.reshape(2 * n, 8, 128), 7, 1).reshape(n, 2, 8, 128)
    edge = [jnp.stack([rows(side, i) for i in range(n)]) for side in range(2)]
    first, last = sub3 == 0, sub3 == 7
    low = jnp.stack([jnp.where(first, edge[0], down[:, 0]), jnp.where(first, down[:, 0], down[:, 1])], axis=1)
    high = jnp.stack([jnp.where(last, up[:, 1], up[:, 0]), jnp.where(last, edge[1], up[:, 1])], axis=1)
    total = total + comb(low, high)
    lanes = lax.broadcasted_iota(jnp.int32, (2 * n, 8, 128), 2)
    flat = along_z.reshape(16 * n, 128)
    sides = []
    for side, shift, at in ((0, 1, 0), (1, 127, 127)):
        edge = jnp.stack([tiles(side, i, t) for i in range(n) for t in range(2)])
        sides.append(jnp.where(lanes == at, edge, pltpu.roll(flat, shift, 1).reshape(2 * n, 8, 128)))
    return total + comb(*sides).reshape(n, 2, 8, 128)


def own_star(comb, along_x, along_y, along_z):
    nothing = jnp.zeros((8, 128), F32)
    end_slab = jnp.zeros((1, 2, 8, 128), F32)
    wide = jnp.concatenate([end_slab, along_x, end_slab], axis=0)
    return slab_star(comb, wide, along_y, along_z, lambda side, i: nothing, lambda side, i, t: nothing)


def add_outside(total, low_sign, x_low, x_high, rows, tiles):
    sub3 = lax.broadcasted_iota(jnp.int32, (16, 8, 128), 1)
    lanes = lax.broadcasted_iota(jnp.int32, (32, 8, 128), 2)
    edge = [jnp.stack([rows(side, i + 1) for i in range(16)]) for side in range(2)]
    along_y = jnp.stack([jnp.where(sub3 == 0, low_sign * edge[0], 0.0), jnp.where(sub3 == 7, edge[1], 0.0)], axis=1)
    edge = [jnp.stack([tiles(side, i + 1, t) for i in range(16) for t in range(2)]) for side in range(2)]
    along_z = jnp.where(lanes == 0, low_sign * edge[0], jnp.where(lanes == 127, edge[1], 0.0))
    total = total + (along_y + along_z.reshape(16, 2, 8, 128))
    return jnp.concatenate(
        [total[0:1] + low_sign * x_low[None], total[1:15], total[15:16] + x_high[None]], axis=0
    )


def layer_star_y(comb, side, fx, fy, fz):
    row = lax.broadcasted_iota(jnp.int32, (16, 128), 0)
    lane16 = lax.broadcasted_iota(jnp.int32, (16, 128), 1)
    plane = fx["plane"][side]
    low = jnp.where(row == 0, jnp.broadcast_to(fx["xy"][0][side], (16, 128)), pltpu.roll(plane, 1, 0))
    high = jnp.where(row == 15, jnp.broadcast_to(fx["xy"][1][side], (16, 128)), pltpu.roll(plane, 15, 0))
    total = comb(low, high)
    outer, own = fy["plane2"][side], fy["own_row"][side]
    total = total + (comb(outer, own) if side == 0 else comb(own, outer))
    plane = fz["plane"][side]
    parity, source = (1, 7) if side == 0 else (0, 0)
    sides = []
    for z_side, shift, at in ((0, 1, 0), (1, 127, 127)):
        values = jnp.broadcast_to(fz["yz"][side][z_side][source : source + 1], (16, 128))
        column = jnp.sum(jnp.where(lane16 == 2 * row + parity, values, 0.0), axis=1, keepdims=True)
        sides.append(jnp.where(lane16 == at, jnp.broadcast_to(column, (16, 128)), pltpu.roll(plane, shift, 1)))
    return total + comb(*sides)


def layer_star_z(comb, side, fx, fy, fz):
    lane, sub = grid_iotas()
    layer = fx["zp"][side]
    low = jnp.where(lane < 2, roll_to(fx["xz"][0][side], 30, 0), pltpu.roll(layer, 2, 1))
    high = jnp.where(lane >= 30, roll_to(fx["xz"][1][side], 0, 30), pltpu.roll(layer, 126, 1))
    total = comb(low, high)
    layer = fy["zp"][side]
    down, up = pltpu.roll(layer, 1, 0), pltpu.roll(layer, 7, 0)
    odd = lax.rem(lane, 2) == 1
    beyond = pltpu.roll(pltpu.roll(fy["yz"][0][side], 1, 0), 127, 1)
    low = jnp.where(sub == 0, jnp.where(odd, pltpu.roll(down, 1, 1), beyond), down)
    beyond = pltpu.roll(pltpu.roll(fy["yz"][1][side], 7, 0), 1, 1)
    high = jnp.where(sub == 7, jnp.where(odd, beyond, pltpu.roll(up, 127, 1)), up)
    total = total + comb(low, high)
    outer, own = fz["zp2"][side], fz["own_z"][side]
    total = total + (comb(outer, own) if side == 0 else comb(own, outer))
    return jnp.where(lane < 32, total, 0.0)


def solve(
    sizes, here, own_rows, tables, own_values, s_ref, ov_ref, out_ref, u_ref, halo_ref, uz_ref,
    m_ref, zs_ref, sx, sy, sxy, sz,
    z5, xa, xb, ya, yb, exy, za, exz, eyz,
    pw, rw, z3, px, rx, py, py2, ry, pxy, pz, pxz, pyz, inv_ref, diag_ref, plane_ref, uzp, pre_ref,
    fx, fy, fxy, fz, s_send, s_recv, g_send, g_recv, h_send, h_recv, f_send, f_recv,
):
    lower = [here[a] > 0 for a in range(3)]
    upper = [here[a] < sizes[a] - 1 for a in range(3)]

    def present(step):
        wanted = [(upper if step[a] > 0 else lower)[a] for a in range(3) if step[a]]
        return functools.reduce(jnp.logical_and, wanted)

    def opposite(step):
        return tuple(-v for v in step)

    def message(step, source, target, send, recv):
        copy = pltpu.make_async_remote_copy(
            src_ref=source, dst_ref=target, send_sem=send, recv_sem=recv,
            device_id=tuple(here[a] + step[a] for a in range(3)), device_id_type=MESH,
        )
        return step, copy

    def start(messages):
        for step, copy in messages:
            @pl.when(present(step))
            def _(copy=copy):
                copy.start()

    def receive(messages):
        for step, copy in messages:
            @pl.when(present(opposite(step)))
            def _(copy=copy):
                copy.wait_recv()

    def drain(messages):
        for step, copy in messages:
            @pl.when(present(step))
            def _(copy=copy):
                copy.wait_send()

    lane, sub = grid_iotas()
    zero = jnp.zeros((8, 128), F32)

    def over(first):
        tile = ov_ref[pl.ds(first, 8), :] + ov_ref[pl.ds(first + 80, 8), :]
        return tile + pltpu.roll(tile, 96, 1)

    packed = zero
    rest = roll_to(over(64), 0, 32)
    for c in range(4):
        for t in range(2):
            tile = over(16 * c + 8 * t)
            at = 32 * c + 16 * t
            packed = jnp.where(jnp.logical_and(lane >= at, lane < at + 16), roll_to(tile, 0, at), packed)
            rest = jnp.where(lane == 4 * t + c, roll_to(tile, 16, 4 * t + c), rest)
    zs_ref[0] = packed
    zs_ref[1] = rest
    out_ref[...] = s_ref[256:304, :] + s_ref[304:352, :]
    sources = [out_ref.at[0:16], out_ref.at[16:32], zs_ref.at[0], out_ref.at[32:33]] + [zs_ref.at[1]] * 3
    targets = [sx, sy, sz.at[0], sxy, sz.at[1], sz.at[2], sz.at[3]]
    mass = [message(UPPER[i], sources[i], targets[i], s_send.at[i], s_recv.at[i]) for i in range(7)]
    start(mass[::-1])
    own_rows()
    for c in range(4):
        columns = slice(128 * c, 128 * c + 128)
        m_ref[c] = (s_ref[0:256, columns] + s_ref[352:608, columns]).reshape(16, 2, 8, 128)
    receive(mass)
    for c in range(4):
        columns = slice(128 * c, 128 * c + 128)
        m_ref[c, 0] += sx[:, columns].reshape(2, 8, 128)
        from_y = sy[:, columns]
        for x in range(16):
            row = from_y[x : x + 1, :] + jnp.where(lane == 0, roll_to(sz[2], 32 + x, 0), 0.0)[c : c + 1, :]
            m_ref[c, x, 0, 0:1, :] += row
        for i in range(32):
            m_ref[c, i // 2, i % 2] += jnp.where(lane == 0, roll_to(sz[0], 32 * c + 16 * (i % 2) + i // 2, 0), 0.0)
        for t in range(2):
            m_ref[c, 0, t] += jnp.where(lane == 0, roll_to(sz[1], 4 * t + c, 0), 0.0)
        corner = sxy[:, columns] + jnp.where(lane == 0, roll_to(sz[3], 48, 0), 0.0)[c : c + 1, :]
        m_ref[c, 0, 0, 0:1, :] += corner

    def end(side, depth, size):
        return size - 1 - depth if side == 0 else depth

    def toward(side):
        return 1 if side == 0 else -1

    def mesh_step(**sides):
        return tuple(toward(sides[name]) if name in sides else 0 for name in "xyz")

    def numbered(entries, send, recv):
        return [message(step, a, b, send.at[i], recv.at[i]) for i, (step, a, b) in enumerate(entries)]

    def difference(low, high):
        return high - low

    def plus(low, high):
        return low + high

    for side in range(2):
        for i, (c, depth) in enumerate(((0, 0), (2, 0), (1, 0), (3, 0), (2, 1))):
            z5[side, i] = pack(lambda k, c=c: m_ref[c, k // 2, k % 2], end(side, depth, 128))
    entries = []
    for a in range(2):
        for b in range(2):
            entries.append((mesh_step(x=a, y=b), m_ref.at[0:2, end(a, 0, 16), 1 - b, 7 - 7 * b, :], exy.at[a, b]))
            entries.append((mesh_step(x=a, z=b), z5.at[b, 0:2], exz.at[a, b]))
            entries.append((mesh_step(y=a, z=b), z5.at[b, 1:3], eyz.at[a, b]))
    for a in range(2):
        first = 14 if a == 0 else 0
        entries.append((mesh_step(x=a), m_ref.at[0, first : first + 2], xa.at[a]))
        entries.append((mesh_step(x=a), m_ref.at[1:4, end(a, 0, 16)], xb.at[a]))
        entries.append((mesh_step(y=a), m_ref.at[:, :, 1 - a, 7 - 7 * a, :], ya.at[a]))
        entries.append((mesh_step(y=a), m_ref.at[1, :, 1 - a, 6 - 5 * a, :], yb.at[a]))
        entries.append((mesh_step(z=a), z5.at[a], za.at[a]))
    ghost = numbered(entries, g_send, g_recv)
    start(ghost)
    pre_ref[...] = own_star(difference, m_ref[0], m_ref[1], m_ref[2])
    tables()
    receive(ghost)

    def tiles_of(zp, xz):
        def tiles(side, i, t):
            at = 0 if side == 0 else 127
            if i == 0:
                return roll_to(xz[0][side], 30 + t, at)
            if i == 17:
                return roll_to(xz[1][side], t, at)
            return roll_to(zp[side], 2 * (i - 1) + t, at)
        return tiles

    def rows_of(row, xy):
        def rows(side, i):
            value = xy[0][side] if i == 0 else xy[1][side] if i == 17 else row(side, i - 1)
            return jnp.broadcast_to(value, (8, 128))
        return rows

    def both(get):
        return [get(0), get(1)]

    def grid2(get):
        return [[get(a, b) for b in range(2)] for a in range(2)]

    nx = {
        "plane": both(lambda a: ya[a, 0]), "xy": grid2(lambda a, b: exy[a, b, 0:1]),
        "zp": both(lambda a: za[a, 0]), "xz": grid2(lambda a, b: exz[a, b, 0]),
    }
    ny = {
        "plane2": both(lambda a: yb[a]), "own_row": both(lambda a: m_ref[1, :, a, 7 * a, :]),
        "zp": both(lambda a: za[a, 2]), "yz": grid2(lambda a, b: eyz[a, b, 1]),
    }
    nz = {
        "plane": both(lambda a: ya[a, 2]), "yz": grid2(lambda a, b: eyz[a, b, 0]),
        "zp2": both(lambda a: za[a, 4]), "own_z": both(lambda a: z5[1 - a, 1]),
    }
    rows = rows_of(lambda side, x: ya[side, 1, x : x + 1, :], grid2(lambda a, b: exy[a, b, 1:2]))
    tiles = tiles_of(both(lambda a: za[a, 1]), grid2(lambda a, b: exz[a, b, 1]))

    def end_star(comb, a, three, along_y, along_z, rows, tiles):
        at = 17 * a
        return slab_star(
            comb, jnp.stack(three), along_y[None], along_z[None],
            lambda side, i: rows(side, at), lambda side, i, t: tiles(side, at, t),
        )

    ends = [
        end_star(difference, 0, [xa[0, 0], xa[0, 1], m_ref[0, 0]], xb[0, 0], xb[0, 1], rows, tiles),
        end_star(difference, 1, [m_ref[0, 15], xa[1, 0], xa[1, 1]], xb[1, 0], xb[1, 1], rows, tiles),
    ]
    inside = add_outside(pre_ref[...], -1.0, xa[0, 1], xa[1, 0], rows, tiles)
    source = -0.5 * jnp.concatenate([ends[0], inside, ends[1]], axis=0)

    def shift_diagonal(mass_part):
        return 6.0 + base_screen + point_screen * mass_part

    def inverse(diagonal, exists):
        return jnp.where(exists, 1.0 / diagonal, 0.0)

    slabs = shift_diagonal(jnp.concatenate([xb[0, 2:3], m_ref[3], xb[1, 2:3]], axis=0))
    diag_ref[...] = slabs
    inv_ref[0] = inverse(slabs[0], lower[0])
    inv_ref[1:17] = 1.0 / slabs[1:17]
    inv_ref[17] = inverse(slabs[17], upper[0])
    exists = lambda axis, side: (lower, upper)[side][axis]
    diag_y = both(lambda a: shift_diagonal(ya[a, 3]))
    inv_y = both(lambda a: inverse(diag_y[a], exists(1, a)))
    diag_z = both(lambda a: shift_diagonal(za[a, 3]))
    inv_z = both(lambda a: inverse(diag_z[a], exists(2, a)))

    def second_sweep(round_index, slabs, planes, layers, residual, keep, push):
        for side in range(2):
            plane_ref[round_index, side] = planes[side]
        own = slabs[1:17]
        around = slab_star(
            plus, slabs, own, own,
            lambda side, i: jnp.broadcast_to(plane_ref[round_index, side, i : i + 1, :], (8, 128)),
            lambda side, i, t: roll_to(layers[side], 2 * i + t, 0 if side == 0 else 127),
        )
        residual = residual - (diag_ref[1:17] * own - around)
        return residual, keep * own + push * (residual * inv_ref[1:17])

    factors = sweep_factors()
    slabs = source * inv_ref[...]
    planes = both(lambda a: -0.5 * layer_star_y(difference, a, nx, ny, nz) * inv_y[a])
    layers = both(lambda a: -0.5 * layer_star_z(difference, a, nx, ny, nz) * inv_z[a])
    u_ref[...] = slabs[1:17]
    residual, following = second_sweep(0, slabs, planes, layers, source[1:17], *factors[0])

    rounds = []
    for e in range(2):
        pw[e] = following
        rw[e] = residual
        for side in range(2):
            for i, (ref, depth) in enumerate(((pw, 0), (pw, 1), (rw, 0))):
                z3[e, side, i] = pack(lambda k, ref=ref: ref[e, k // 2, k % 2], end(side, depth, 128))
        entries = []
        for a in range(2):
            for b in range(2):
                row = pw.at[e, end(a, 0, 16), 1 - b, 7 - 7 * b : 8 - 7 * b, :]
                entries.append((mesh_step(x=a, y=b), row, pxy.at[e, a, b]))
                entries.append((mesh_step(x=a, z=b), z3.at[e, b, 0], pxz.at[e, a, b]))
                entries.append((mesh_step(y=a, z=b), z3.at[e, b, 0], pyz.at[e, a, b]))
        for a in range(2):
            first = 14 if a == 0 else 0
            entries.append((mesh_step(x=a), pw.at[e, first : first + 2], px.at[e, a]))
            entries.append((mesh_step(x=a), rw.at[e, end(a, 0, 16)], rx.at[e, a]))
            entries.append((mesh_step(y=a), pw.at[e, :, 1 - a, 7 - 7 * a, :], py.at[e, a]))
            entries.append((mesh_step(y=a), pw.at[e, :, 1 - a, 6 - 5 * a, :], py2.at[e, a]))
            entries.append((mesh_step(y=a), rw.at[e, :, 1 - a, 7 - 7 * a, :], ry.at[e, a]))
            entries.append((mesh_step(z=a), z3.at[e, a], pz.at[e, a]))
        ghosts = numbered(entries, h_send.at[e], h_recv.at[e])
        rounds.append(ghosts)
        start(ghosts)
        u_ref[...] += following
        own = pw[e]
        pre_ref[...] = rw[e] - (diag_ref[1:17] * own - own_star(plus, own, own, own))
        receive(ghosts)
        p = {
            "plane": both(lambda a: py[e, a]), "plane2": both(lambda a: py2[e, a]),
            "own_row": both(lambda a: pw[e, :, a, 7 * a, :]), "xy": grid2(lambda a, b: pxy[e, a, b]),
            "zp": both(lambda a: pz[e, a, 0]), "zp2": both(lambda a: pz[e, a, 1]),
            "own_z": both(lambda a: z3[e, 1 - a, 0]),
            "xz": grid2(lambda a, b: pxz[e, a, b]), "yz": grid2(lambda a, b: pyz[e, a, b]),
        }
        rows = rows_of(lambda side, x: py[e, side, x : x + 1, :], p["xy"])
        tiles = tiles_of(p["zp"], p["xz"])
        inside = add_outside(pre_ref[...], 1.0, px[e, 0, 1], px[e, 1, 0], rows, tiles)
        ends = []
        for a, three in enumerate(([px[e, 0, 0], px[e, 0, 1], pw[e, 0]], [pw[e, 15], px[e, 1, 0], px[e, 1, 1]])):
            around = end_star(plus, a, three, three[1], three[1], rows, tiles)
            ends.append(rx[e, a][None] - (diag_ref[17 * a][None] * three[1][None] - around))
        middle = jnp.concatenate([px[e, 0, 1][None], pw[e], px[e, 1, 0][None]], axis=0)
        residual = jnp.concatenate([ends[0], inside, ends[1]], axis=0)
        keep, push = factors[2 * e + 1]
        slabs = keep * middle + push * (residual * inv_ref[...])

        def outside(own, rest, diagonal, inverse_diagonal, star):
            rest = rest - (diagonal * own - star)
            return keep * own + push * (rest * inverse_diagonal)

        planes = both(lambda a: outside(p["plane"][a], ry[e, a], diag_y[a], inv_y[a], layer_star_y(plus, a, p, p, p)))
        layers = both(lambda a: outside(p["zp"][a], pz[e, a, 2], diag_z[a], inv_z[a], layer_star_z(plus, a, p, p, p)))
        u_ref[...] += slabs[1:17]
        residual, following = second_sweep(e + 1, slabs, planes, layers, residual[1:17], *factors[2 * e + 2])
    u_ref[...] += following

    uzp[...] = pack(lambda i: u_ref[i // 2, i % 2], 0)
    sources = [u_ref.at[0], u_ref.at[:, 0, 0, :], uzp, u_ref.at[0, 0, 0:1]] + [uzp] * 3
    targets = [fx, fy, fz.at[0], fxy, fz.at[1], fz.at[2], fz.at[3]]
    layer = [message(opposite(UPPER[i]), sources[i], targets[i], f_send.at[i], f_recv.at[i]) for i in range(7)]
    start(layer[::-1])
    own_values()
    receive(layer)
    halo_ref[0:16] = fx[...].reshape(16, 128)
    halo_ref[16:32] = fy[...]
    halo_ref[32:40] = jnp.where(sub == 0, jnp.broadcast_to(fxy[...], (8, 128)), 0.0)
    halo_ref[40:48] = zero
    for i in range(32):
        uz_ref[8 * i : 8 * i + 8] = roll_to(fz[0], i, 0)
    for t in range(2):
        uz_ref[256 + 8 * t : 264 + 8 * t] = roll_to(fz[1], t, 0)
        picked = jnp.where(lane == 2 * (8 * t + sub), jnp.broadcast_to(fz[2, 0:1], (8, 128)), 0.0)
        column = jnp.sum(picked, axis=1, keepdims=True)
        uz_ref[272 + 8 * t : 280 + 8 * t] = jnp.broadcast_to(column, (8, 128))
    uz_ref[288:296] = jnp.where(sub == 0, fz[3], 0.0)
    uz_ref[296:304] = zero

    def finish():
        for messages in (mass, ghost, *rounds, layer):
            drain(messages)

    return finish


FIELD = (16, 2, 8, 128)
SOLVE_SHAPES = [
    (4, *FIELD), (2, 8, 128), (16, 512), (16, 512), (1, 512), (4, 8, 128),
    (2, 5, 8, 128), (2, 2, 2, 8, 128), (2, 3, 2, 8, 128), (2, 4, 16, 128), (2, 16, 128), (2, 2, 2, 128),
    (2, 5, 8, 128), (2, 2, 2, 8, 128), (2, 2, 2, 8, 128),
    (2, *FIELD), (2, *FIELD), (2, 2, 3, 8, 128), (2, 2, 2, 2, 8, 128), (2, 2, 2, 8, 128),
    (2, 2, 16, 128), (2, 2, 16, 128), (2, 2, 16, 128), (2, 2, 2, 1, 128), (2, 2, 3, 8, 128),
    (2, 2, 2, 8, 128), (2, 2, 2, 8, 128), (18, 2, 8, 128), (18, 2, 8, 128), (3, 2, 16, 128), (8, 128), FIELD,
    (2, 8, 128), (16, 128), (1, 128), (4, 8, 128),
]
LANDING = [2, 3, 4, 5, 7, 8, 9, 10, 11, 12, 13, 14, 18, 19, 20, 21, 22, 23, 24, 25, 26, 32, 33, 34, 35]


def kernel(sizes, data_hbm, cells_hbm, counts_hbm, u_ref, out_ref, *scratch):
    tiles, scratch = [scratch[i::GROUPS][:4] for i in range(GROUPS)], scratch[4 * GROUPS :]
    (data_ref, cells_ref, counts_ref, send, recv, sent, d_ref, acc_ref, ov_ref, face_ref,
     l_ref, r_ref, w_ref, part_ref, halo_ref, uz_ref, val_ref, back_send, back_recv, back_sent,
     in_sem, send_sem, recv_sem, *rest) = scratch
    here = position(sizes)
    me = (here[0] * sizes[1] + here[1]) * sizes[2] + here[2]
    for at in LANDING:
        rest[at][...] = jnp.zeros(rest[at].shape, F32)
    loads = [
        pltpu.make_async_copy(source, target, in_sem.at[i])
        for i, (source, target) in enumerate(((data_hbm, data_ref), (cells_hbm, cells_ref), (counts_hbm, counts_ref)))
    ]
    for load in loads:
        load.start()

    def meanwhile():
        for load in loads:
            load.wait()
        prepare_rows(data_ref, cells_ref, counts_ref, send)
        acc_ref[...] = jnp.zeros_like(acc_ref)
        ov_ref[...] = jnp.zeros_like(ov_ref)

    greet(me, meanwhile)
    exchange_rows(me, send, recv, sent, send_sem.at[0], recv_sem.at[0])
    d_ref[...] = recv[...].T[: CAP * CHANNELS].reshape(CHANNELS, CAP, DEVICES)
    splat_outside(d_ref, acc_ref, ov_ref, tiles)
    finish = solve(
        sizes, here, lambda: splat_inside(acc_ref, tiles), lambda: interpolation_tables(d_ref, r_ref, w_ref),
        lambda: interpolate_inside(u_ref, part_ref, l_ref, r_ref, w_ref),
        acc_ref, ov_ref, face_ref, u_ref, halo_ref, uz_ref, *rest,
    )
    interpolate(halo_ref, uz_ref, part_ref, val_ref, l_ref, r_ref, w_ref)
    padded = jnp.concatenate([val_ref[...], jnp.zeros((DEVICES - CAP, DEVICES), F32)], axis=0)
    back_send[...] = padded.T
    exchange_rows(me, back_send, back_recv, back_sent, send_sem.at[1], recv_sem.at[1])
    slot = lax.broadcasted_iota(jnp.int32, (CAP, DEVICES), 0)
    out_ref[...] = jnp.where(slot < counts_ref[...], back_recv[...].T[:CAP], 0.0)
    finish()
    pltpu.make_async_copy(send, recv, send_sem.at[0]).wait()
    pltpu.make_async_copy(back_send, back_recv, send_sem.at[1]).wait()


def on_device(sizes, point_data, point_cells, send_counts):
    data = jnp.transpose(point_data[0], (1, 2, 0))
    cells = jnp.transpose(point_cells[0], (1, 2, 0))
    dma = pltpu.SemaphoreType.DMA
    tile_rows = (608, 1024, 160, 64)
    shapes = [((rows, POINTS), BF16) for rows in tile_rows for _ in range(GROUPS)] + [
        ((7, CAP, DEVICES), F32), ((3, CAP, DEVICES), jnp.int32), ((1, DEVICES), jnp.int32),
        ((DEVICES, WIDTH), F32), ((DEVICES, WIDTH), F32), ((1, WIDTH), F32), ((CHANNELS, CAP, DEVICES), F32),
        ((608, 512), F32), ((160, 128), F32), ((48, 512), F32), ((ROWS, 512), BF16),
        ((GROUPS, 512, POINTS), BF16), ((GROUPS, ROWS, POINTS), F32), ((GROUPS, 8, POINTS), F32),
        ((48, 128), F32), ((ROWS, 128), F32), ((CAP, DEVICES), F32),
        ((DEVICES, DEVICES), F32), ((DEVICES, DEVICES), F32), ((1, DEVICES), F32),
    ]
    u, returned = pl.pallas_call(
        functools.partial(kernel, sizes),
        out_shape=[jax.ShapeDtypeStruct(s, F32) for s in (FIELD, (CAP, DEVICES))],
        in_specs=[pl.BlockSpec(memory_space=pltpu.HBM)] * 3,
        out_specs=[vmem()] * 2,
        scratch_shapes=[pltpu.VMEM(*s) for s in shapes]
        + [dma((3,)), dma((2,)), dma((2,))]
        + [pltpu.VMEM(s, F32) for s in SOLVE_SHAPES]
        + [dma((7,)), dma((7,)), dma((22,)), dma((22,)), dma((2, 24)), dma((2, 24)), dma((7,)), dma((7,))],
        compiler_params=pltpu.CompilerParams(
            vmem_limit_bytes=48 * 1024 * 1024, collective_id=0, has_side_effects=True
        ),
        name="reconstruct",
    )(*[pltpu.with_memory_space_constraint(v, pltpu.HBM) for v in (data, cells, send_counts)])
    u, returned = pl.pallas_call(
        put_out,
        out_shape=[jax.ShapeDtypeStruct(s, F32) for s in (FIELD, (CAP, DEVICES))],
        in_specs=[vmem()] * 2,
        out_specs=[pl.BlockSpec(memory_space=pl.ANY)] * 2,
        scratch_shapes=[dma((2,))],
        compiler_params=pltpu.CompilerParams(vmem_limit_bytes=1024 * 1024),
        name="put_out",
    )(u, returned)
    return u.reshape(16, 16, 128), returned.T[None]


def put_out(u_ref, value_ref, u_out, value_out, sems):
    copies = [
        pltpu.make_async_copy(u_ref, u_out, sems.at[0]),
        pltpu.make_async_copy(value_ref, value_out, sems.at[1]),
    ]
    for copy in copies:
        copy.start()
    for copy in copies:
        copy.wait()


def solution(mesh):
    sizes = tuple(mesh.shape[name] for name in ("gx", "gy", "gz"))
    spread_over = ("gx", "gy", "gz")
    in_specs = (P(spread_over, None, None, None), P(spread_over, None, None, None), P(spread_over, None))
    out_specs = (P("gx", "gy", "gz"), P(spread_over, None, None))
    return jax.shard_map(
        functools.partial(on_device, sizes), mesh=mesh, in_specs=in_specs, out_specs=out_specs, check_vma=False
    )
```

```python
import functools

import jax
import jax.numpy as jnp
from jax import lax
from jax.experimental import pallas as pl
from jax.experimental.pallas import tpu as pltpu
from jax.sharding import PartitionSpec as P

MESH = pl.DeviceIdType.MESH
F32 = jnp.float32
BF16 = jnp.bfloat16

DEVICES = 128
CAP = 32
CHANNELS = 10
WIDTH = 384
POINTS = 512
ROWS = 304
ITERS = 6
GROUPS = CAP * DEVICES // POINTS

base_screen = 0.25
point_screen = 4.0


def sweep_factors():
    half_width = 6.0 / (6.0 + base_screen)
    rho_prev = half_width
    factors = []
    for _ in range(ITERS - 1):
        rho_next = 1.0 / (2.0 / half_width - rho_prev)
        factors.append((rho_next * rho_prev, 2.0 * rho_next / half_width))
        rho_prev = rho_next
    return factors


def position(sizes):
    return tuple(lax.axis_index(name) for name in ("gx", "gy", "gz"))


def vmem():
    return pl.BlockSpec(memory_space=pltpu.VMEM)


def far_first():
    def hops(offset):
        fields = (offset >> 5) & 3, (offset >> 3) & 3, offset & 3
        return sum((0, 1, 2, 1)[field] for field in fields) + 0.5 * ((offset >> 2) & 1)

    return sorted(range(1, DEVICES), key=lambda offset: (-hops(offset), offset * 37 % DEVICES))


def greet(me, meanwhile):
    barrier = pltpu.get_barrier_semaphore()
    for offset in far_first():
        pl.semaphore_signal(barrier, inc=1, device_id=me ^ offset, device_id_type=pl.DeviceIdType.LOGICAL)
    meanwhile()
    pl.semaphore_wait(barrier, DEVICES - 1)


def exchange_rows(me, send, recv, sent, send_sem, recv_sem):
    for offset in far_first():
        other = me ^ offset
        pltpu.make_async_remote_copy(
            src_ref=send.at[pl.ds(other, 1)],
            dst_ref=recv.at[pl.ds(me, 1)],
            send_sem=send_sem,
            recv_sem=recv_sem,
            device_id=other,
            device_id_type=pl.DeviceIdType.LOGICAL,
        ).start()
    pltpu.make_async_copy(send.at[pl.ds(me, 1)], recv.at[pl.ds(me, 1)], recv_sem).start()
    pltpu.make_async_copy(send.at[pl.ds(me, 1)], sent, send_sem).start()
    pltpu.make_async_copy(send, recv, recv_sem).wait()


def prepare_rows(data_ref, cells_ref, counts_ref, send):
    slot = lax.broadcasted_iota(jnp.int32, (CAP, DEVICES), 0)
    weight = jnp.where(slot < counts_ref[...], data_ref[3], 0.0)
    parts = [data_ref[c] * weight for c in range(3)] + [weight]
    parts += [data_ref[4 + c] for c in range(3)] + [cells_ref[c].astype(F32) for c in range(3)]
    parts += [jnp.zeros((WIDTH - CAP * CHANNELS, DEVICES), F32)]
    send[...] = jnp.concatenate(parts, axis=0).T


def split(value):
    high = value.astype(BF16)
    return high, (value - high.astype(F32)).astype(BF16)


WIDE = 256


def tile(value):
    return jnp.concatenate([value, value], axis=0).astype(BF16)


def split_tile(value):
    high = tile(value)
    return high, tile(value - high[0:8].astype(F32))


def lane_rows(d_ref, group, block, channels, rows):
    first = (group * POINTS + block * WIDE) // DEVICES
    wide = lambda c, q: jnp.broadcast_to(d_ref[c, pl.ds(first + q, 1), :], (rows, DEVICES))
    return [jnp.concatenate([wide(c, q) for q in range(WIDE // DEVICES)], axis=1) for c in channels]


def tile_iota():
    return lax.broadcasted_iota(jnp.int32, (16, WIDE), 0).astype(F32).astype(BF16)


def build_block(d_ref, group, block, a_ref, b_ref, c_ref, x_ref):
    iota = tile_iota()
    zero = jnp.zeros((16, WIDE), BF16)
    lanes = slice(block * WIDE, (block + 1) * WIDE)
    v = lane_rows(d_ref, group, block, range(4), 8)
    fx, fy, fz, cx, cy, cz = lane_rows(d_ref, group, block, range(4, 10), 8)
    bz = tile(cz)
    bz1 = tile(cz + 1.0)
    g0 = [split_tile(v[c] * (1.0 - fz)) for c in range(4)]
    g1 = [split_tile(v[c] * fz) for c in range(4)]
    for t in range(8):
        at = iota + jnp.asarray(16 * t, BF16)
        z0, z1 = bz == at, bz1 == at
        for c in range(4):
            for part in range(2):
                value = jnp.where(z0, g0[c][part], jnp.where(z1, g1[c][part], zero))
                b_ref[512 * part + 128 * c + 16 * t : 512 * part + 128 * c + 16 * t + 16, lanes] = value
    by, by1 = tile(cy), tile(cy + 1.0)
    y0, y1 = by == iota, by1 == iota
    near, far = [], []
    for along, out in ((1.0 - fx, near), (fx, far)):
        w0, w1 = split_tile(along * (1.0 - fy)), split_tile(along * fy)
        for part in range(2):
            out.append(jnp.where(y0, w0[part], jnp.where(y1, w1[part], zero)))
    bx = tile(cx)
    below = None
    for x in range(17):
        here = bx == x
        for part in range(2):
            value = near[part] if below is None else jnp.where(below, far[part], zero)
            value = jnp.where(here, near[part], zero if below is None else value)
            first = (352 * part + 16 * x) if x < 16 else 256 + 48 * part
            a_ref[first : first + 16, lanes] = value
        below = here
    bx1 = tile(cx + 1.0)
    edge = jnp.where(cy == 15.0, fy, 0.0)
    e0, e1 = split_tile((1.0 - fx) * edge), split_tile(fx * edge)
    for t in range(2):
        at = iota + jnp.asarray(16 * t, BF16)
        x0, x1 = bx == at, bx1 == at
        for part in range(2):
            first = 272 + 48 * part + 16 * t
            a_ref[first : first + 16, lanes] = jnp.where(x0, e0[part], jnp.where(x1, e1[part], zero))
    x_near, x_far = split_tile(1.0 - fx), split_tile(fx)
    for t in range(2):
        at = iota + jnp.asarray(16 * t, BF16)
        x0, x1 = bx == at, bx1 == at
        for part in range(2):
            first = 32 * part + 16 * t
            x_ref[first : first + 16, lanes] = jnp.where(x0, x_near[part], jnp.where(x1, x_far[part], zero))
    over = jnp.where(cz == 127.0, fz, 0.0)
    over0, over1 = over * (1.0 - fy), over * fy
    last = [zero, zero]
    for c in range(4):
        w0, w1 = split_tile(v[c] * over0), split_tile(v[c] * over1)
        for part in range(2):
            first = 80 * part + 16 * c
            c_ref[first : first + 16, lanes] = jnp.where(y0, w0[part], jnp.where(y1, w1[part], zero))
            last[part] = jnp.where(iota == c, w1[part], last[part])
    for part in range(2):
        c_ref[80 * part + 64 : 80 * part + 80, lanes] = jnp.where(by == 15, last[part], zero)


ROW_DIMS = (((1,), (1,)), ((), ()))


def rows_by_rows(left, right):
    return lax.dot_general(left, right, ROW_DIMS, preferred_element_type=F32)


def multiply_outside(piece, a_ref, b_ref, c_ref, x_ref, acc_ref, ov_ref):
    if piece == 0:
        acc_ref[0:352, 0:256] += rows_by_rows(a_ref[0:352, :], b_ref[0:256, :])
    elif piece == 1:
        acc_ref[0:352, 256:512] += rows_by_rows(a_ref[0:352, :], b_ref[256:512, :])
    elif piece == 2:
        acc_ref[256:304, :] += rows_by_rows(a_ref[256:304, :], b_ref[512:1024, :])
    else:
        ov_ref[:, 0:64] += rows_by_rows(c_ref[...], x_ref[...])


def splat_outside(d_ref, acc_ref, ov_ref, tiles):
    blocks = POINTS // WIDE
    for block in range(blocks):
        build_block(d_ref, 0, block, *tiles[0])
    for group in range(GROUPS):
        for piece in range(4):
            if group + 1 < GROUPS and piece < blocks:
                build_block(d_ref, group + 1, piece, *tiles[group + 1])
            multiply_outside(piece, *tiles[group], acc_ref, ov_ref)


def splat_inside(acc_ref, tiles):
    for a_ref, b_ref, _, _ in tiles:
        acc_ref[352:608, :] += rows_by_rows(a_ref[352:608, :], b_ref[0:512, :])
        acc_ref[0:256, :] += rows_by_rows(a_ref[0:256, :], b_ref[512:1024, :])


def interpolation_tables(d_ref, r_ref, w_ref):
    iota = tile_iota()
    iota_f = iota.astype(F32)
    zero = jnp.zeros((16, WIDE), BF16)

    @pl.loop(0, GROUPS)
    def _(group):
        r_ref[group, 400:512, :] = jnp.zeros((112, POINTS), BF16)
        for block in range(POINTS // WIDE):
            lanes = slice(block * WIDE, (block + 1) * WIDE)
            fx, fy, fz, cx, cy, cz = lane_rows(d_ref, group, block, range(4, 10), 16)
            bz, bz1 = cz.astype(BF16), (cz + 1.0).astype(BF16)
            g0, g1 = split(1.0 - fz), split(fz)
            for t in range(8):
                at = iota + jnp.asarray(16 * t, BF16)
                z0, z1 = bz == at, bz1 == at
                high, low = [jnp.where(z0, g0[part], jnp.where(z1, g1[part], zero)) for part in range(2)]
                r_ref[group, 16 * t : 16 * t + 16, lanes] = high
                r_ref[group, 128 + 16 * t : 144 + 16 * t, lanes] = high
                r_ref[group, 256 + 16 * t : 272 + 16 * t, lanes] = low
            picked = jnp.where(iota <= 1, g1[0], jnp.where(iota == 2, g1[1], zero))
            r_ref[group, 384:400, lanes] = jnp.where(bz == 127, picked, zero)
            hat_y = jnp.where(cy == iota_f, 1.0 - fy, jnp.where(cy + 1.0 == iota_f, fy, 0.0))
            near, far = (1.0 - fx) * hat_y, fx * hat_y
            for x in range(17):
                w_ref[group, 16 * x : 16 * x + 16, lanes] = jnp.where(cx == x, near, jnp.where(cx == x - 1, far, 0.0))
            edge = jnp.where(cy == 15.0, fy, 0.0)
            for t in range(2):
                at = iota_f + 16.0 * t
                hat = jnp.where(cx == at, 1.0 - fx, jnp.where(cx + 1.0 == at, fx, 0.0))
                w_ref[group, 272 + 16 * t : 288 + 16 * t, lanes] = hat * edge


def weighted(g, w_ref, group, first):
    rows = g.shape[0]
    total = g[0:8] * w_ref[group, first : first + 8]
    for i in range(1, rows // 8):
        total = total + g[8 * i : 8 * i + 8] * w_ref[group, first + 8 * i : first + 8 * i + 8]
    return total


def high_and_low(l_ref, first, value):
    rows = pl.ds(first, value.shape[0])
    high, low = split(value)
    l_ref[rows, 0:128] = high
    l_ref[rows, 128:256] = low
    l_ref[rows, 256:384] = high


def interpolate_inside(u_ref, part_ref, l_ref, r_ref, w_ref):
    high_and_low(l_ref, 0, u_ref[...].reshape(256, 128))

    @pl.loop(0, GROUPS, step=8)
    def _(first):
        for step in range(8):
            group = first + step
            g = jnp.dot(l_ref[0:256, 0:384], r_ref[group, 0:384], preferred_element_type=F32)
            part_ref[group] = weighted(g, w_ref, group, 0)


def interpolate(halo_ref, uz_ref, part_ref, out_ref, l_ref, r_ref, w_ref):
    high_and_low(l_ref, 256, halo_ref[...])
    top = jnp.broadcast_to(uz_ref[:, 0:1], (ROWS, 128))
    high = top.astype(BF16).astype(F32)
    lane = lax.broadcasted_iota(jnp.int32, (ROWS, 128), 1)
    low = jnp.where(lane == 1, top - high, 0.0)
    l_ref[:, 384:512] = jnp.where(jnp.logical_or(lane == 0, lane == 2), high, low).astype(BF16)

    @pl.loop(0, GROUPS, step=8)
    def _(first):
        for step in range(8):
            group = first + step
            g = jnp.dot(l_ref[256:ROWS, :], r_ref[group], preferred_element_type=F32)
            total = part_ref[group] + weighted(g, w_ref, group, 256)
            g = jnp.dot(l_ref[0:256, 384:512], r_ref[group, 384:512], preferred_element_type=F32)
            value = jnp.sum(total + weighted(g, w_ref, group, 0), axis=0, keepdims=True)
            count = POINTS // DEVICES
            for q in range(count):
                out_ref[pl.ds(group * count + q, 1), :] = value[:, q * DEVICES : (q + 1) * DEVICES]


FACES = [(1, 0, 0), (0, 1, 0), (0, 0, 1)]
UPPER = FACES + [(1, 1, 0), (1, 0, 1), (0, 1, 1), (1, 1, 1)]


def roll_to(tile, source, target):
    shift = (target - source) % 128
    return pltpu.roll(tile, shift, 1) if shift else tile


def grid_iotas():
    lane = lax.broadcasted_iota(jnp.int32, (8, 128), 1)
    sub = lax.broadcasted_iota(jnp.int32, (8, 128), 0)
    return lane, sub


def pack(read, source):
    lane, _ = grid_iotas()
    packed = jnp.zeros((8, 128), F32)
    for i in range(32):
        packed = jnp.where(lane == i, roll_to(read(i), source, i), packed)
    return packed


def slab_star(comb, along_x, along_y, along_z, rows, tiles):
    n = along_y.shape[0]
    total = comb(along_x[0:n], along_x[2 : n + 2])
    sub3 = lax.broadcasted_iota(jnp.int32, (n, 8, 128), 1)
    down = pltpu.roll(along_y.reshape(2 * n, 8, 128), 1, 1).reshape(n, 2, 8, 128)
    up = pltpu.roll(along_y.reshape(2 * n, 8, 128), 7, 1).reshape(n, 2, 8, 128)
    edge = [jnp.stack([rows(side, i) for i in range(n)]) for side in range(2)]
    first, last = sub3 == 0, sub3 == 7
    low = jnp.stack([jnp.where(first, edge[0], down[:, 0]), jnp.where(first, down[:, 0], down[:, 1])], axis=1)
    high = jnp.stack([jnp.where(last, up[:, 1], up[:, 0]), jnp.where(last, edge[1], up[:, 1])], axis=1)
    total = total + comb(low, high)
    lanes = lax.broadcasted_iota(jnp.int32, (2 * n, 8, 128), 2)
    flat = along_z.reshape(16 * n, 128)
    sides = []
    for side, shift, at in ((0, 1, 0), (1, 127, 127)):
        edge = jnp.stack([tiles(side, i, t) for i in range(n) for t in range(2)])
        sides.append(jnp.where(lanes == at, edge, pltpu.roll(flat, shift, 1).reshape(2 * n, 8, 128)))
    return total + comb(*sides).reshape(n, 2, 8, 128)


def own_star(comb, along_x, along_y, along_z):
    nothing = jnp.zeros((8, 128), F32)
    end_slab = jnp.zeros((1, 2, 8, 128), F32)
    wide = jnp.concatenate([end_slab, along_x, end_slab], axis=0)
    return slab_star(comb, wide, along_y, along_z, lambda side, i: nothing, lambda side, i, t: nothing)


def add_outside(total, low_sign, x_low, x_high, rows, tiles):
    sub3 = lax.broadcasted_iota(jnp.int32, (16, 8, 128), 1)
    lanes = lax.broadcasted_iota(jnp.int32, (32, 8, 128), 2)
    edge = [jnp.stack([rows(side, i + 1) for i in range(16)]) for side in range(2)]
    along_y = jnp.stack([jnp.where(sub3 == 0, low_sign * edge[0], 0.0), jnp.where(sub3 == 7, edge[1], 0.0)], axis=1)
    edge = [jnp.stack([tiles(side, i + 1, t) for i in range(16) for t in range(2)]) for side in range(2)]
    along_z = jnp.where(lanes == 0, low_sign * edge[0], jnp.where(lanes == 127, edge[1], 0.0))
    total = total + (along_y + along_z.reshape(16, 2, 8, 128))
    return jnp.concatenate(
        [total[0:1] + low_sign * x_low[None], total[1:15], total[15:16] + x_high[None]], axis=0
    )


def layer_star_y(comb, side, fx, fy, fz):
    row = lax.broadcasted_iota(jnp.int32, (16, 128), 0)
    lane16 = lax.broadcasted_iota(jnp.int32, (16, 128), 1)
    plane = fx["plane"][side]
    low = jnp.where(row == 0, jnp.broadcast_to(fx["xy"][0][side], (16, 128)), pltpu.roll(plane, 1, 0))
    high = jnp.where(row == 15, jnp.broadcast_to(fx["xy"][1][side], (16, 128)), pltpu.roll(plane, 15, 0))
    total = comb(low, high)
    outer, own = fy["plane2"][side], fy["own_row"][side]
    total = total + (comb(outer, own) if side == 0 else comb(own, outer))
    plane = fz["plane"][side]
    parity, source = (1, 7) if side == 0 else (0, 0)
    sides = []
    for z_side, shift, at in ((0, 1, 0), (1, 127, 127)):
        values = jnp.broadcast_to(fz["yz"][side][z_side][source : source + 1], (16, 128))
        column = jnp.sum(jnp.where(lane16 == 2 * row + parity, values, 0.0), axis=1, keepdims=True)
        sides.append(jnp.where(lane16 == at, jnp.broadcast_to(column, (16, 128)), pltpu.roll(plane, shift, 1)))
    return total + comb(*sides)


def layer_star_z(comb, side, fx, fy, fz):
    lane, sub = grid_iotas()
    layer = fx["zp"][side]
    low = jnp.where(lane < 2, roll_to(fx["xz"][0][side], 30, 0), pltpu.roll(layer, 2, 1))
    high = jnp.where(lane >= 30, roll_to(fx["xz"][1][side], 0, 30), pltpu.roll(layer, 126, 1))
    total = comb(low, high)
    layer = fy["zp"][side]
    down, up = pltpu.roll(layer, 1, 0), pltpu.roll(layer, 7, 0)
    odd = lax.rem(lane, 2) == 1
    beyond = pltpu.roll(pltpu.roll(fy["yz"][0][side], 1, 0), 127, 1)
    low = jnp.where(sub == 0, jnp.where(odd, pltpu.roll(down, 1, 1), beyond), down)
    beyond = pltpu.roll(pltpu.roll(fy["yz"][1][side], 7, 0), 1, 1)
    high = jnp.where(sub == 7, jnp.where(odd, beyond, pltpu.roll(up, 127, 1)), up)
    total = total + comb(low, high)
    outer, own = fz["zp2"][side], fz["own_z"][side]
    total = total + (comb(outer, own) if side == 0 else comb(own, outer))
    return jnp.where(lane < 32, total, 0.0)


def solve(
    sizes, here, own_rows, tables, own_values, s_ref, ov_ref, out_ref, u_ref, halo_ref, uz_ref,
    m_ref, zs_ref, sx, sy, sxy, sz,
    z5, xa, xb, ya, yb, exy, za, exz, eyz,
    pw, rw, z3, px, rx, py, py2, ry, pxy, pz, pxz, pyz, inv_ref, diag_ref, plane_ref, uzp, pre_ref,
    fx, fy, fxy, fz, s_send, s_recv, g_send, g_recv, h_send, h_recv, f_send, f_recv,
):
    lower = [here[a] > 0 for a in range(3)]
    upper = [here[a] < sizes[a] - 1 for a in range(3)]

    def present(step):
        wanted = [(upper if step[a] > 0 else lower)[a] for a in range(3) if step[a]]
        return functools.reduce(jnp.logical_and, wanted)

    def opposite(step):
        return tuple(-v for v in step)

    def message(step, source, target, send, recv):
        copy = pltpu.make_async_remote_copy(
            src_ref=source, dst_ref=target, send_sem=send, recv_sem=recv,
            device_id=tuple(here[a] + step[a] for a in range(3)), device_id_type=MESH,
        )
        return step, copy

    def start(messages):
        for step, copy in messages:
            @pl.when(present(step))
            def _(copy=copy):
                copy.start()

    def receive(messages):
        for step, copy in messages:
            @pl.when(present(opposite(step)))
            def _(copy=copy):
                copy.wait_recv()

    def drain(messages):
        for step, copy in messages:
            @pl.when(present(step))
            def _(copy=copy):
                copy.wait_send()

    lane, sub = grid_iotas()
    zero = jnp.zeros((8, 128), F32)

    def over(first):
        tile = ov_ref[pl.ds(first, 8), :] + ov_ref[pl.ds(first + 80, 8), :]
        return tile + pltpu.roll(tile, 96, 1)

    packed = zero
    rest = roll_to(over(64), 0, 32)
    for c in range(4):
        for t in range(2):
            tile = over(16 * c + 8 * t)
            at = 32 * c + 16 * t
            packed = jnp.where(jnp.logical_and(lane >= at, lane < at + 16), roll_to(tile, 0, at), packed)
            rest = jnp.where(lane == 4 * t + c, roll_to(tile, 16, 4 * t + c), rest)
    zs_ref[0] = packed
    zs_ref[1] = rest
    out_ref[...] = s_ref[256:304, :] + s_ref[304:352, :]
    sources = [out_ref.at[0:16], out_ref.at[16:32], zs_ref.at[0], out_ref.at[32:33]] + [zs_ref.at[1]] * 3
    targets = [sx, sy, sz.at[0], sxy, sz.at[1], sz.at[2], sz.at[3]]
    mass = [message(UPPER[i], sources[i], targets[i], s_send.at[i], s_recv.at[i]) for i in range(7)]
    start(mass[::-1])
    own_rows()
    for c in range(4):
        columns = slice(128 * c, 128 * c + 128)
        m_ref[c] = (s_ref[0:256, columns] + s_ref[352:608, columns]).reshape(16, 2, 8, 128)
    receive(mass)
    for c in range(4):
        columns = slice(128 * c, 128 * c + 128)
        m_ref[c, 0] += sx[:, columns].reshape(2, 8, 128)
        from_y = sy[:, columns]
        for x in range(16):
            row = from_y[x : x + 1, :] + jnp.where(lane == 0, roll_to(sz[2], 32 + x, 0), 0.0)[c : c + 1, :]
            m_ref[c, x, 0, 0:1, :] += row
        for i in range(32):
            m_ref[c, i // 2, i % 2] += jnp.where(lane == 0, roll_to(sz[0], 32 * c + 16 * (i % 2) + i // 2, 0), 0.0)
        for t in range(2):
            m_ref[c, 0, t] += jnp.where(lane == 0, roll_to(sz[1], 4 * t + c, 0), 0.0)
        corner = sxy[:, columns] + jnp.where(lane == 0, roll_to(sz[3], 48, 0), 0.0)[c : c + 1, :]
        m_ref[c, 0, 0, 0:1, :] += corner

    def end(side, depth, size):
        return size - 1 - depth if side == 0 else depth

    def toward(side):
        return 1 if side == 0 else -1

    def mesh_step(**sides):
        return tuple(toward(sides[name]) if name in sides else 0 for name in "xyz")

    def numbered(entries, send, recv):
        return [message(step, a, b, send.at[i], recv.at[i]) for i, (step, a, b) in enumerate(entries)]

    def difference(low, high):
        return high - low

    def plus(low, high):
        return low + high

    for side in range(2):
        for i, (c, depth) in enumerate(((0, 0), (2, 0), (1, 0), (3, 0), (2, 1))):
            z5[side, i] = pack(lambda k, c=c: m_ref[c, k // 2, k % 2], end(side, depth, 128))
    entries = []
    for a in range(2):
        for b in range(2):
            entries.append((mesh_step(x=a, y=b), m_ref.at[0:2, end(a, 0, 16), 1 - b, 7 - 7 * b, :], exy.at[a, b]))
            entries.append((mesh_step(x=a, z=b), z5.at[b, 0:2], exz.at[a, b]))
            entries.append((mesh_step(y=a, z=b), z5.at[b, 1:3], eyz.at[a, b]))
    for a in range(2):
        first = 14 if a == 0 else 0
        entries.append((mesh_step(x=a), m_ref.at[0, first : first + 2], xa.at[a]))
        entries.append((mesh_step(x=a), m_ref.at[1:4, end(a, 0, 16)], xb.at[a]))
        entries.append((mesh_step(y=a), m_ref.at[:, :, 1 - a, 7 - 7 * a, :], ya.at[a]))
        entries.append((mesh_step(y=a), m_ref.at[1, :, 1 - a, 6 - 5 * a, :], yb.at[a]))
        entries.append((mesh_step(z=a), z5.at[a], za.at[a]))
    ghost = numbered(entries, g_send, g_recv)
    start(ghost)
    pre_ref[...] = own_star(difference, m_ref[0], m_ref[1], m_ref[2])
    tables()
    receive(ghost)

    def tiles_of(zp, xz):
        def tiles(side, i, t):
            at = 0 if side == 0 else 127
            if i == 0:
                return roll_to(xz[0][side], 30 + t, at)
            if i == 17:
                return roll_to(xz[1][side], t, at)
            return roll_to(zp[side], 2 * (i - 1) + t, at)
        return tiles

    def rows_of(row, xy):
        def rows(side, i):
            value = xy[0][side] if i == 0 else xy[1][side] if i == 17 else row(side, i - 1)
            return jnp.broadcast_to(value, (8, 128))
        return rows

    def both(get):
        return [get(0), get(1)]

    def grid2(get):
        return [[get(a, b) for b in range(2)] for a in range(2)]

    nx = {
        "plane": both(lambda a: ya[a, 0]), "xy": grid2(lambda a, b: exy[a, b, 0:1]),
        "zp": both(lambda a: za[a, 0]), "xz": grid2(lambda a, b: exz[a, b, 0]),
    }
    ny = {
        "plane2": both(lambda a: yb[a]), "own_row": both(lambda a: m_ref[1, :, a, 7 * a, :]),
        "zp": both(lambda a: za[a, 2]), "yz": grid2(lambda a, b: eyz[a, b, 1]),
    }
    nz = {
        "plane": both(lambda a: ya[a, 2]), "yz": grid2(lambda a, b: eyz[a, b, 0]),
        "zp2": both(lambda a: za[a, 4]), "own_z": both(lambda a: z5[1 - a, 1]),
    }
    rows = rows_of(lambda side, x: ya[side, 1, x : x + 1, :], grid2(lambda a, b: exy[a, b, 1:2]))
    tiles = tiles_of(both(lambda a: za[a, 1]), grid2(lambda a, b: exz[a, b, 1]))

    def end_star(comb, a, three, along_y, along_z, rows, tiles):
        at = 17 * a
        return slab_star(
            comb, jnp.stack(three), along_y[None], along_z[None],
            lambda side, i: rows(side, at), lambda side, i, t: tiles(side, at, t),
        )

    ends = [
        end_star(difference, 0, [xa[0, 0], xa[0, 1], m_ref[0, 0]], xb[0, 0], xb[0, 1], rows, tiles),
        end_star(difference, 1, [m_ref[0, 15], xa[1, 0], xa[1, 1]], xb[1, 0], xb[1, 1], rows, tiles),
    ]
    inside = add_outside(pre_ref[...], -1.0, xa[0, 1], xa[1, 0], rows, tiles)
    source = -0.5 * jnp.concatenate([ends[0], inside, ends[1]], axis=0)

    def shift_diagonal(mass_part):
        return 6.0 + base_screen + point_screen * mass_part

    def inverse(diagonal, exists):
        return jnp.where(exists, 1.0 / diagonal, 0.0)

    slabs = shift_diagonal(jnp.concatenate([xb[0, 2:3], m_ref[3], xb[1, 2:3]], axis=0))
    diag_ref[...] = slabs
    inv_ref[0] = inverse(slabs[0], lower[0])
    inv_ref[1:17] = 1.0 / slabs[1:17]
    inv_ref[17] = inverse(slabs[17], upper[0])
    exists = lambda axis, side: (lower, upper)[side][axis]
    diag_y = both(lambda a: shift_diagonal(ya[a, 3]))
    inv_y = both(lambda a: inverse(diag_y[a], exists(1, a)))
    diag_z = both(lambda a: shift_diagonal(za[a, 3]))
    inv_z = both(lambda a: inverse(diag_z[a], exists(2, a)))

    def second_sweep(round_index, slabs, planes, layers, residual, keep, push):
        for side in range(2):
            plane_ref[round_index, side] = planes[side]
        own = slabs[1:17]
        around = slab_star(
            plus, slabs, own, own,
            lambda side, i: jnp.broadcast_to(plane_ref[round_index, side, i : i + 1, :], (8, 128)),
            lambda side, i, t: roll_to(layers[side], 2 * i + t, 0 if side == 0 else 127),
        )
        residual = residual - (diag_ref[1:17] * own - around)
        return residual, keep * own + push * (residual * inv_ref[1:17])

    factors = sweep_factors()
    slabs = source * inv_ref[...]
    planes = both(lambda a: -0.5 * layer_star_y(difference, a, nx, ny, nz) * inv_y[a])
    layers = both(lambda a: -0.5 * layer_star_z(difference, a, nx, ny, nz) * inv_z[a])
    u_ref[...] = slabs[1:17]
    residual, following = second_sweep(0, slabs, planes, layers, source[1:17], *factors[0])

    rounds = []
    for e in range(2):
        pw[e] = following
        rw[e] = residual
        for side in range(2):
            for i, (ref, depth) in enumerate(((pw, 0), (pw, 1), (rw, 0))):
                z3[e, side, i] = pack(lambda k, ref=ref: ref[e, k // 2, k % 2], end(side, depth, 128))
        entries = []
        for a in range(2):
            for b in range(2):
                row = pw.at[e, end(a, 0, 16), 1 - b, 7 - 7 * b : 8 - 7 * b, :]
                entries.append((mesh_step(x=a, y=b), row, pxy.at[e, a, b]))
                entries.append((mesh_step(x=a, z=b), z3.at[e, b, 0], pxz.at[e, a, b]))
                entries.append((mesh_step(y=a, z=b), z3.at[e, b, 0], pyz.at[e, a, b]))
        for a in range(2):
            first = 14 if a == 0 else 0
            entries.append((mesh_step(x=a), pw.at[e, first : first + 2], px.at[e, a]))
            entries.append((mesh_step(x=a), rw.at[e, end(a, 0, 16)], rx.at[e, a]))
            entries.append((mesh_step(y=a), pw.at[e, :, 1 - a, 7 - 7 * a, :], py.at[e, a]))
            entries.append((mesh_step(y=a), pw.at[e, :, 1 - a, 6 - 5 * a, :], py2.at[e, a]))
            entries.append((mesh_step(y=a), rw.at[e, :, 1 - a, 7 - 7 * a, :], ry.at[e, a]))
            entries.append((mesh_step(z=a), z3.at[e, a], pz.at[e, a]))
        ghosts = numbered(entries, h_send.at[e], h_recv.at[e])
        rounds.append(ghosts)
        start(ghosts)
        u_ref[...] += following
        own = pw[e]
        pre_ref[...] = rw[e] - (diag_ref[1:17] * own - own_star(plus, own, own, own))
        receive(ghosts)
        p = {
            "plane": both(lambda a: py[e, a]), "plane2": both(lambda a: py2[e, a]),
            "own_row": both(lambda a: pw[e, :, a, 7 * a, :]), "xy": grid2(lambda a, b: pxy[e, a, b]),
            "zp": both(lambda a: pz[e, a, 0]), "zp2": both(lambda a: pz[e, a, 1]),
            "own_z": both(lambda a: z3[e, 1 - a, 0]),
            "xz": grid2(lambda a, b: pxz[e, a, b]), "yz": grid2(lambda a, b: pyz[e, a, b]),
        }
        rows = rows_of(lambda side, x: py[e, side, x : x + 1, :], p["xy"])
        tiles = tiles_of(p["zp"], p["xz"])
        inside = add_outside(pre_ref[...], 1.0, px[e, 0, 1], px[e, 1, 0], rows, tiles)
        ends = []
        for a, three in enumerate(([px[e, 0, 0], px[e, 0, 1], pw[e, 0]], [pw[e, 15], px[e, 1, 0], px[e, 1, 1]])):
            around = end_star(plus, a, three, three[1], three[1], rows, tiles)
            ends.append(rx[e, a][None] - (diag_ref[17 * a][None] * three[1][None] - around))
        middle = jnp.concatenate([px[e, 0, 1][None], pw[e], px[e, 1, 0][None]], axis=0)
        residual = jnp.concatenate([ends[0], inside, ends[1]], axis=0)
        keep, push = factors[2 * e + 1]
        slabs = keep * middle + push * (residual * inv_ref[...])

        def outside(own, rest, diagonal, inverse_diagonal, star):
            rest = rest - (diagonal * own - star)
            return keep * own + push * (rest * inverse_diagonal)

        planes = both(lambda a: outside(p["plane"][a], ry[e, a], diag_y[a], inv_y[a], layer_star_y(plus, a, p, p, p)))
        layers = both(lambda a: outside(p["zp"][a], pz[e, a, 2], diag_z[a], inv_z[a], layer_star_z(plus, a, p, p, p)))
        u_ref[...] += slabs[1:17]
        residual, following = second_sweep(e + 1, slabs, planes, layers, residual[1:17], *factors[2 * e + 2])
    u_ref[...] += following

    uzp[...] = pack(lambda i: u_ref[i // 2, i % 2], 0)
    sources = [u_ref.at[0], u_ref.at[:, 0, 0, :], uzp, u_ref.at[0, 0, 0:1]] + [uzp] * 3
    targets = [fx, fy, fz.at[0], fxy, fz.at[1], fz.at[2], fz.at[3]]
    layer = [message(opposite(UPPER[i]), sources[i], targets[i], f_send.at[i], f_recv.at[i]) for i in range(7)]
    start(layer[::-1])
    own_values()
    receive(layer)
    halo_ref[0:16] = fx[...].reshape(16, 128)
    halo_ref[16:32] = fy[...]
    halo_ref[32:40] = jnp.where(sub == 0, jnp.broadcast_to(fxy[...], (8, 128)), 0.0)
    halo_ref[40:48] = zero
    for i in range(32):
        uz_ref[8 * i : 8 * i + 8] = roll_to(fz[0], i, 0)
    for t in range(2):
        uz_ref[256 + 8 * t : 264 + 8 * t] = roll_to(fz[1], t, 0)
        picked = jnp.where(lane == 2 * (8 * t + sub), jnp.broadcast_to(fz[2, 0:1], (8, 128)), 0.0)
        column = jnp.sum(picked, axis=1, keepdims=True)
        uz_ref[272 + 8 * t : 280 + 8 * t] = jnp.broadcast_to(column, (8, 128))
    uz_ref[288:296] = jnp.where(sub == 0, fz[3], 0.0)
    uz_ref[296:304] = zero

    def finish():
        for messages in (mass, ghost, *rounds, layer):
            drain(messages)

    return finish


FIELD = (16, 2, 8, 128)
SOLVE_SHAPES = [
    (4, *FIELD), (2, 8, 128), (16, 512), (16, 512), (1, 512), (4, 8, 128),
    (2, 5, 8, 128), (2, 2, 2, 8, 128), (2, 3, 2, 8, 128), (2, 4, 16, 128), (2, 16, 128), (2, 2, 2, 128),
    (2, 5, 8, 128), (2, 2, 2, 8, 128), (2, 2, 2, 8, 128),
    (2, *FIELD), (2, *FIELD), (2, 2, 3, 8, 128), (2, 2, 2, 2, 8, 128), (2, 2, 2, 8, 128),
    (2, 2, 16, 128), (2, 2, 16, 128), (2, 2, 16, 128), (2, 2, 2, 1, 128), (2, 2, 3, 8, 128),
    (2, 2, 2, 8, 128), (2, 2, 2, 8, 128), (18, 2, 8, 128), (18, 2, 8, 128), (3, 2, 16, 128), (8, 128), FIELD,
    (2, 8, 128), (16, 128), (1, 128), (4, 8, 128),
]
LANDING = [2, 3, 4, 5, 7, 8, 9, 10, 11, 12, 13, 14, 18, 19, 20, 21, 22, 23, 24, 25, 26, 32, 33, 34, 35]


def kernel(sizes, data_hbm, cells_hbm, counts_hbm, u_ref, out_ref, *scratch):
    tiles, scratch = [scratch[i::GROUPS][:4] for i in range(GROUPS)], scratch[4 * GROUPS :]
    (data_ref, cells_ref, counts_ref, send, recv, sent, d_ref, acc_ref, ov_ref, face_ref,
     l_ref, r_ref, w_ref, part_ref, halo_ref, uz_ref, val_ref, back_send, back_recv, back_sent,
     in_sem, send_sem, recv_sem, *rest) = scratch
    here = position(sizes)
    me = (here[0] * sizes[1] + here[1]) * sizes[2] + here[2]
    loads = [
        pltpu.make_async_copy(source, target, in_sem.at[i])
        for i, (source, target) in enumerate(((data_hbm, data_ref), (cells_hbm, cells_ref), (counts_hbm, counts_ref)))
    ]
    for load in loads:
        load.start()
    for at in LANDING:
        rest[at][...] = jnp.zeros(rest[at].shape, F32)

    def meanwhile():
        for load in loads:
            load.wait()
        prepare_rows(data_ref, cells_ref, counts_ref, send)
        acc_ref[...] = jnp.zeros_like(acc_ref)
        ov_ref[...] = jnp.zeros_like(ov_ref)

    greet(me, meanwhile)
    exchange_rows(me, send, recv, sent, send_sem.at[0], recv_sem.at[0])
    d_ref[...] = recv[...].T[: CAP * CHANNELS].reshape(CHANNELS, CAP, DEVICES)
    splat_outside(d_ref, acc_ref, ov_ref, tiles)
    finish = solve(
        sizes, here, lambda: splat_inside(acc_ref, tiles), lambda: interpolation_tables(d_ref, r_ref, w_ref),
        lambda: interpolate_inside(u_ref, part_ref, l_ref, r_ref, w_ref),
        acc_ref, ov_ref, face_ref, u_ref, halo_ref, uz_ref, *rest,
    )
    interpolate(halo_ref, uz_ref, part_ref, val_ref, l_ref, r_ref, w_ref)
    padded = jnp.concatenate([val_ref[...], jnp.zeros((DEVICES - CAP, DEVICES), F32)], axis=0)
    back_send[...] = padded.T
    exchange_rows(me, back_send, back_recv, back_sent, send_sem.at[1], recv_sem.at[1])
    slot = lax.broadcasted_iota(jnp.int32, (CAP, DEVICES), 0)
    out_ref[...] = jnp.where(slot < counts_ref[...], back_recv[...].T[:CAP], 0.0)
    finish()
    pltpu.make_async_copy(send, recv, send_sem.at[0]).wait()
    pltpu.make_async_copy(back_send, back_recv, send_sem.at[1]).wait()


def on_device(sizes, point_data, point_cells, send_counts):
    data = jnp.transpose(point_data[0], (1, 2, 0))
    cells = jnp.transpose(point_cells[0], (1, 2, 0))
    dma = pltpu.SemaphoreType.DMA
    tile_rows = (608, 1024, 160, 64)
    shapes = [((rows, POINTS), BF16) for rows in tile_rows for _ in range(GROUPS)] + [
        ((7, CAP, DEVICES), F32), ((3, CAP, DEVICES), jnp.int32), ((1, DEVICES), jnp.int32),
        ((DEVICES, WIDTH), F32), ((DEVICES, WIDTH), F32), ((1, WIDTH), F32), ((CHANNELS, CAP, DEVICES), F32),
        ((608, 512), F32), ((160, 128), F32), ((48, 512), F32), ((ROWS, 512), BF16),
        ((GROUPS, 512, POINTS), BF16), ((GROUPS, ROWS, POINTS), F32), ((GROUPS, 8, POINTS), F32),
        ((48, 128), F32), ((ROWS, 128), F32), ((CAP, DEVICES), F32),
        ((DEVICES, DEVICES), F32), ((DEVICES, DEVICES), F32), ((1, DEVICES), F32),
    ]
    u, returned = pl.pallas_call(
        functools.partial(kernel, sizes),
        out_shape=[jax.ShapeDtypeStruct(s, F32) for s in (FIELD, (CAP, DEVICES))],
        in_specs=[pl.BlockSpec(memory_space=pltpu.HBM)] * 3,
        out_specs=[vmem()] * 2,
        scratch_shapes=[pltpu.VMEM(*s) for s in shapes]
        + [dma((3,)), dma((2,)), dma((2,))]
        + [pltpu.VMEM(s, F32) for s in SOLVE_SHAPES]
        + [dma((7,)), dma((7,)), dma((22,)), dma((22,)), dma((2, 24)), dma((2, 24)), dma((7,)), dma((7,))],
        compiler_params=pltpu.CompilerParams(
            vmem_limit_bytes=48 * 1024 * 1024, collective_id=0, has_side_effects=True
        ),
        name="reconstruct",
    )(*[pltpu.with_memory_space_constraint(v, pltpu.HBM) for v in (data, cells, send_counts)])
    u, returned = pl.pallas_call(
        put_out,
        out_shape=[jax.ShapeDtypeStruct(s, F32) for s in (FIELD, (CAP, DEVICES))],
        in_specs=[vmem()] * 2,
        out_specs=[pl.BlockSpec(memory_space=pl.ANY)] * 2,
        scratch_shapes=[dma((2,))],
        compiler_params=pltpu.CompilerParams(vmem_limit_bytes=1024 * 1024),
        name="put_out",
    )(u, returned)
    return u.reshape(16, 16, 128), returned.T[None]


def put_out(u_ref, value_ref, u_out, value_out, sems):
    copies = [
        pltpu.make_async_copy(u_ref, u_out, sems.at[0]),
        pltpu.make_async_copy(value_ref, value_out, sems.at[1]),
    ]
    for copy in copies:
        copy.start()
    for copy in copies:
        copy.wait()


def solution(mesh):
    sizes = tuple(mesh.shape[name] for name in ("gx", "gy", "gz"))
    spread_over = ("gx", "gy", "gz")
    in_specs = (P(spread_over, None, None, None), P(spread_over, None, None, None), P(spread_over, None))
    out_specs = (P("gx", "gy", "gz"), P(spread_over, None, None))
    return jax.shard_map(
        functools.partial(on_device, sizes), mesh=mesh, in_specs=in_specs, out_specs=out_specs, check_vma=False
    )
```
